128 devices in a mesh: row: 16 (over y, x_lo, core), col: 8 (over x_hi, z).
Axes of the slice: x: 4 (x_hi: 2, x_lo: 2; x = x_hi * 2 + x_lo), y: 4, z: 4, core: 2. Of those that a mesh axis runs over, the one named last changes fastest.
Arguments:
- tiles: bfloat16 [2, 32768, 16384], P(None, 'row', 'col'), may hold values from -0.046875 to 0.046875
- probe: bfloat16 [2, 32768, 256], P(None, ('row', 'col')), may hold values from -6 to 6
- cluster_perm: int32 [2, 16, 2048], P(None, 'row'), may hold values from 0 to 2047, each once within a row
- tile_keep: int32 [2, 16, 8], P(None, 'row', 'col'), may hold values 0 or 1
Outputs:
- samples: float32 [2, 32768, 256], P(None, ('row', 'col'))
- leaf_basis: float32 [2, 32768, 256], P(None, ('row', 'col'))
The draws below stay inside these ranges and needn't reach their ends.
Inputs may be any that keep to these rules, and one draw needn't show every extreme that they name: Each row of cluster_perm is a permutation. `tile_keep`: entries with c = 0 are not read.
All inputs are finite; a program needn't handle non-finite values. No bound on the sum of `tile_keep` on one device may be relied on, other than what follows from the above.
Results may differ from the reference program's by a relative error of at most 0.0003.
Values may be sent and summed in bfloat16 or wider, within the bound.
No kernel may reach another device: no remote copies, remote signals or barrier semaphores. Data moves between devices by JAX's collectives and lax.ppermute only.
A program may use at most 128 MiB of HBM per device.

```python
import jax
import jax.numpy as jnp
from jax import lax

TILE = 2048
P_SIZE = 256
CPR = 2
NCL = 32
N_ROW = 16
N_COL = 8


def plant(array, rng, low, largest):
    index_at = [jax.random.randint(jax.random.fold_in(rng, axis), (), 0, length) for axis, length in enumerate(array.shape)]
    longest = array.shape.index(max(array.shape))
    next_to = index_at[:longest] + [(index_at[longest] + 1) % array.shape[longest]] + index_at[longest + 1:]
    return array.at[tuple(index_at)].set(low).at[tuple(next_to)].set(largest)


def block_levels(stream_key, extent, shards, low, top_value):
    def one(axis_at, blocks):
        heights = jax.random.uniform(jax.random.fold_in(jax.random.fold_in(stream_key, 6), axis_at), (blocks,), jnp.float32, low / len(shards), top_value / len(shards))
        return jnp.repeat(jnp.exp(heights), extent[axis_at] // blocks).reshape((-1,) + (1,) * (len(extent) - axis_at - 1))

    loudness = one(*shards[0])
    for cut in shards[1:]:
        loudness = loudness * one(*cut)
    return loudness


def normal_values(key, dims, width, most, cuts=(), dtype=jnp.bfloat16):
    values = jax.random.normal(key, dims, jnp.float32) * width
    if len(cuts) > 0:
        values = block_levels(key, dims, cuts, -0.22, 0.18) * values
    return jnp.clip(values, min=-most, max=most).astype(dtype)


def setup_inputs(seed: int = 0) -> dict:
    splits = jax.random.split(jax.random.key(seed), 5)
    tiles = normal_values(splits[0], (CPR, N_ROW * TILE, N_COL * TILE), (N_COL * TILE) ** -0.5, 0.046875, ((1, 16), (2, 8)))
    probe = normal_values(splits[1], (CPR, N_ROW * TILE, P_SIZE), 1.0, 6.0, ((1, 128),))
    cluster_perm = jax.vmap(lambda own: jax.random.permutation(own, TILE))(jax.random.split(splits[2], CPR * N_ROW)).reshape((CPR, N_ROW, TILE)).astype(jnp.int32)
    tile_keep = plant((jax.random.randint(splits[3], (CPR, N_ROW, N_COL), 0, 4) < 3).astype(jnp.int32), jax.random.fold_in(splits[3], 1), 0, 1)
    return {"tiles": tiles, "probe": probe, "cluster_perm": cluster_perm, "tile_keep": tile_keep}


def reference(tiles, probe, cluster_perm, tile_keep):
    grouped = probe.reshape(CPR, N_ROW, TILE, P_SIZE)
    order = cluster_perm.astype(jnp.int32)[:, :, :, None]
    omega = jnp.take_along_axis(grouped, order, axis=2).reshape(NCL, TILE, P_SIZE)
    keep_flags = tile_keep.astype(jnp.float32)
    partial_value = [jnp.zeros((TILE, P_SIZE), jnp.float32) for index in range(NCL)]
    for slot in range(CPR):
        for row_cl in range(N_ROW):
            first = slot * N_ROW + row_cl
            for offset in range(N_COL):
                second = (first + offset) % NCL
                tile_block = tiles[slot, row_cl * TILE:(row_cl + 1) * TILE, offset * TILE:(offset + 1) * TILE]
                weight = 0.5 if offset == 0 else keep_flags[slot, row_cl, offset]
                forward = jnp.dot(tile_block.astype(jnp.float32), omega[second].astype(jnp.float32), preferred_element_type=jnp.float32)
                backward = lax.dot_general(tile_block.astype(jnp.float32), omega[first].astype(jnp.float32), (((0,), (0,)), ((), ())), preferred_element_type=jnp.float32)
                partial_value[first] = partial_value[first] + weight * forward
                partial_value[second] = partial_value[second] + weight * backward
    blocks = jnp.stack(partial_value, 0)

    def orthogonal(block):
        gram_sum = jnp.dot(block.T, block, precision=lax.Precision.HIGHEST) / TILE
        factor = jnp.linalg.cholesky(gram_sum)
        return jax.scipy.linalg.solve_triangular(factor, block.T, lower=True).T
    bases = jax.vmap(orthogonal)(blocks)
    return (blocks.reshape(CPR, N_ROW * TILE, P_SIZE), bases.reshape(CPR, N_ROW * TILE, P_SIZE))
```

```python
import functools

import jax
import jax.numpy as jnp
from jax import lax
from jax.experimental import pallas as pl
from jax.experimental.pallas import tpu as pltpu
from jax.sharding import PartitionSpec as P

AXES = ("row", "col")
EXACT = lax.Precision.HIGHEST
LEVELS = 32767.0


def sent(value, to):
    nrows, ncols = lax.axis_size("row"), lax.axis_size("col")
    pairs = []
    for r in range(nrows):
        for c in range(ncols):
            r_to, c_to = to(r, c)
            pairs.append((r * ncols + c, (r_to % nrows) * ncols + c_to))
    return lax.ppermute(value, AXES, pairs)


def coded(value):
    largest = jnp.max(jnp.abs(value), axis=-2, keepdims=True)
    scale = jnp.maximum(largest, 1e-30)
    return jnp.round(value * (LEVELS / scale)).astype(jnp.int16), scale


def decoded(code, scale):
    return code.astype(jnp.float32) * (scale * (1.0 / LEVELS))


def half_inverse(a_ref, m_ref, n):
    rows = lax.broadcasted_iota(jnp.int32, (n, n), 0)
    cols = lax.broadcasted_iota(jnp.int32, (n, n), 1)
    m_ref[...] = (rows == cols).astype(jnp.float32)
    lane = lax.broadcasted_iota(jnp.int32, (8, n), 1)
    sub = lax.broadcasted_iota(jnp.int32, (8, n), 0)

    def group(b, carry):
        at = pl.multiple_of(b * 8, 8)
        panel = a_ref[pl.ds(at, 8), :]
        inv_rows = m_ref[pl.ds(at, 8), :]
        small = pltpu.roll(panel, n - at, axis=1)
        small = jnp.where(lane < 8, small, (lane - 8 == sub).astype(jnp.float32))
        scale = jnp.zeros((8, n), jnp.float32)
        for t in range(8):
            pivot_row = jnp.broadcast_to(small[t : t + 1, :], (8, n))
            column = jnp.broadcast_to(small[:, t : t + 1], (8, n))
            pivot = jnp.broadcast_to(column[t : t + 1, :], (8, n))
            scale = jnp.where(sub == t, pivot, scale)
            small = small - jnp.where(sub > t, column * (pivot_row / pivot), 0.0)
        scale = lax.rsqrt(scale)
        new_panel = jnp.zeros((8, n), jnp.float32)
        new_inv = jnp.zeros((8, n), jnp.float32)
        for t in range(8):
            factor = jnp.broadcast_to(small[:, 8 + t : 9 + t], (8, n))
            new_panel = new_panel + factor * panel[t : t + 1, :]
            new_inv = new_inv + factor * inv_rows[t : t + 1, :]
        new_panel = jnp.where(lane >= at + sub, new_panel * scale, 0.0)
        new_inv = new_inv * scale
        tall = new_panel.T
        acc_a = a_ref[...]
        acc_m = m_ref[...]
        for t in range(8):
            factor = jnp.broadcast_to(tall[:, t : t + 1], (n, n))
            acc_a = acc_a - factor * new_panel[t : t + 1, :]
            acc_m = acc_m - jnp.where(rows >= at + 8, factor * new_inv[t : t + 1, :], 0.0)
        a_ref[...] = acc_a
        m_ref[...] = acc_m
        m_ref[pl.ds(at, 8), :] = new_inv
        return carry

    lax.fori_loop(0, n // 8, group, 0)


def factor_kernel(scale, g_ref, out_ref, a_ref, m1_ref, m2_ref):
    half = a_ref.shape[0]

    def product(a, b, over):
        return lax.dot_general(
            a, b, ((over[:1], over[1:]), ((), ())), preferred_element_type=jnp.float32, precision=EXACT
        )

    a_ref[...] = g_ref[:half, :half] * scale
    half_inverse(a_ref, m1_ref, half)
    first = m1_ref[...]
    cross = product(first, g_ref[:half, half:] * scale, (1, 0))
    a_ref[...] = g_ref[half:, half:] * scale - product(cross, cross, (0, 0))
    half_inverse(a_ref, m2_ref, half)
    second = m2_ref[...]
    out_ref[:half, :half] = first
    out_ref[:half, half:] = jnp.zeros((half, half), jnp.float32)
    out_ref[half:, :half] = -product(second, product(cross, first, (0, 0)), (1, 0))
    out_ref[half:, half:] = second


def inverse_factor(gram, scale):
    half = gram.shape[0] // 2
    return pl.pallas_call(
        functools.partial(factor_kernel, scale),
        out_shape=jax.ShapeDtypeStruct(gram.shape, jnp.float32),
        scratch_shapes=[pltpu.VMEM((half, half), jnp.float32)] * 3,
        name="inverse_factor",
    )(gram)


def per_device(tiles, probe, cluster_perm, tile_keep):
    row_id = lax.axis_index("row")
    col_id = lax.axis_index("col")
    nrows = lax.axis_size("row")
    ncols = lax.axis_size("col")
    slots, points = probe.shape[0], probe.shape[1]
    tile_len = tiles.shape[1]
    nz = ncols // 2
    plane, depth = col_id // nz, col_id % nz
    weight = jnp.where(col_id == 0, 0.5, tile_keep[:, 0, 0].astype(jnp.float32))[:, None, None]

    blocks = [probe] + [sent(probe, lambda r, c, o=o: (r, c ^ o)) for o in range(1, ncols)]
    raw = jnp.concatenate(blocks, axis=1)
    source = cluster_perm[:, 0, :] ^ (col_id * points)
    chosen = (source[:, :, None] == lax.broadcasted_iota(jnp.int32, (1, 1, tile_len), 2)).astype(jnp.bfloat16)
    omega = jnp.einsum("kij,kjp->kip", chosen, raw, preferred_element_type=jnp.float32).astype(jnp.bfloat16)

    omega_far = sent(omega, lambda r, c: (r - c, c))
    omega_far = jnp.where(row_id + col_id >= nrows, jnp.roll(omega_far, 1, axis=0), omega_far)

    backward = weight * jnp.einsum("kij,kip->kjp", tiles, omega, preferred_element_type=jnp.float32)
    code, scale = coded(backward.reshape(slots, ncols, points, -1))
    code = sent(code, lambda r, c: (r + c, c))
    scale = sent(scale, lambda r, c: (r + c, c))
    arrived = decoded(code, scale)
    arrived = jnp.where(row_id - col_id < 0, jnp.roll(arrived, 1, axis=0), arrived)
    forward = weight * jnp.einsum("kij,kjp->kip", tiles, omega_far, preferred_element_type=jnp.float32)
    combined = (forward.reshape(arrived.shape) + arrived).reshape(slots, 2, nz, points, -1)

    code, scale = coded(combined)

    def at_depth(array, d):
        return lax.dynamic_index_in_dim(array, depth ^ d, axis=2, keepdims=False)

    total = at_depth(combined, 0)
    for d in range(1, nz):
        pieces = [sent(at_depth(part, d), lambda r, c, d=d: (r, c ^ d)) for part in (code, scale)]
        total = total + decoded(*pieces)

    def other_plane(array):
        return sent(array, lambda r, c: (r, c ^ nz))

    def pick(array, i):
        return lax.dynamic_index_in_dim(array, i, axis=0, keepdims=False)

    code, scale = coded(pick(total, 1 - plane))
    own = pick(total, plane) + decoded(other_plane(code), other_plane(scale))
    gram = jnp.einsum("bip,biq->pq", own, own, precision=EXACT)
    for d in (1, nz - 1):
        gram = gram + sent(gram, lambda r, c, d=d: (r, c ^ d))
    inverse = inverse_factor(gram, 1.0 / tile_len)
    basis = jnp.einsum("bip,qp->biq", own, inverse, precision=EXACT)

    def placed(array):
        kept = pick(array, plane)
        other = other_plane(pick(array, 1 - plane))
        return jnp.where(plane == 0, jnp.stack([kept, other]), jnp.stack([other, kept]))

    return (placed(own), placed(basis))


def solution(mesh):
    whole = P(None, ("row", "col"), None)
    return jax.shard_map(
        per_device,
        mesh=mesh,
        in_specs=(P(None, "row", "col"), whole, P(None, "row", None), P(None, "row", "col")),
        out_specs=(whole, whole),
        check_vma=False,
    )
```

```python
import functools

import jax
import jax.numpy as jnp
from jax import lax
from jax.experimental import pallas as pl
from jax.experimental.pallas import tpu as pltpu
from jax.sharding import PartitionSpec as P

AXES = ("row", "col")
EXACT = lax.Precision.HIGHEST
LEVELS = 32767.0
EXTRA = 16


def sent(value, to):
    nrows, ncols = lax.axis_size("row"), lax.axis_size("col")
    pairs = []
    for r in range(nrows):
        for c in range(ncols):
            r_to, c_to = to(r, c)
            pairs.append((r * ncols + c, (r_to % nrows) * ncols + c_to))
    return lax.ppermute(value, AXES, pairs)


def scale_of(exponent, mantissa):
    return jnp.exp2(exponent) * (mantissa * (1.0 / (LEVELS * LEVELS)))


def coded(block):
    largest = jnp.maximum(jnp.max(jnp.abs(block), axis=0, keepdims=True), 1e-30)
    exponent = jnp.floor(jnp.log2(largest * 1.0001)) + 1.0
    mantissa = jnp.ceil(largest * jnp.exp2(-exponent) * LEVELS)
    scale = scale_of(exponent, mantissa)
    values = jnp.clip(jnp.round(block * (1.0 / scale)), -LEVELS, LEVELS)
    at = lax.broadcasted_iota(jnp.int32, (EXTRA, block.shape[1]), 0)
    tail = jnp.where(at == 0, exponent, mantissa)
    return jnp.concatenate([values, tail], axis=0).astype(jnp.int32).astype(jnp.int16)


def decoded(code):
    wide = code.astype(jnp.int32).astype(jnp.float32)
    rows = code.shape[0] - EXTRA
    return wide[:rows] * scale_of(wide[rows : rows + 1], wide[rows + 1 : rows + 2])


def order_kernel(flipped, ids_ref, perm_ref, own_ref, other_ref, g1_ref, g2_ref, g3_ref, out_ref, raw_ref):
    k = pl.program_id(0)
    points = own_ref.shape[1]

    @pl.when(pl.program_id(1) == 0)
    def _():
        for d, ref in enumerate((None, g1_ref, g2_ref, g3_ref)):
            for a in range(2):
                piece = ref[k, a] if d else (other_ref[k] if a else own_ref[k])
                at = (4 * a + d) * points
                raw_ref[:, at : at + points] = piece.T

    length = raw_ref.shape[1]
    index = perm_ref[0] ^ (ids_ref[0] * points)
    place = lax.broadcasted_iota(jnp.int32, (length, index.shape[1]), 0)
    chosen = jnp.where(place == index, 1.0, 0.0).astype(jnp.bfloat16)
    found = jnp.dot(raw_ref[...], chosen, preferred_element_type=jnp.float32)
    out_ref[0] = (found.T if flipped else found).astype(jnp.bfloat16)


def ordered(ids, perm, own, other, gathered, flipped):
    slots, points, probes = own.shape
    length = perm.shape[2]
    step = 512
    whole = [pl.BlockSpec(x.shape, lambda k, i, ids, n=x.ndim: (0,) * n) for x in (own, other, *gathered)]
    shape = (slots, length, probes) if flipped else (slots, probes, length)
    out = (
        pl.BlockSpec((1, step, probes), lambda k, i, ids: (k, i, 0))
        if flipped
        else pl.BlockSpec((1, probes, step), lambda k, i, ids: (k, 0, i))
    )
    return pl.pallas_call(
        functools.partial(order_kernel, flipped),
        out_shape=jax.ShapeDtypeStruct(shape, jnp.bfloat16),
        grid_spec=pltpu.PrefetchScalarGridSpec(
            num_scalar_prefetch=1,
            grid=(slots, length // step),
            in_specs=[pl.BlockSpec((1, 1, step), lambda k, i, ids: (k, 0, i)), *whole],
            out_specs=out,
            scratch_shapes=[pltpu.VMEM((probes, length), jnp.bfloat16)],
        ),
        cost_estimate=pl.CostEstimate(flops=slots * 2 * length * length * probes, bytes_accessed=8 << 20, transcendentals=0),
        name="order_far" if flipped else "order_own",
    )(ids, perm, own, other, *gathered)


def product_kernel(back, ids_ref, weight_ref, tile_ref, omega_ref, *out_refs):
    d, k, a = pl.program_id(0), pl.program_id(1), pl.program_id(2)
    swapped = k ^ ids_ref[2]
    if back:
        value = jnp.dot(omega_ref[k], tile_ref[0], preferred_element_type=jnp.float32).T
    else:
        value = jnp.dot(tile_ref[0], omega_ref[swapped], preferred_element_type=jnp.float32)
    code = coded(value * weight_ref[k])
    slot = swapped if back else k
    for e, ref in enumerate(out_refs):

        @pl.when(d == e)
        def _(ref=ref):
            ref[slot, a] = code


def products(ids, weight, tiles, omega, points, back):
    slots, length = tiles.shape[0], tiles.shape[1]
    probes = omega.shape[1] if back else omega.shape[2]
    nz = length // points // 2

    def at(d, k, a, ids, weight):
        block = a * nz + (ids[1] ^ d)
        return (k, 0, block) if back else (k, block, 0)

    shape = (slots, 2, points + EXTRA, probes)
    return pl.pallas_call(
        functools.partial(product_kernel, back),
        out_shape=[jax.ShapeDtypeStruct(shape, jnp.int16)] * nz,
        grid_spec=pltpu.PrefetchScalarGridSpec(
            num_scalar_prefetch=2,
            grid=(nz, slots, 2),
            in_specs=[
                pl.BlockSpec((1, length, points) if back else (1, points, length), at),
                pl.BlockSpec(omega.shape, lambda d, k, a, ids, weight: (0, 0, 0)),
            ],
            out_specs=[pl.BlockSpec(shape, lambda d, k, a, ids, weight: (0, 0, 0, 0))] * nz,
        ),
        cost_estimate=pl.CostEstimate(flops=slots * 2 * length * length * probes, bytes_accessed=20 << 20, transcendentals=0),
        name="product_back" if back else "product_ahead",
    )(ids, weight, tiles, omega)


def sum_kernel(*refs):
    *in_refs, out_ref = refs
    for k in range(out_ref.shape[0]):
        for a in range(out_ref.shape[1]):
            total = decoded(in_refs[0][k, a])
            for ref in in_refs[1:]:
                total = total + decoded(ref[k, a])
            out_ref[k, a] = coded(total)


def summed(codes):
    return pl.pallas_call(sum_kernel, out_shape=jax.ShapeDtypeStruct(codes[0].shape, jnp.int16), name="sum_back")(*codes)


def merge_kernel(ids_ref, *refs):
    *in_refs, kept_ref, code_ref = refs
    plane = ids_ref[3]
    for a in range(2):
        for ref_of, slot in ((kept_ref, plane), (code_ref, 1 - plane)):
            total = decoded(in_refs[0][slot, a])
            for ref in in_refs[1:]:
                total = total + decoded(ref[slot, a])
            ref_of[a] = total if ref_of is kept_ref else coded(total)


def merged(ids, codes):
    _, _, rows, probes = codes[0].shape
    return pl.pallas_call(
        merge_kernel,
        in_specs=[pl.BlockSpec(memory_space=pltpu.SMEM)] + [pl.BlockSpec(memory_space=pltpu.VMEM)] * len(codes),
        out_shape=[
            jax.ShapeDtypeStruct((2, rows - EXTRA, probes), jnp.float32),
            jax.ShapeDtypeStruct((2, rows, probes), jnp.int16),
        ],
        name="merge",
    )(ids, *codes)


def gram_kernel(ids_ref, kept_ref, code_ref, own_ref, other_ref, gram_ref):
    plane = ids_ref[3]
    total = None
    for ref, a in ((own_ref, plane), (other_ref, 1 - plane)):
        block = kept_ref[a] + decoded(code_ref[a])
        ref[...] = block
        part = lax.dot_general(
            block, block, (((0,), (0,)), ((), ())), preferred_element_type=jnp.float32, precision=EXACT
        )
        total = part if total is None else total + part
    gram_ref[...] = total


def gram_of(ids, kept, code):
    _, points, probes = kept.shape
    block = jax.ShapeDtypeStruct((points, probes), jnp.float32)
    return pl.pallas_call(
        gram_kernel,
        in_specs=[pl.BlockSpec(memory_space=pltpu.SMEM)] + [pl.BlockSpec(memory_space=pltpu.VMEM)] * 2,
        out_shape=[block, block, jax.ShapeDtypeStruct((probes, probes), jnp.float32)],
        name="gram",
    )(ids, kept, code)

def half_inverse(a_ref, m_ref, n):
    rows = lax.broadcasted_iota(jnp.int32, (n, n), 0)
    cols = lax.broadcasted_iota(jnp.int32, (n, n), 1)
    m_ref[...] = (rows == cols).astype(jnp.float32)
    lane = lax.broadcasted_iota(jnp.int32, (8, n), 1)
    sub = lax.broadcasted_iota(jnp.int32, (8, n), 0)

    def group(b, carry):
        at = pl.multiple_of(b * 8, 8)
        panel = a_ref[pl.ds(at, 8), :]
        inv_rows = m_ref[pl.ds(at, 8), :]
        small = pltpu.roll(panel, n - at, axis=1)
        small = jnp.where(lane < 8, small, (lane - 8 == sub).astype(jnp.float32))
        scale = jnp.zeros((8, n), jnp.float32)
        for t in range(8):
            pivot_row = jnp.broadcast_to(small[t : t + 1, :], (8, n))
            column = jnp.broadcast_to(small[:, t : t + 1], (8, n))
            pivot = jnp.broadcast_to(column[t : t + 1, :], (8, n))
            scale = jnp.where(sub == t, pivot, scale)
            small = small - jnp.where(sub > t, column * (pivot_row / pivot), 0.0)
        scale = lax.rsqrt(scale)
        new_panel = jnp.zeros((8, n), jnp.float32)
        new_inv = jnp.zeros((8, n), jnp.float32)
        for t in range(8):
            factor = jnp.broadcast_to(small[:, 8 + t : 9 + t], (8, n))
            new_panel = new_panel + factor * panel[t : t + 1, :]
            new_inv = new_inv + factor * inv_rows[t : t + 1, :]
        new_panel = jnp.where(lane >= at + sub, new_panel * scale, 0.0)
        new_inv = new_inv * scale
        tall = new_panel.T
        acc_a = a_ref[...]
        acc_m = m_ref[...]
        for t in range(8):
            factor = jnp.broadcast_to(tall[:, t : t + 1], (n, n))
            acc_a = acc_a - factor * new_panel[t : t + 1, :]
            acc_m = acc_m - jnp.where(rows >= at + 8, factor * new_inv[t : t + 1, :], 0.0)
        a_ref[...] = acc_a
        m_ref[...] = acc_m
        m_ref[pl.ds(at, 8), :] = new_inv
        return carry

    lax.fori_loop(0, n // 8, group, 0)


def factor_kernel(scale, g1_ref, g2_ref, own_ref, other_ref, own_out, other_out, a_ref, m1_ref, m2_ref):
    half = a_ref.shape[0]

    def product(a, b, over):
        return lax.dot_general(
            a, b, ((over[:1], over[1:]), ((), ())), preferred_element_type=jnp.float32, precision=EXACT
        )

    def gram(rows, cols):
        return (g1_ref[rows, cols] + g2_ref[rows, cols]) * scale

    low, high = slice(0, half), slice(half, 2 * half)
    a_ref[...] = gram(low, low)
    half_inverse(a_ref, m1_ref, half)
    first = m1_ref[...]
    cross = product(first, gram(low, high), (1, 0))
    a_ref[...] = gram(high, high) - product(cross, cross, (0, 0))
    half_inverse(a_ref, m2_ref, half)
    second = m2_ref[...]
    mixed = -product(second, product(cross, first, (0, 0)), (1, 0))
    for ref, out in ((own_ref, own_out), (other_ref, other_out)):
        left, right = ref[:, low], ref[:, high]
        out[:, low] = product(left, first, (1, 1))
        out[:, high] = product(left, mixed, (1, 1)) + product(right, second, (1, 1))


def orthogonal(gram, gram_more, own, other, scale):
    half = gram.shape[0] // 2
    return pl.pallas_call(
        functools.partial(factor_kernel, scale),
        out_shape=[jax.ShapeDtypeStruct(own.shape, jnp.float32)] * 2,
        scratch_shapes=[pltpu.VMEM((half, half), jnp.float32)] * 3,
        name="orthogonal",
    )(gram, gram_more, own, other)


def per_device(tiles, probe, cluster_perm, tile_keep):
    row_id = lax.axis_index("row")
    col_id = lax.axis_index("col")
    nrows = lax.axis_size("row")
    ncols = lax.axis_size("col")
    points, tile_len = probe.shape[1], tiles.shape[1]
    nz = ncols // 2
    plane, depth = col_id // nz, col_id % nz
    wraps = (row_id + col_id >= nrows).astype(jnp.int32)
    ids = jnp.stack([col_id, depth, wraps, plane]).astype(jnp.int32)
    weight = jnp.where(col_id == 0, 0.5, tile_keep[:, 0, 0].astype(jnp.float32))

    def same(d):
        return lambda r, c: (r, c ^ d)

    def slanted(d):
        return lambda r, c: (r + c - (c ^ d), c ^ d)

    other = sent(probe, same(nz))
    far_own = sent(probe, lambda r, c: (r - c, c))
    far_other = sent(probe, lambda r, c: (r - (c ^ nz), c ^ nz))
    far_perm = sent(cluster_perm, lambda r, c: (r - c, c))
    pair = jnp.stack([probe, other], axis=1)
    gathered = [sent(pair, same(d)) for d in range(1, nz)]
    far_pair = jnp.stack([far_own, far_other], axis=1)
    far_gathered = [sent(far_pair, slanted(d)) for d in range(1, nz)]

    omega = ordered(ids, cluster_perm.reshape(-1, 1, tile_len), probe, other, gathered, False)
    back = products(ids, weight, tiles, omega, points, True)
    back = [back[0]] + [sent(back[d], slanted(d)) for d in range(1, nz)]
    omega_far = ordered(ids, far_perm.reshape(-1, 1, tile_len), far_own, far_other, far_gathered, True)
    ahead = products(ids, weight, tiles, omega_far, points, False)
    ahead = [ahead[0]] + [sent(ahead[d], same(d)) for d in range(1, nz)]
    arrived = sent(summed(back), lambda r, c: (r + c, c))
    kept, code = merged(ids, [*ahead, arrived])
    own, swapped, gram = gram_of(ids, kept, sent(code, same(nz)))
    gram = gram + sent(gram, same(1))
    own_basis, swapped_basis = orthogonal(gram, sent(gram, same(nz - 1)), own, swapped, 1.0 / tile_len)

    def placed(mine, theirs):
        theirs = sent(theirs, same(nz))
        return jnp.where(plane == 0, jnp.stack([mine, theirs]), jnp.stack([theirs, mine]))

    return (placed(own, swapped), placed(own_basis, swapped_basis))


def solution(mesh):
    whole = P(None, ("row", "col"), None)
    return jax.shard_map(
        per_device,
        mesh=mesh,
        in_specs=(P(None, "row", "col"), whole, P(None, "row", None), P(None, "row", "col")),
        out_specs=(whole, whole),
        check_vma=False,
    )
```

```python
import functools

import jax
import jax.numpy as jnp
from jax import lax
from jax.experimental import pallas as pl
from jax.experimental.pallas import tpu as pltpu
from jax.sharding import PartitionSpec as P

AXES = ("row", "col")
EXACT = lax.Precision.HIGHEST
LEVELS = 32767.0
EXTRA = 16


def sent(value, to):
    nrows, ncols = lax.axis_size("row"), lax.axis_size("col")
    pairs = []
    for r in range(nrows):
        for c in range(ncols):
            r_to, c_to = to(r, c)
            pairs.append((r * ncols + c, (r_to % nrows) * ncols + c_to))
    return lax.ppermute(value, AXES, pairs)


def scale_of(exponent, mantissa):
    return jnp.exp2(exponent) * (mantissa * (1.0 / (LEVELS * LEVELS)))


def coded(block):
    largest = jnp.maximum(jnp.max(jnp.abs(block), axis=0, keepdims=True), 1e-30)
    exponent = jnp.floor(jnp.log2(largest * 1.0001)) + 1.0
    mantissa = jnp.ceil(largest * jnp.exp2(-exponent) * LEVELS)
    scale = scale_of(exponent, mantissa)
    values = jnp.clip(jnp.round(block * (1.0 / scale)), -LEVELS, LEVELS)
    at = lax.broadcasted_iota(jnp.int32, (EXTRA, block.shape[1]), 0)
    tail = jnp.where(at == 0, exponent, mantissa)
    return jnp.concatenate([values, tail], axis=0).astype(jnp.int32).astype(jnp.int16)


def decoded(code):
    wide = code.astype(jnp.int32).astype(jnp.float32)
    rows = code.shape[0] - EXTRA
    return wide[:rows] * scale_of(wide[rows : rows + 1], wide[rows + 1 : rows + 2])


def product_kernel(back, ids_ref, weight_ref, perm_ref, own_ref, other_ref, *refs):
    *near_refs, tiles_ref = refs[:4]
    out_refs = refs[4:8]
    tile_ref, raw_ref, omega_ref, sems = refs[8:]
    slots, points, probes = own_ref.shape
    length = raw_ref.shape[1]
    nz = len(out_refs)
    step = 512

    def tile_slot(k):
        return k if back else k ^ ids_ref[2]

    def piece_copy(k, q):
        rows = pl.ds(q * step, step)
        return pltpu.make_async_copy(tiles_ref.at[tile_slot(k), rows], tile_ref.at[k, rows], sems.at[k, q])

    for k in range(slots):
        for q in range(length // step):
            piece_copy(k, q).start()

    def slot_step(k, carry):
        for d in range(nz):
            for a in range(2):
                piece = near_refs[d - 1][k, a] if d else (other_ref[k] if a else own_ref[k])
                at = (nz * a + d) * points
                raw_ref[:, at : at + points] = piece.T

        def order_step(i, carry):
            at = pl.multiple_of(i * step, step)
            index = perm_ref[k, :, pl.ds(at, step)] ^ (ids_ref[0] * points)
            place = lax.broadcasted_iota(jnp.int32, (length, step), 0)
            chosen = jnp.where(place == index, 1.0, 0.0).astype(jnp.bfloat16)
            found = jnp.dot(raw_ref[...], chosen, preferred_element_type=jnp.float32)
            if back:
                omega_ref[:, pl.ds(at, step)] = found.astype(jnp.bfloat16)
            else:
                omega_ref[pl.ds(at, step), :] = found.T.astype(jnp.bfloat16)
            return carry

        lax.fori_loop(0, length // step, order_step, 0)
        for q in range(length // step):
            piece_copy(k, q).wait()
        weight = weight_ref[tile_slot(k)]
        slot = k ^ ids_ref[2]
        for d in range(nz):
            for a in range(2):
                at = pl.multiple_of((a * nz + (ids_ref[1] ^ d)) * points, points)
                if back:
                    value = jnp.dot(omega_ref[...], tile_ref[k, :, pl.ds(at, points)], preferred_element_type=jnp.float32).T
                else:
                    value = jnp.dot(tile_ref[k, pl.ds(at, points), :], omega_ref[...], preferred_element_type=jnp.float32)
                out_refs[d][slot, a] = coded(value * weight)
        return carry

    lax.fori_loop(0, slots, slot_step, 0)


def products(ids, weight, perm, own, other, near, tiles, back):
    slots, points, probes = own.shape
    length = tiles.shape[1]
    nz = len(near) + 1
    shape = (slots, 2, points + EXTRA, probes)
    smem, vmem = pl.BlockSpec(memory_space=pltpu.SMEM), pl.BlockSpec(memory_space=pltpu.VMEM)
    return pl.pallas_call(
        functools.partial(product_kernel, back),
        out_shape=[jax.ShapeDtypeStruct(shape, jnp.int16)] * nz,
        in_specs=[smem, smem] + [vmem] * (3 + len(near)) + [pl.BlockSpec(memory_space=pl.ANY)],
        out_specs=[vmem] * nz,
        scratch_shapes=[
            pltpu.VMEM(tiles.shape, jnp.bfloat16),
            pltpu.VMEM((probes, length), jnp.bfloat16),
            pltpu.VMEM((probes, length) if back else (length, probes), jnp.bfloat16),
            pltpu.SemaphoreType.DMA((slots, length // 512)),
        ],
        compiler_params=pltpu.CompilerParams(vmem_limit_bytes=40 << 20),
        cost_estimate=pl.CostEstimate(
            flops=slots * 4 * length * length * probes, bytes_accessed=22 << 20, transcendentals=0
        ),
        name="product_back" if back else "product_ahead",
    )(ids, weight, perm, own, other, *near, tiles)


def sum_kernel(*refs):
    *in_refs, out_ref = refs
    for k in range(out_ref.shape[0]):
        for a in range(out_ref.shape[1]):
            total = decoded(in_refs[0][k, a])
            for ref in in_refs[1:]:
                total = total + decoded(ref[k, a])
            out_ref[k, a] = coded(total)


def summed(codes):
    return pl.pallas_call(sum_kernel, out_shape=jax.ShapeDtypeStruct(codes[0].shape, jnp.int16), name="sum_back")(*codes)


def merge_kernel(ids_ref, *refs):
    *in_refs, kept_ref, code_ref = refs
    plane = ids_ref[3]
    for a in range(2):
        for ref_of, slot in ((kept_ref, plane), (code_ref, 1 - plane)):
            total = decoded(in_refs[0][slot, a])
            for ref in in_refs[1:]:
                total = total + decoded(ref[slot, a])
            ref_of[a] = total if ref_of is kept_ref else coded(total)


def merged(ids, codes):
    _, _, rows, probes = codes[0].shape
    return pl.pallas_call(
        merge_kernel,
        in_specs=[pl.BlockSpec(memory_space=pltpu.SMEM)] + [pl.BlockSpec(memory_space=pltpu.VMEM)] * len(codes),
        out_shape=[
            jax.ShapeDtypeStruct((2, rows - EXTRA, probes), jnp.float32),
            jax.ShapeDtypeStruct((2, rows, probes), jnp.int16),
        ],
        name="merge",
    )(ids, *codes)


def gram_kernel(ids_ref, kept_ref, code_ref, own_ref, other_ref, gram_ref):
    plane = ids_ref[3]
    total = None
    for ref, a in ((own_ref, plane), (other_ref, 1 - plane)):
        block = kept_ref[a] + decoded(code_ref[a])
        ref[...] = block
        part = lax.dot_general(
            block, block, (((0,), (0,)), ((), ())), preferred_element_type=jnp.float32, precision=EXACT
        )
        total = part if total is None else total + part
    gram_ref[...] = total


def gram_of(ids, kept, code):
    _, points, probes = kept.shape
    block = jax.ShapeDtypeStruct((points, probes), jnp.float32)
    return pl.pallas_call(
        gram_kernel,
        in_specs=[pl.BlockSpec(memory_space=pltpu.SMEM)] + [pl.BlockSpec(memory_space=pltpu.VMEM)] * 2,
        out_shape=[block, block, jax.ShapeDtypeStruct((probes, probes), jnp.float32)],
        name="gram",
    )(ids, kept, code)

def half_inverse(a_ref, out_ref, m_ref, tall_ref, u_ref, v_ref):
    n, size = a_ref.shape[0], u_ref.shape[0]
    rows = lax.broadcasted_iota(jnp.int32, (n, n), 0)
    cols = lax.broadcasted_iota(jnp.int32, (n, n), 1)
    m_ref[...] = (rows == cols).astype(jnp.float32)
    for ref in (tall_ref, u_ref, v_ref):
        ref[...] = jnp.zeros_like(ref)
    lane = lax.broadcasted_iota(jnp.int32, (size, n), 1)
    sub = lax.broadcasted_iota(jnp.int32, (size, n), 0)

    def spread(array, i):
        return jnp.broadcast_to(array[i : i + 1, :], (size, n))

    def group(b, carry):
        at = pl.multiple_of(b * size, size)
        u, v, near = u_ref[...], v_ref[...], tall_ref[pl.ds(at, size), :]
        panel, inverse = a_ref[pl.ds(at, size), :], m_ref[pl.ds(at, size), :]
        old_a, old_m, tall = a_ref[...], m_ref[...], tall_ref[...]
        for t in range(size):
            factor = jnp.broadcast_to(near[:, t : t + 1], (size, n))
            panel = panel - factor * u[t : t + 1, :]
            inverse = inverse - factor * v[t : t + 1, :]
        small = pltpu.roll(panel, n - at, axis=1)
        s = [[None] * size for _ in range(size)]
        e = [[None] * size for _ in range(size)]
        for t in range(size):
            column = jnp.broadcast_to(small[:, t : t + 1], (size, n))
            for i in range(t, size):
                s[i][t] = spread(column, i)
        for t in range(size - 1):
            ratio = 1.0 / s[t][t]
            for i in range(t + 1, size):
                factor = s[i][t] * ratio
                for j in range(t + 1, i + 1):
                    s[i][j] = s[i][j] - factor * s[j][t]
                for j in range(t):
                    e[i][j] = e[i][j] - factor * e[t][j]
                e[i][t] = -factor
        scale = s[0][0]
        for t in range(1, size):
            scale = jnp.where(sub == t, s[t][t], scale)
        scale = lax.rsqrt(scale)
        new_u, new_v = panel, inverse
        for t in range(size - 1):
            factor = jnp.zeros((size, n), jnp.float32)
            for i in range(t + 1, size):
                factor = jnp.where(sub == i, e[i][t], factor)
            new_u = new_u + factor * panel[t : t + 1, :]
            new_v = new_v + factor * inverse[t : t + 1, :]
        new_u = jnp.where(lane >= at + sub, new_u * scale, 0.0)
        new_v = new_v * scale
        for t in range(size):
            factor = jnp.broadcast_to(tall[:, t : t + 1], (n, n))
            old_a = old_a - factor * u[t : t + 1, :]
            old_m = old_m - factor * v[t : t + 1, :]
        a_ref[...], m_ref[...] = old_a, old_m
        out_ref[pl.ds(at, size), :] = new_v
        u_ref[...], v_ref[...] = new_u, new_v
        tall_ref[...] = new_u.T
        return carry

    lax.fori_loop(0, n // size, group, 0)


def factor_kernel(scale, g1_ref, g2_ref, own_ref, other_ref, own_out, other_out, a_ref, m1_ref, m2_ref, *work):
    half = a_ref.shape[0]

    def product(a, b, over):
        return lax.dot_general(
            a, b, ((over[:1], over[1:]), ((), ())), preferred_element_type=jnp.float32, precision=EXACT
        )

    def gram(rows, cols):
        return (g1_ref[rows, cols] + g2_ref[rows, cols]) * scale

    low, high = slice(0, half), slice(half, 2 * half)
    a_ref[...] = gram(low, low)
    half_inverse(a_ref, m1_ref, *work)
    first = m1_ref[...]
    cross = product(first, gram(low, high), (1, 0))
    a_ref[...] = gram(high, high) - product(cross, cross, (0, 0))
    half_inverse(a_ref, m2_ref, *work)
    second = m2_ref[...]
    mixed = -product(second, product(cross, first, (0, 0)), (1, 0))
    for ref, out in ((own_ref, own_out), (other_ref, other_out)):
        left, right = ref[:, low], ref[:, high]
        out[:, low] = product(left, first, (1, 1))
        out[:, high] = product(left, mixed, (1, 1)) + product(right, second, (1, 1))


def orthogonal(gram, gram_more, own, other, scale):
    half = gram.shape[0] // 2
    return pl.pallas_call(
        functools.partial(factor_kernel, scale),
        out_shape=[jax.ShapeDtypeStruct(own.shape, jnp.float32)] * 2,
        scratch_shapes=[
            pltpu.VMEM(shape, jnp.float32) for shape in [(half, half)] * 4 + [(half, 8), (8, half), (8, half)]
        ],
        name="orthogonal",
    )(gram, gram_more, own, other)


def per_device(tiles, probe, cluster_perm, tile_keep):
    row_id = lax.axis_index("row")
    col_id = lax.axis_index("col")
    nrows = lax.axis_size("row")
    ncols = lax.axis_size("col")
    points, tile_len = probe.shape[1], tiles.shape[1]
    nz = ncols // 2
    plane, depth = col_id // nz, col_id % nz
    wraps = (row_id + col_id >= nrows).astype(jnp.int32)
    ids = jnp.stack([col_id, depth, wraps, plane]).astype(jnp.int32)
    weight = jnp.where(col_id == 0, 0.5, tile_keep[:, 0, 0].astype(jnp.float32))

    def same(d):
        return lambda r, c: (r, c ^ d)

    def slanted(d):
        return lambda r, c: (r + c - (c ^ d), c ^ d)

    other = sent(probe, same(nz))
    far_own = sent(probe, lambda r, c: (r - c, c))
    far_other = sent(probe, lambda r, c: (r - (c ^ nz), c ^ nz))
    far_perm = sent(cluster_perm, lambda r, c: (r - c, c))
    pair = jnp.stack([probe, other], axis=1)
    gathered = [sent(pair, same(d)) for d in range(1, nz)]
    gathered, far_own, far_other = lax.optimization_barrier((gathered, far_own, far_other))
    far_pair = jnp.stack([far_own, far_other], axis=1)
    far_gathered = [sent(far_pair, slanted(d)) for d in range(1, nz)]

    perm, far_perm = (x.reshape(-1, 1, tile_len) for x in (cluster_perm, far_perm))
    back = products(ids, weight, perm, probe, other, gathered, tiles, True)
    back = [back[0]] + [sent(back[d], slanted(d)) for d in range(1, nz)]
    ahead = products(ids, weight, far_perm, far_own, far_other, far_gathered, tiles, False)
    ahead = [ahead[0]] + [sent(ahead[d], same(d)) for d in range(1, nz)]
    arrived = sent(summed(back), lambda r, c: (r + c, c))
    kept, code = merged(ids, [*ahead, arrived])
    own, swapped, gram = gram_of(ids, kept, sent(code, same(nz)))
    gram = gram + sent(gram, same(1))
    own_basis, swapped_basis = orthogonal(gram, sent(gram, same(nz - 1)), own, swapped, 1.0 / tile_len)

    def placed(mine, theirs):
        theirs = sent(theirs, same(nz))
        return jnp.where(plane == 0, jnp.stack([mine, theirs]), jnp.stack([theirs, mine]))

    return (placed(own, swapped), placed(own_basis, swapped_basis))


def solution(mesh):
    whole = P(None, ("row", "col"), None)
    return jax.shard_map(
        per_device,
        mesh=mesh,
        in_specs=(P(None, "row", "col"), whole, P(None, "row", None), P(None, "row", "col")),
        out_specs=(whole, whole),
        check_vma=False,
    )
```

```python
import functools

import jax
import jax.numpy as jnp
from jax import lax
from jax.experimental import pallas as pl
from jax.experimental.pallas import tpu as pltpu
from jax.sharding import PartitionSpec as P

AXES = ("row", "col")
EXACT = lax.Precision.HIGHEST
LEVELS = 32767.0
EXTRA = 16


def sent(value, to):
    nrows, ncols = lax.axis_size("row"), lax.axis_size("col")
    pairs = []
    for r in range(nrows):
        for c in range(ncols):
            r_to, c_to = to(r, c)
            pairs.append((r * ncols + c, (r_to % nrows) * ncols + c_to))
    return lax.ppermute(value, AXES, pairs)


def scale_of(exponent, mantissa):
    return jnp.exp2(exponent) * (mantissa * (1.0 / (LEVELS * LEVELS)))


def coded(block):
    largest = jnp.maximum(jnp.max(jnp.abs(block), axis=0, keepdims=True), 1e-30)
    exponent = jnp.floor(jnp.log2(largest * 1.0001)) + 1.0
    mantissa = jnp.ceil(largest * jnp.exp2(-exponent) * LEVELS)
    scale = scale_of(exponent, mantissa)
    values = jnp.clip(jnp.round(block * (1.0 / scale)), -LEVELS, LEVELS)
    at = lax.broadcasted_iota(jnp.int32, (EXTRA, block.shape[1]), 0)
    tail = jnp.where(at == 0, exponent, mantissa)
    return jnp.concatenate([values, tail], axis=0).astype(jnp.int32).astype(jnp.int16)


def decoded(code):
    wide = code.astype(jnp.int32).astype(jnp.float32)
    rows = code.shape[0] - EXTRA
    return wide[:rows] * scale_of(wide[rows : rows + 1], wide[rows + 1 : rows + 2])


def product_kernel(back, ids_ref, weight_ref, perm_ref, *refs):
    *pair_refs, plane_ref, cross_ref, tiles_ref = refs[:7]
    out_refs = refs[7:11]
    tile_ref, raw_ref, omega_ref, sems = refs[11:]
    nz, points, probes = plane_ref.shape
    slots = perm_ref.shape[0]
    length = raw_ref.shape[1]
    step = 512

    def tile_slot(k):
        return k if back else k ^ ids_ref[2]

    def piece_copy(k, q):
        rows = pl.ds(q * step, step)
        return pltpu.make_async_copy(tiles_ref.at[tile_slot(k), rows], tile_ref.at[k, rows], sems.at[k, q])

    for k in range(slots):
        for q in range(length // step):
            piece_copy(k, q).start()

    def slot_step(k, carry):
        for slot in range(slots):

            @pl.when(k == slot)
            def _(slot=slot):
                for d in range(nz):
                    for a in range(2):
                        piece = (cross_ref[d] if a else plane_ref[d]) if slot else pair_refs[d][a]
                        at = (nz * a + d) * points
                        raw_ref[:, at : at + points] = piece.T

        def order_step(i, carry):
            at = pl.multiple_of(i * step, step)
            index = perm_ref[k, :, pl.ds(at, step)] ^ (ids_ref[0] * points)
            place = lax.broadcasted_iota(jnp.int32, (length, step), 0)
            chosen = jnp.where(place == index, 1.0, 0.0).astype(jnp.bfloat16)
            found = jnp.dot(raw_ref[...], chosen, preferred_element_type=jnp.float32)
            if back:
                omega_ref[:, pl.ds(at, step)] = found.astype(jnp.bfloat16)
            else:
                omega_ref[pl.ds(at, step), :] = found.T.astype(jnp.bfloat16)
            return carry

        lax.fori_loop(0, length // step, order_step, 0)
        for q in range(length // step):
            piece_copy(k, q).wait()
        weight = weight_ref[tile_slot(k)]
        slot = k ^ ids_ref[2]
        for d in range(nz):
            for a in range(2):
                at = pl.multiple_of((a * nz + (ids_ref[1] ^ d)) * points, points)
                if back:
                    value = jnp.dot(omega_ref[...], tile_ref[k, :, pl.ds(at, points)], preferred_element_type=jnp.float32).T
                else:
                    value = jnp.dot(tile_ref[k, pl.ds(at, points), :], omega_ref[...], preferred_element_type=jnp.float32)
                out_refs[d][slot, a] = coded(value * weight)
        return carry

    lax.fori_loop(0, slots, slot_step, 0)


def products(ids, weight, perm, pairs, plane, cross, tiles, back):
    nz, points, probes = plane.shape
    slots, length = tiles.shape[:2]
    shape = (slots, 2, points + EXTRA, probes)
    smem, vmem = pl.BlockSpec(memory_space=pltpu.SMEM), pl.BlockSpec(memory_space=pltpu.VMEM)
    return pl.pallas_call(
        functools.partial(product_kernel, back),
        out_shape=[jax.ShapeDtypeStruct(shape, jnp.int16)] * nz,
        in_specs=[smem, smem] + [vmem] * (3 + nz) + [pl.BlockSpec(memory_space=pl.ANY)],
        out_specs=[vmem] * nz,
        scratch_shapes=[
            pltpu.VMEM(tiles.shape, jnp.bfloat16),
            pltpu.VMEM((probes, length), jnp.bfloat16),
            pltpu.VMEM((probes, length) if back else (length, probes), jnp.bfloat16),
            pltpu.SemaphoreType.DMA((slots, length // 512)),
        ],
        compiler_params=pltpu.CompilerParams(vmem_limit_bytes=40 << 20),
        cost_estimate=pl.CostEstimate(
            flops=slots * 4 * length * length * probes, bytes_accessed=22 << 20, transcendentals=0
        ),
        name="product_back" if back else "product_ahead",
    )(ids, weight, perm, *pairs, plane, cross, tiles)


def sum_kernel(*refs):
    *in_refs, out_ref = refs
    for k in range(out_ref.shape[0]):
        for a in range(out_ref.shape[1]):
            total = decoded(in_refs[0][k, a])
            for ref in in_refs[1:]:
                total = total + decoded(ref[k, a])
            out_ref[k, a] = coded(total)


def summed(codes):
    return pl.pallas_call(sum_kernel, out_shape=jax.ShapeDtypeStruct(codes[0].shape, jnp.int16), name="sum_back")(*codes)


def merge_kernel(ids_ref, *refs):
    *in_refs, kept_ref, code_ref = refs
    plane = ids_ref[3]
    for a in range(2):
        for ref_of, slot in ((kept_ref, plane), (code_ref, 1 - plane)):
            total = decoded(in_refs[0][slot, a])
            for ref in in_refs[1:]:
                total = total + decoded(ref[slot, a])
            ref_of[a] = total if ref_of is kept_ref else coded(total)


def merged(ids, codes):
    _, _, rows, probes = codes[0].shape
    return pl.pallas_call(
        merge_kernel,
        in_specs=[pl.BlockSpec(memory_space=pltpu.SMEM)] + [pl.BlockSpec(memory_space=pltpu.VMEM)] * len(codes),
        out_shape=[
            jax.ShapeDtypeStruct((2, rows - EXTRA, probes), jnp.float32),
            jax.ShapeDtypeStruct((2, rows, probes), jnp.int16),
        ],
        name="merge",
    )(ids, *codes)


def gram_kernel(ids_ref, kept_ref, code_ref, samples_ref, other_ref, gram_ref):
    plane = ids_ref[3]
    half = gram_ref.shape[1]
    total = None
    for a in (plane, 1 - plane):
        block = kept_ref[a] + decoded(code_ref[a])
        if total is None:
            samples_ref[plane] = block
        else:
            other_ref[...] = block
        left, right = block[:, :half], block[:, half:]
        parts = [
            lax.dot_general(x, y, (((0,), (0,)), ((), ())), preferred_element_type=jnp.float32, precision=EXACT)
            for x, y in ((left, left), (left, right), (right, right))
        ]
        total = parts if total is None else [x + y for x, y in zip(total, parts)]
    for n, part in enumerate(total):
        gram_ref[n * half : (n + 1) * half, :] = part


def gram_of(ids, kept, code):
    _, points, probes = kept.shape
    return pl.pallas_call(
        gram_kernel,
        in_specs=[pl.BlockSpec(memory_space=pltpu.SMEM)] + [pl.BlockSpec(memory_space=pltpu.VMEM)] * 2,
        out_shape=[
            jax.ShapeDtypeStruct((2, points, probes), jnp.float32),
            jax.ShapeDtypeStruct((points, probes), jnp.float32),
            jax.ShapeDtypeStruct((3 * probes // 2, probes // 2), jnp.float32),
        ],
        name="gram",
    )(ids, kept, code)


def half_inverse(a_ref, out_ref, m_ref, tall_ref, u_ref, v_ref):
    n, size = a_ref.shape[0], u_ref.shape[0]
    rows = lax.broadcasted_iota(jnp.int32, (n, n), 0)
    cols = lax.broadcasted_iota(jnp.int32, (n, n), 1)
    m_ref[...] = (rows == cols).astype(jnp.float32)
    for ref in (tall_ref, u_ref, v_ref):
        ref[...] = jnp.zeros_like(ref)
    lane = lax.broadcasted_iota(jnp.int32, (size, n), 1)
    sub = lax.broadcasted_iota(jnp.int32, (size, n), 0)

    def spread(array, i):
        return jnp.broadcast_to(array[i : i + 1, :], (size, n))

    def group(b, carry):
        at = pl.multiple_of(b * size, size)
        u, v, near = u_ref[...], v_ref[...], tall_ref[pl.ds(at, size), :]
        panel, inverse = a_ref[pl.ds(at, size), :], m_ref[pl.ds(at, size), :]
        old_a, old_m, tall = a_ref[...], m_ref[...], tall_ref[...]
        for t in range(size):
            factor = jnp.broadcast_to(near[:, t : t + 1], (size, n))
            panel = panel - factor * u[t : t + 1, :]
            inverse = inverse - factor * v[t : t + 1, :]
        small = pltpu.roll(panel, n - at, axis=1)
        s = [[None] * size for _ in range(size)]
        e = [[None] * size for _ in range(size)]
        for t in range(size):
            column = jnp.broadcast_to(small[:, t : t + 1], (size, n))
            for i in range(t, size):
                s[i][t] = spread(column, i)
        for t in range(size - 1):
            ratio = 1.0 / s[t][t]
            for i in range(t + 1, size):
                factor = s[i][t] * ratio
                for j in range(t + 1, i + 1):
                    s[i][j] = s[i][j] - factor * s[j][t]
                for j in range(t):
                    e[i][j] = e[i][j] - factor * e[t][j]
                e[i][t] = -factor
        scale = s[0][0]
        for t in range(1, size):
            scale = jnp.where(sub == t, s[t][t], scale)
        scale = lax.rsqrt(scale)
        new_u, new_v = panel, inverse
        for t in range(size - 1):
            factor = jnp.zeros((size, n), jnp.float32)
            for i in range(t + 1, size):
                factor = jnp.where(sub == i, e[i][t], factor)
            new_u = new_u + factor * panel[t : t + 1, :]
            new_v = new_v + factor * inverse[t : t + 1, :]
        new_u = jnp.where(lane >= at + sub, new_u * scale, 0.0)
        new_v = new_v * scale
        for t in range(size):
            factor = jnp.broadcast_to(tall[:, t : t + 1], (n, n))
            old_a = old_a - factor * u[t : t + 1, :]
            old_m = old_m - factor * v[t : t + 1, :]
        a_ref[...], m_ref[...] = old_a, old_m
        out_ref[pl.ds(at, size), :] = new_v
        u_ref[...], v_ref[...] = new_u, new_v
        tall_ref[...] = new_u.T
        return carry

    lax.fori_loop(0, n // size, group, 0)


def factor_kernel(scale, ids_ref, samples_ref, other_ref, *refs):
    *gram_refs, basis_ref, out_ref, a_ref, m1_ref, m2_ref = refs[:9]
    work = refs[9:]
    half = a_ref.shape[0]
    plane = ids_ref[3]

    def product(a, b, over):
        return lax.dot_general(
            a, b, ((over[:1], over[1:]), ((), ())), preferred_element_type=jnp.float32, precision=EXACT
        )

    def gram(n):
        rows = slice(n * half, (n + 1) * half)
        one, two, three, four = (ref[rows, :] for ref in gram_refs)
        return ((one + two) + (three + four)) * scale

    a_ref[...] = gram(0)
    half_inverse(a_ref, m1_ref, *work)
    first = m1_ref[...]
    cross = product(first, gram(1), (1, 0))
    a_ref[...] = gram(2) - product(cross, cross, (0, 0))
    half_inverse(a_ref, m2_ref, *work)
    second = m2_ref[...]
    mixed = -product(second, product(cross, first, (0, 0)), (1, 0))
    for n, block in enumerate((samples_ref[plane], other_ref[...])):
        left, right = block[:, :half], block[:, half:]
        made = (product(left, first, (1, 1)), product(left, mixed, (1, 1)) + product(right, second, (1, 1)))
        for m, value in enumerate(made):
            columns = slice(m * half, (m + 1) * half)
            if n:
                out_ref[:, columns] = value
            else:
                basis_ref[plane, :, columns] = value


def orthogonal(ids, samples, other, grams, scale):
    half = grams[0].shape[1]
    return pl.pallas_call(
        functools.partial(factor_kernel, scale),
        in_specs=[pl.BlockSpec(memory_space=pltpu.SMEM)] + [pl.BlockSpec(memory_space=pltpu.VMEM)] * (2 + len(grams)),
        out_shape=[jax.ShapeDtypeStruct(x.shape, jnp.float32) for x in (samples, other)],
        scratch_shapes=[
            pltpu.VMEM(shape, jnp.float32) for shape in [(half, half)] * 4 + [(half, 8), (8, half), (8, half)]
        ],
        name="orthogonal",
    )(ids, samples, other, *grams)


def per_device(tiles, probe, cluster_perm, tile_keep):
    row_id = lax.axis_index("row")
    col_id = lax.axis_index("col")
    nrows = lax.axis_size("row")
    ncols = lax.axis_size("col")
    tile_len = tiles.shape[1]
    nz = ncols // 2
    plane, depth = col_id // nz, col_id % nz
    wraps = (row_id + col_id >= nrows).astype(jnp.int32)
    ids = jnp.stack([col_id, depth, wraps, plane]).astype(jnp.int32)
    weight = jnp.where(col_id == 0, 0.5, tile_keep[:, 0, 0].astype(jnp.float32))

    def same(d):
        return lambda r, c: (r, c ^ d)

    def slanted(d):
        return lambda r, c: (r + c - (c ^ d), c ^ d)

    def far(r, c):
        return (r - c, c)

    depths = range(1, nz)
    other = sent(probe[0], same(nz))
    singles = [sent(probe[1], same(d)) for d in depths]
    pair = jnp.stack([probe[0], other])
    line = jnp.stack([probe[1], *singles])
    pairs = [sent(pair, same(d)) for d in depths]
    cross = sent(line, same(nz))

    far_pair = sent(pair, far)
    far_line = sent(line, far)
    far_perm = sent(cluster_perm, far)
    pairs, cross, far_pair = lax.optimization_barrier((pairs, cross, far_pair))
    far_pairs = [sent(far_pair, slanted(d)) for d in depths]
    far_cross = sent(cross, far)

    perm, far_perm = (x.reshape(-1, 1, tile_len) for x in (cluster_perm, far_perm))
    back = products(ids, weight, perm, [pair, *pairs], line, cross, tiles, True)
    back, far_pairs = lax.optimization_barrier((back, far_pairs))
    back = [back[0]] + [sent(back[d], slanted(d)) for d in depths]
    ahead = products(ids, weight, far_perm, [far_pair, *far_pairs], far_line, far_cross, tiles, False)
    ahead = [ahead[0]] + [sent(ahead[d], same(d)) for d in depths]
    arrived = sent(summed(back), lambda r, c: (r + c, c))
    kept, code = merged(ids, [*ahead, arrived])
    samples, swapped, gram = gram_of(ids, kept, sent(code, same(nz)))
    grams = [gram] + [sent(gram, same(d)) for d in depths]
    basis, swapped_basis = orthogonal(ids, samples, swapped, grams, 1.0 / tile_len)

    def placed(array, theirs):
        return lax.dynamic_update_index_in_dim(array, sent(theirs, same(nz)), 1 - plane, 0)

    return (placed(samples, swapped), placed(basis, swapped_basis))


def solution(mesh):
    whole = P(None, ("row", "col"), None)
    return jax.shard_map(
        per_device,
        mesh=mesh,
        in_specs=(P(None, "row", "col"), whole, P(None, "row", None), P(None, "row", "col")),
        out_specs=(whole, whole),
        check_vma=False,
    )
```

```python
import functools

import jax
import jax.numpy as jnp
from jax import lax
from jax.experimental import pallas as pl
from jax.experimental.pallas import tpu as pltpu
from jax.sharding import PartitionSpec as P

AXES = ("row", "col")
EXACT = lax.Precision.HIGHEST
LEVELS = 32767.0
EXTRA = 16


def sent(value, to):
    nrows, ncols = lax.axis_size("row"), lax.axis_size("col")
    pairs = []
    for r in range(nrows):
        for c in range(ncols):
            r_to, c_to = to(r, c)
            pairs.append((r * ncols + c, (r_to % nrows) * ncols + c_to))
    return lax.ppermute(value, AXES, pairs)


def scale_of(exponent, mantissa):
    return jnp.exp2(exponent) * (mantissa * (1.0 / (LEVELS * LEVELS)))


def coded(block):
    largest = jnp.maximum(jnp.max(jnp.abs(block), axis=0, keepdims=True), 1e-30)
    exponent = jnp.floor(jnp.log2(largest * 1.0001)) + 1.0
    mantissa = jnp.ceil(largest * jnp.exp2(-exponent) * LEVELS)
    scale = scale_of(exponent, mantissa)
    values = jnp.clip(jnp.round(block * (1.0 / scale)), -LEVELS, LEVELS)
    at = lax.broadcasted_iota(jnp.int32, (EXTRA, block.shape[1]), 0)
    tail = jnp.where(at == 0, exponent, mantissa)
    return jnp.concatenate([values, tail], axis=0).astype(jnp.int32).astype(jnp.int16)


def decoded(code):
    wide = code.astype(jnp.int32).astype(jnp.float32)
    rows = code.shape[0] - EXTRA
    return wide[:rows] * scale_of(wide[rows : rows + 1], wide[rows + 1 : rows + 2])


def product_kernel(back, ids_ref, weight_ref, perm_ref, *refs):
    *pair_refs, plane_ref, cross_ref, tiles_ref = refs[:7]
    *out_refs, tile_ref, raw_ref, omega_ref, sems = refs[7:]
    nz, points, probes = plane_ref.shape
    slots = perm_ref.shape[0]
    length = raw_ref.shape[1]
    step = 512

    def tile_slot(k):
        return k if back else k ^ ids_ref[2]

    def piece_copy(k, q):
        rows = pl.ds(q * step, step)
        return pltpu.make_async_copy(tiles_ref.at[tile_slot(k), rows], tile_ref.at[k, rows], sems.at[k, q])

    for n in range(slots):
        for q in range(length // step):
            piece_copy(n if back else n ^ ids_ref[3] ^ ids_ref[2], q).start()

    def slot_step(n, carry):
        k = n if back else n ^ ids_ref[3] ^ ids_ref[2]
        for slot in range(slots):

            @pl.when(k == slot)
            def _(slot=slot):
                for d in range(nz):
                    for a in range(2):
                        piece = (cross_ref[d] if a else plane_ref[d]) if slot else pair_refs[d][a]
                        at = (nz * a + d) * points
                        raw_ref[:, at : at + points] = piece.T

        def order_step(i, carry):
            at = pl.multiple_of(i * step, step)
            index = perm_ref[k, :, pl.ds(at, step)] ^ (ids_ref[0] * points)
            place = lax.broadcasted_iota(jnp.int32, (length, step), 0)
            chosen = jnp.where(place == index, 1.0, 0.0).astype(jnp.bfloat16)
            found = jnp.dot(raw_ref[...], chosen, preferred_element_type=jnp.float32)
            if back:
                omega_ref[:, pl.ds(at, step)] = found.astype(jnp.bfloat16)
            else:
                omega_ref[pl.ds(at, step), :] = found.T.astype(jnp.bfloat16)
            return carry

        lax.fori_loop(0, length // step, order_step, 0)
        for q in range(length // step):
            piece_copy(k, q).wait()
        weight = weight_ref[tile_slot(k)]
        for d in range(nz):
            for a in range(2):
                at = pl.multiple_of((a * nz + (ids_ref[1] ^ d)) * points, points)
                if back:
                    value = jnp.dot(omega_ref[...], tile_ref[k, :, pl.ds(at, points)], preferred_element_type=jnp.float32).T
                else:
                    value = jnp.dot(tile_ref[k, pl.ds(at, points), :], omega_ref[...], preferred_element_type=jnp.float32)
                code = coded(value * weight)
                if back:
                    out_refs[d][k ^ ids_ref[2], a] = code
                else:
                    for other in range(slots):

                        @pl.when(n == other)
                        def _(at=nz * other + d, code=code):
                            out_refs[at][a] = code

        return carry

    lax.fori_loop(0, slots, slot_step, 0)


def products(ids, weight, perm, pairs, plane, cross, tiles, back):
    nz, points, probes = plane.shape
    slots, length = tiles.shape[:2]
    shape = (slots, 2, points + EXTRA, probes) if back else (2, points + EXTRA, probes)
    outs = nz if back else 2 * nz
    smem, vmem = pl.BlockSpec(memory_space=pltpu.SMEM), pl.BlockSpec(memory_space=pltpu.VMEM)
    return pl.pallas_call(
        functools.partial(product_kernel, back),
        out_shape=[jax.ShapeDtypeStruct(shape, jnp.int16)] * outs,
        in_specs=[smem, smem] + [vmem] * (3 + nz) + [pl.BlockSpec(memory_space=pl.ANY)],
        out_specs=[vmem] * outs,
        scratch_shapes=[
            pltpu.VMEM(tiles.shape, jnp.bfloat16),
            pltpu.VMEM((probes, length), jnp.bfloat16),
            pltpu.VMEM((probes, length) if back else (length, probes), jnp.bfloat16),
            pltpu.SemaphoreType.DMA((slots, length // 512)),
        ],
        compiler_params=pltpu.CompilerParams(vmem_limit_bytes=40 << 20),
        cost_estimate=pl.CostEstimate(
            flops=slots * 4 * length * length * probes, bytes_accessed=22 << 20, transcendentals=0
        ),
        name="product_back" if back else "product_ahead",
    )(ids, weight, perm, *pairs, plane, cross, tiles)


def sum_kernel(ids_ref, *refs):
    *in_refs, own_ref, other_ref = refs
    for ref_of, slot in ((own_ref, ids_ref[3]), (other_ref, 1 - ids_ref[3])):
        for a in range(2):
            total = decoded(in_refs[0][slot, a])
            for ref in in_refs[1:]:
                total = total + decoded(ref[slot, a])
            ref_of[a] = coded(total)


def summed(ids, codes):
    return pl.pallas_call(
        sum_kernel,
        in_specs=[pl.BlockSpec(memory_space=pltpu.SMEM)] + [pl.BlockSpec(memory_space=pltpu.VMEM)] * len(codes),
        out_shape=[jax.ShapeDtypeStruct(codes[0].shape[1:], jnp.int16)] * 2,
        name="sum_back",
    )(ids, *codes)


def gram_kernel(ids_ref, *refs):
    *in_refs, samples_ref, other_ref, gram_ref = refs
    plane = ids_ref[3]
    half = gram_ref.shape[1]
    total = None
    for a in (plane, 1 - plane):
        block = decoded(in_refs[0][a])
        for ref in in_refs[1:]:
            block = block + decoded(ref[a])
        if total is None:
            samples_ref[plane] = block
        else:
            other_ref[...] = block
        left, right = block[:, :half], block[:, half:]
        parts = [
            lax.dot_general(x, y, (((0,), (0,)), ((), ())), preferred_element_type=jnp.float32, precision=EXACT)
            for x, y in ((left, left), (left, right), (right, right))
        ]
        total = parts if total is None else [x + y for x, y in zip(total, parts)]
    for n, part in enumerate(total):
        gram_ref[n * half : (n + 1) * half, :] = part


def gram_of(ids, codes):
    _, rows, probes = codes[0].shape
    points = rows - EXTRA
    return pl.pallas_call(
        gram_kernel,
        in_specs=[pl.BlockSpec(memory_space=pltpu.SMEM)] + [pl.BlockSpec(memory_space=pltpu.VMEM)] * len(codes),
        out_shape=[
            jax.ShapeDtypeStruct((2, points, probes), jnp.float32),
            jax.ShapeDtypeStruct((points, probes), jnp.float32),
            jax.ShapeDtypeStruct((3 * probes // 2, probes // 2), jnp.float32),
        ],
        name="gram",
    )(ids, *codes)


def half_inverse(a_ref, out_ref, m_ref, tall_ref, u_ref, v_ref):
    n, size = a_ref.shape[0], u_ref.shape[0]
    rows = lax.broadcasted_iota(jnp.int32, (n, n), 0)
    cols = lax.broadcasted_iota(jnp.int32, (n, n), 1)
    m_ref[...] = (rows == cols).astype(jnp.float32)
    for ref in (tall_ref, u_ref, v_ref):
        ref[...] = jnp.zeros_like(ref)
    lane = lax.broadcasted_iota(jnp.int32, (size, n), 1)
    sub = lax.broadcasted_iota(jnp.int32, (size, n), 0)

    def spread(array, i):
        return jnp.broadcast_to(array[i : i + 1, :], (size, n))

    def group(b, carry):
        at = pl.multiple_of(b * size, size)
        u, v, near = u_ref[...], v_ref[...], tall_ref[pl.ds(at, size), :]
        panel, inverse = a_ref[pl.ds(at, size), :], m_ref[pl.ds(at, size), :]
        old_a, old_m, tall = a_ref[...], m_ref[...], tall_ref[...]
        for t in range(size):
            factor = jnp.broadcast_to(near[:, t : t + 1], (size, n))
            panel = panel - factor * u[t : t + 1, :]
            inverse = inverse - factor * v[t : t + 1, :]
        small = pltpu.roll(panel, n - at, axis=1)
        s = [[None] * size for _ in range(size)]
        e = [[None] * size for _ in range(size)]
        for t in range(size):
            column = jnp.broadcast_to(small[:, t : t + 1], (size, n))
            for i in range(t, size):
                s[i][t] = spread(column, i)
        for t in range(size - 1):
            ratio = 1.0 / s[t][t]
            for i in range(t + 1, size):
                factor = s[i][t] * ratio
                for j in range(t + 1, i + 1):
                    s[i][j] = s[i][j] - factor * s[j][t]
                for j in range(t):
                    e[i][j] = e[i][j] - factor * e[t][j]
                e[i][t] = -factor
        scale = s[0][0]
        for t in range(1, size):
            scale = jnp.where(sub == t, s[t][t], scale)
        scale = lax.rsqrt(scale)
        new_u, new_v = panel, inverse
        for t in range(size - 1):
            factor = jnp.zeros((size, n), jnp.float32)
            for i in range(t + 1, size):
                factor = jnp.where(sub == i, e[i][t], factor)
            new_u = new_u + factor * panel[t : t + 1, :]
            new_v = new_v + factor * inverse[t : t + 1, :]
        new_u = jnp.where(lane >= at + sub, new_u * scale, 0.0)
        new_v = new_v * scale
        for t in range(size):
            factor = jnp.broadcast_to(tall[:, t : t + 1], (n, n))
            old_a = old_a - factor * u[t : t + 1, :]
            old_m = old_m - factor * v[t : t + 1, :]
        a_ref[...], m_ref[...] = old_a, old_m
        out_ref[pl.ds(at, size), :] = new_v
        u_ref[...], v_ref[...] = new_u, new_v
        tall_ref[...] = new_u.T
        return carry

    lax.fori_loop(0, n // size, group, 0)


def factor_kernel(scale, ids_ref, samples_ref, other_ref, *refs):
    *gram_refs, basis_ref, out_ref, a_ref, m1_ref, m2_ref = refs[:9]
    work = refs[9:]
    half = a_ref.shape[0]
    plane = ids_ref[3]

    def product(a, b, over):
        return lax.dot_general(
            a, b, ((over[:1], over[1:]), ((), ())), preferred_element_type=jnp.float32, precision=EXACT
        )

    def gram(n):
        rows = slice(n * half, (n + 1) * half)
        one, two, three, four = (ref[rows, :] for ref in gram_refs)
        return ((one + two) + (three + four)) * scale

    a_ref[...] = gram(0)
    half_inverse(a_ref, m1_ref, *work)
    first = m1_ref[...]
    cross = product(first, gram(1), (1, 0))
    a_ref[...] = gram(2) - product(cross, cross, (0, 0))
    half_inverse(a_ref, m2_ref, *work)
    second = m2_ref[...]
    mixed = -product(second, product(cross, first, (0, 0)), (1, 0))
    for n, block in enumerate((samples_ref[plane], other_ref[...])):
        left, right = block[:, :half], block[:, half:]
        made = (product(left, first, (1, 1)), product(left, mixed, (1, 1)) + product(right, second, (1, 1)))
        for m, value in enumerate(made):
            columns = slice(m * half, (m + 1) * half)
            if n:
                out_ref[:, columns] = value
            else:
                basis_ref[plane, :, columns] = value


def orthogonal(ids, samples, other, grams, scale):
    half = grams[0].shape[1]
    return pl.pallas_call(
        functools.partial(factor_kernel, scale),
        in_specs=[pl.BlockSpec(memory_space=pltpu.SMEM)] + [pl.BlockSpec(memory_space=pltpu.VMEM)] * (2 + len(grams)),
        out_shape=[jax.ShapeDtypeStruct(x.shape, jnp.float32) for x in (samples, other)],
        scratch_shapes=[
            pltpu.VMEM(shape, jnp.float32) for shape in [(half, half)] * 4 + [(half, 8), (8, half), (8, half)]
        ],
        name="orthogonal",
    )(ids, samples, other, *grams)


def per_device(tiles, probe, cluster_perm, tile_keep):
    row_id = lax.axis_index("row")
    col_id = lax.axis_index("col")
    nrows = lax.axis_size("row")
    ncols = lax.axis_size("col")
    tile_len = tiles.shape[1]
    nz = ncols // 2
    plane, depth = col_id // nz, col_id % nz
    wraps = (row_id + col_id >= nrows).astype(jnp.int32)
    ids = jnp.stack([col_id, depth, wraps, plane]).astype(jnp.int32)
    weight = jnp.where(col_id == 0, 0.5, tile_keep[:, 0, 0].astype(jnp.float32))

    def same(d):
        return lambda r, c: (r, c ^ d)

    def slanted(d):
        return lambda r, c: (r + c - (c ^ d), c ^ d)

    def far(r, c):
        return (r - c, c)

    depths = range(1, nz)
    other = sent(probe[0], same(nz))
    singles = [sent(probe[1], same(d)) for d in depths]
    pair = jnp.stack([probe[0], other])
    line = jnp.stack([probe[1], *singles])
    pairs = [sent(pair, same(d)) for d in depths]
    cross = sent(line, same(nz))

    far_pair = sent(pair, far)
    far_line = sent(line, far)
    far_perm = sent(cluster_perm, far)
    far_pairs = [sent(far_pair, slanted(d)) for d in depths]
    far_cross = sent(cross, far)

    perm, far_perm = (x.reshape(-1, 1, tile_len) for x in (cluster_perm, far_perm))
    back = products(ids, weight, perm, [pair, *pairs], line, cross, tiles, True)
    back, far_pairs = lax.optimization_barrier((back, far_pairs))
    back = [back[0]] + [sent(back[d], slanted(d)) for d in depths]
    ahead = products(ids, weight, far_perm, [far_pair, *far_pairs], far_line, far_cross, tiles, False)
    ahead = [ahead[0]] + [sent(ahead[o], same(o)) for o in range(1, ncols)]
    back_own, back_other = summed(ids, back)
    arrived = [sent(back_own, lambda r, c: (r + c, c)), sent(back_other, lambda r, c: (r + c, c ^ nz))]
    samples, swapped, gram = gram_of(ids, [*ahead, *arrived])
    grams = [gram] + [sent(gram, same(d)) for d in depths]
    basis, swapped_basis = orthogonal(ids, samples, swapped, grams, 1.0 / tile_len)

    def placed(array, theirs):
        return lax.dynamic_update_index_in_dim(array, sent(theirs, same(nz)), 1 - plane, 0)

    return (placed(samples, swapped), placed(basis, swapped_basis))


def solution(mesh):
    whole = P(None, ("row", "col"), None)
    return jax.shard_map(
        per_device,
        mesh=mesh,
        in_specs=(P(None, "row", "col"), whole, P(None, "row", None), P(None, "row", "col")),
        out_specs=(whole, whole),
        check_vma=False,
    )
```

```python
import functools

import jax
import jax.numpy as jnp
from jax import lax
from jax.experimental import pallas as pl
from jax.experimental.pallas import tpu as pltpu
from jax.sharding import PartitionSpec as P


AXES = ("row", "col")
EXACT = lax.Precision.HIGHEST
LEVELS = 32767.0
EXTRA = 16


def sent(value, to):
    nrows, ncols = lax.axis_size("row"), lax.axis_size("col")
    pairs = []
    for r in range(nrows):
        for c in range(ncols):
            r_to, c_to = to(r, c)
            pairs.append((r * ncols + c, (r_to % nrows) * ncols + c_to))
    return lax.ppermute(value, AXES, pairs)


def scale_of(exponent, mantissa):
    return jnp.exp2(exponent) * (mantissa * (1.0 / (LEVELS * LEVELS)))


def coded(block):
    largest = jnp.maximum(jnp.max(jnp.abs(block), axis=0, keepdims=True), 1e-30)
    exponent = jnp.floor(jnp.log2(largest * 1.0001)) + 1.0
    mantissa = jnp.ceil(largest * jnp.exp2(-exponent) * LEVELS)
    scale = scale_of(exponent, mantissa)
    values = jnp.clip(jnp.round(block * (1.0 / scale)), -LEVELS, LEVELS)
    at = lax.broadcasted_iota(jnp.int32, (EXTRA, block.shape[1]), 0)
    tail = jnp.where(at == 0, exponent, mantissa)
    return jnp.concatenate([values, tail], axis=0).astype(jnp.int32).astype(jnp.int16)


def decoded(code):
    wide = code.astype(jnp.int32).astype(jnp.float32)
    rows = code.shape[0] - EXTRA
    return wide[:rows] * scale_of(wide[rows : rows + 1], wide[rows + 1 : rows + 2])


def product_kernel(back, part, ids_ref, weight_ref, perm_ref, *refs):
    *pair_refs, plane_ref, cross_ref, tiles_ref = refs[:7]
    *out_refs, tile_ref, raw_ref, omega_ref, sems = refs[7:]
    nz, points, _ = plane_ref.shape
    length = raw_ref.shape[1]
    step = 512
    k = ids_ref[3] ^ ids_ref[2] ^ part
    tile_slot = k if back else k ^ ids_ref[2]

    def piece_copy(q):
        rows = pl.ds(q * step, step)
        return pltpu.make_async_copy(tiles_ref.at[tile_slot, rows], tile_ref.at[rows], sems.at[q])

    for q in range(length // step):
        piece_copy(q).start()
    for slot in range(2):

        @pl.when(k == slot)
        def _(slot=slot):
            for d in range(nz):
                for a in range(2):
                    piece = (cross_ref[d] if a else plane_ref[d]) if slot else pair_refs[d][a]
                    at = (nz * a + d) * points
                    raw_ref[:, at : at + points] = piece.T

    def order_step(i, carry):
        at = pl.multiple_of(i * step, step)
        index = perm_ref[k, :, pl.ds(at, step)] ^ (ids_ref[0] * points)
        place = lax.broadcasted_iota(jnp.int32, (length, step), 0)
        chosen = jnp.where(place == index, 1.0, 0.0).astype(jnp.bfloat16)
        found = jnp.dot(raw_ref[...], chosen, preferred_element_type=jnp.float32)
        if back:
            omega_ref[:, pl.ds(at, step)] = found.astype(jnp.bfloat16)
        else:
            omega_ref[pl.ds(at, step), :] = found.T.astype(jnp.bfloat16)
        return carry

    lax.fori_loop(0, length // step, order_step, 0)
    for q in range(length // step):
        piece_copy(q).wait()
    weight = weight_ref[tile_slot]
    for d in range(nz):
        for a in range(2):
            at = pl.multiple_of((a * nz + (ids_ref[1] ^ d)) * points, points)
            if back:
                value = jnp.dot(omega_ref[...], tile_ref[:, pl.ds(at, points)], preferred_element_type=jnp.float32).T
            else:
                value = jnp.dot(tile_ref[pl.ds(at, points), :], omega_ref[...], preferred_element_type=jnp.float32)
            code = coded(value * weight)
            if len(out_refs) == 1:
                out_refs[0][d, a] = code
            else:
                out_refs[d][a] = code


def products(ids, weight, perm, pairs, plane, cross, tiles, back, part):
    nz, points, probes = plane.shape
    length = tiles.shape[1]
    block = (2, points + EXTRA, probes)
    shapes = [(nz, *block)] if back and part else [block] * nz
    smem, vmem = pl.BlockSpec(memory_space=pltpu.SMEM), pl.BlockSpec(memory_space=pltpu.VMEM)
    return pl.pallas_call(
        functools.partial(product_kernel, back, part),
        out_shape=[jax.ShapeDtypeStruct(shape, jnp.int16) for shape in shapes],
        in_specs=[smem, smem] + [vmem] * (3 + nz) + [pl.BlockSpec(memory_space=pl.ANY)],
        out_specs=[vmem] * len(shapes),
        scratch_shapes=[
            pltpu.VMEM(tiles.shape[1:], jnp.bfloat16),
            pltpu.VMEM((probes, length), jnp.bfloat16),
            pltpu.VMEM((probes, length) if back else (length, probes), jnp.bfloat16),
            pltpu.SemaphoreType.DMA((length // 512,)),
        ],
        compiler_params=pltpu.CompilerParams(vmem_limit_bytes=32 << 20),
        cost_estimate=pl.CostEstimate(flops=4 * length * length * probes, bytes_accessed=11 << 20, transcendentals=0),
    )(ids, weight, perm, *pairs, plane, cross, tiles)


def sum_kernel(*refs):
    *in_refs, unread_ref, out_ref = refs
    for a in range(2):
        total = decoded(in_refs[0][a])
        for ref in in_refs[1:]:
            total = total + decoded(ref[a])
        out_ref[a] = coded(total)


def summed(codes, after):
    return pl.pallas_call(
        sum_kernel,
        in_specs=[pl.BlockSpec(memory_space=pltpu.VMEM)] * len(codes) + [pl.BlockSpec(memory_space=pl.ANY)],
        out_shape=jax.ShapeDtypeStruct(codes[0].shape, jnp.int16),
        name="sum_back",
    )(*codes, after)


def join_kernel(nz, *refs):
    more_ref = refs[nz]
    for d in range(nz):
        for a in range(2):
            refs[nz + 1 + d][a] = coded(decoded(refs[d][a]) + decoded(more_ref[d, a]))


def joined(codes, more):
    return pl.pallas_call(
        functools.partial(join_kernel, len(codes)),
        out_shape=[jax.ShapeDtypeStruct(x.shape, jnp.int16) for x in codes],
        name="join",
    )(*codes, more)


def gram_kernel(ids_ref, *refs):
    *in_refs, samples_ref, other_ref, gram_ref = refs
    plane = ids_ref[3]
    half = gram_ref.shape[1]
    total = None
    for a in (plane, 1 - plane):
        block = decoded(in_refs[0][a])
        for ref in in_refs[1:]:
            block = block + decoded(ref[a])
        if total is None:
            samples_ref[plane] = block
        else:
            other_ref[...] = block
        left, right = block[:, :half], block[:, half:]
        parts = [
            lax.dot_general(x, y, (((0,), (0,)), ((), ())), preferred_element_type=jnp.float32, precision=EXACT)
            for x, y in ((left, left), (left, right), (right, right))
        ]
        total = parts if total is None else [x + y for x, y in zip(total, parts)]
    for n, part in enumerate(total):
        gram_ref[n * half : (n + 1) * half, :] = part


def gram_of(ids, codes):
    _, rows, probes = codes[0].shape
    points = rows - EXTRA
    return pl.pallas_call(
        gram_kernel,
        in_specs=[pl.BlockSpec(memory_space=pltpu.SMEM)] + [pl.BlockSpec(memory_space=pltpu.VMEM)] * len(codes),
        out_shape=[
            jax.ShapeDtypeStruct((2, points, probes), jnp.float32),
            jax.ShapeDtypeStruct((points, probes), jnp.float32),
            jax.ShapeDtypeStruct((3 * probes // 2, probes // 2), jnp.float32),
        ],
        name="gram",
    )(ids, *codes)


def half_inverse(a_ref, out_ref, m_ref, tall_ref, u_ref, v_ref):
    n, size = a_ref.shape[0], u_ref.shape[0]
    rows = lax.broadcasted_iota(jnp.int32, (n, n), 0)
    cols = lax.broadcasted_iota(jnp.int32, (n, n), 1)
    m_ref[...] = (rows == cols).astype(jnp.float32)
    for ref in (tall_ref, u_ref, v_ref):
        ref[...] = jnp.zeros_like(ref)
    lane = lax.broadcasted_iota(jnp.int32, (size, n), 1)
    sub = lax.broadcasted_iota(jnp.int32, (size, n), 0)

    def spread(array, i):
        return jnp.broadcast_to(array[i : i + 1, :], (size, n))

    def group(b, carry):
        at = pl.multiple_of(b * size, size)
        u, v, near = u_ref[...], v_ref[...], tall_ref[pl.ds(at, size), :]
        panel, inverse = a_ref[pl.ds(at, size), :], m_ref[pl.ds(at, size), :]
        old_a, old_m, tall = a_ref[...], m_ref[...], tall_ref[...]
        for t in range(size):
            factor = jnp.broadcast_to(near[:, t : t + 1], (size, n))
            panel = panel - factor * u[t : t + 1, :]
            inverse = inverse - factor * v[t : t + 1, :]
        small = pltpu.roll(panel, n - at, axis=1)
        s = [[None] * size for _ in range(size)]
        e = [[None] * size for _ in range(size)]
        for t in range(size):
            column = jnp.broadcast_to(small[:, t : t + 1], (size, n))
            for i in range(t, size):
                s[i][t] = spread(column, i)
        for t in range(size - 1):
            ratio = 1.0 / s[t][t]
            for i in range(t + 1, size):
                factor = s[i][t] * ratio
                for j in range(t + 1, i + 1):
                    s[i][j] = s[i][j] - factor * s[j][t]
                for j in range(t):
                    e[i][j] = e[i][j] - factor * e[t][j]
                e[i][t] = -factor
        scale = s[0][0]
        for t in range(1, size):
            scale = jnp.where(sub == t, s[t][t], scale)
        scale = lax.rsqrt(scale)
        new_u, new_v = panel, inverse
        for t in range(size - 1):
            factor = jnp.zeros((size, n), jnp.float32)
            for i in range(t + 1, size):
                factor = jnp.where(sub == i, e[i][t], factor)
            new_u = new_u + factor * panel[t : t + 1, :]
            new_v = new_v + factor * inverse[t : t + 1, :]
        new_u = jnp.where(lane >= at + sub, new_u * scale, 0.0)
        new_v = new_v * scale
        for t in range(size):
            factor = jnp.broadcast_to(tall[:, t : t + 1], (n, n))
            old_a = old_a - factor * u[t : t + 1, :]
            old_m = old_m - factor * v[t : t + 1, :]
        a_ref[...], m_ref[...] = old_a, old_m
        out_ref[pl.ds(at, size), :] = new_v
        u_ref[...], v_ref[...] = new_u, new_v
        tall_ref[...] = new_u.T
        return carry

    lax.fori_loop(0, n // size, group, 0)


def factor_kernel(scale, ids_ref, samples_ref, other_ref, *refs):
    *gram_refs, basis_ref, out_ref, a_ref, m1_ref, m2_ref = refs[:9]
    work = refs[9:]
    half = a_ref.shape[0]
    plane = ids_ref[3]

    def product(a, b, over):
        return lax.dot_general(
            a, b, ((over[:1], over[1:]), ((), ())), preferred_element_type=jnp.float32, precision=EXACT
        )

    def gram(n):
        rows = slice(n * half, (n + 1) * half)
        one, two, three, four = (ref[rows, :] for ref in gram_refs)
        return ((one + two) + (three + four)) * scale

    a_ref[...] = gram(0)
    half_inverse(a_ref, m1_ref, *work)
    first = m1_ref[...]
    cross = product(first, gram(1), (1, 0))
    a_ref[...] = gram(2) - product(cross, cross, (0, 0))
    half_inverse(a_ref, m2_ref, *work)
    second = m2_ref[...]
    mixed = -product(second, product(cross, first, (0, 0)), (1, 0))
    for n, block in enumerate((samples_ref[plane], other_ref[...])):
        left, right = block[:, :half], block[:, half:]
        made = (product(left, first, (1, 1)), product(left, mixed, (1, 1)) + product(right, second, (1, 1)))
        for m, value in enumerate(made):
            columns = slice(m * half, (m + 1) * half)
            if n:
                out_ref[:, columns] = value
            else:
                basis_ref[plane, :, columns] = value


def orthogonal(ids, samples, other, grams, scale):
    half = grams[0].shape[1]
    return pl.pallas_call(
        functools.partial(factor_kernel, scale),
        in_specs=[pl.BlockSpec(memory_space=pltpu.SMEM)] + [pl.BlockSpec(memory_space=pltpu.VMEM)] * (2 + len(grams)),
        out_shape=[jax.ShapeDtypeStruct(x.shape, jnp.float32) for x in (samples, other)],
        scratch_shapes=[
            pltpu.VMEM(shape, jnp.float32) for shape in [(half, half)] * 4 + [(half, 8), (8, half), (8, half)]
        ],
        name="orthogonal",
    )(ids, samples, other, *grams)


def whole_step(tiles, probe, cluster_perm, tile_keep):
    row_id = lax.axis_index("row")
    col_id = lax.axis_index("col")
    nrows = lax.axis_size("row")
    ncols = lax.axis_size("col")
    tile_len = tiles.shape[1]
    nz = ncols // 2
    plane, depth = col_id // nz, col_id % nz
    wraps = (row_id + col_id >= nrows).astype(jnp.int32)
    ids = jnp.stack([col_id, depth, wraps, plane]).astype(jnp.int32)
    weight = jnp.where(col_id == 0, 0.5, tile_keep[:, 0, 0].astype(jnp.float32))

    def same(d):
        return lambda r, c: (r, c ^ d)

    def slanted(d):
        return lambda r, c: (r + c - (c ^ d), c ^ d)

    def far(r, c):
        return (r - c, c)

    depths = range(1, nz)
    other = sent(probe[0], same(nz))
    singles = [sent(probe[1], same(d)) for d in depths]
    pair = jnp.stack([probe[0], other])
    line = jnp.stack([probe[1], *singles])
    pairs = [sent(pair, same(d)) for d in depths]
    cross = sent(line, same(nz))

    far_pair = sent(pair, far)
    far_line = sent(line, far)
    far_perm = sent(cluster_perm, far)
    far_pairs = [sent(far_pair, slanted(d)) for d in depths]
    far_cross = sent(cross, far)

    perm, far_perm = (x.reshape(-1, 1, tile_len) for x in (cluster_perm, far_perm))
    own_blocks = ([pair, *pairs], line, cross)
    far_blocks = ([far_pair, *far_pairs], far_line, far_cross)

    def home(r, c):
        return (r + c, c)

    (more,) = products(ids, weight, perm, *own_blocks, tiles, True, 1)
    more = sent(more, home)
    back = products(ids, weight, perm, *own_blocks, tiles, True, 0)
    back, far_pairs = lax.optimization_barrier((back, far_pairs))
    back = [back[0]] + [sent(back[d], slanted(d)) for d in depths]
    kept = products(ids, weight, far_perm, *far_blocks, tiles, False, 0)
    kept = [kept[0]] + [sent(kept[d], same(d)) for d in depths]
    given = products(ids, weight, far_perm, *far_blocks, tiles, False, 1)
    arrived = sent(summed(back, given[0]), home)
    given = [sent(code, same(nz + d)) for d, code in enumerate(joined(given, more))]
    samples, swapped, gram = gram_of(ids, [*kept, *given, arrived])
    grams = [gram] + [sent(gram, same(d)) for d in depths]
    basis, swapped_basis = orthogonal(ids, samples, swapped, grams, 1.0 / tile_len)

    def placed(array, theirs):
        return lax.dynamic_update_index_in_dim(array, sent(theirs, same(nz)), 1 - plane, 0)

    return (placed(samples, swapped), placed(basis, swapped_basis))


def solution(mesh):
    whole = P(None, ("row", "col"), None)
    return jax.shard_map(
        whole_step,
        mesh=mesh,
        in_specs=(P(None, "row", "col"), whole, P(None, "row", None), P(None, "row", "col")),
        out_specs=(whole, whole),
        check_vma=False,
    )
```

```python
import functools

import jax
import jax.numpy as jnp
from jax import lax
from jax.experimental import pallas as pl
from jax.experimental.pallas import tpu as pltpu
from jax.sharding import PartitionSpec as P


AXES = ("row", "col")
EXACT = lax.Precision.HIGHEST
LEVELS = 32767.0
EXTRA = 16


def sent(value, to):
    nrows, ncols = lax.axis_size("row"), lax.axis_size("col")
    pairs = []
    for r in range(nrows):
        for c in range(ncols):
            r_to, c_to = to(r, c)
            pairs.append((r * ncols + c, (r_to % nrows) * ncols + c_to))
    return lax.ppermute(value, AXES, pairs)


def scale_of(exponent, mantissa):
    return jnp.exp2(exponent) * (mantissa * (1.0 / (LEVELS * LEVELS)))


def coded(block):
    largest = jnp.maximum(jnp.max(jnp.abs(block), axis=0, keepdims=True), 1e-30)
    exponent = jnp.floor(jnp.log2(largest * 1.0001)) + 1.0
    mantissa = jnp.ceil(largest * jnp.exp2(-exponent) * LEVELS)
    scale = scale_of(exponent, mantissa)
    values = jnp.clip(jnp.round(block * (1.0 / scale)), -LEVELS, LEVELS)
    at = lax.broadcasted_iota(jnp.int32, (EXTRA, block.shape[1]), 0)
    tail = jnp.where(at == 0, exponent, mantissa)
    return jnp.concatenate([values, tail], axis=0).astype(jnp.int32).astype(jnp.int16)


def decoded(code):
    wide = code.astype(jnp.int32).astype(jnp.float32)
    rows = code.shape[0] - EXTRA
    return wide[:rows] * scale_of(wide[rows : rows + 1], wide[rows + 1 : rows + 2])


def product_kernel(back, part, ids_ref, weight_ref, perm_ref, *refs):
    *pair_refs, plane_ref, cross_ref, tiles_ref = refs[:7]
    joins = not back and part == 0
    more_ref = refs[7] if joins else None
    *out_refs, tile_ref, raw_ref, omega_ref, sems = refs[8 if joins else 7 :]
    nz, points, _ = plane_ref.shape
    length = raw_ref.shape[1]
    step = 512
    k = ids_ref[3] ^ ids_ref[2] ^ part
    tile_slot = k if back else k ^ ids_ref[2]

    def piece_copy(q):
        rows = pl.ds(q * step, step)
        return pltpu.make_async_copy(tiles_ref.at[tile_slot, rows], tile_ref.at[rows], sems.at[q])

    for q in range(length // step):
        piece_copy(q).start()
    for slot in range(2):

        @pl.when(k == slot)
        def _(slot=slot):
            for d in range(nz):
                for a in range(2):
                    piece = (cross_ref[d] if a else plane_ref[d]) if slot else pair_refs[d][a]
                    at = (nz * a + d) * points
                    raw_ref[:, at : at + points] = piece.T

    def order_step(i, carry):
        at = pl.multiple_of(i * step, step)
        index = perm_ref[k, :, pl.ds(at, step)] ^ (ids_ref[0] * points)
        place = lax.broadcasted_iota(jnp.int32, (length, step), 0)
        chosen = jnp.where(place == index, 1.0, 0.0).astype(jnp.bfloat16)
        found = jnp.dot(raw_ref[...], chosen, preferred_element_type=jnp.float32)
        if back:
            omega_ref[:, pl.ds(at, step)] = found.astype(jnp.bfloat16)
        else:
            omega_ref[pl.ds(at, step), :] = found.T.astype(jnp.bfloat16)
        return carry

    lax.fori_loop(0, length // step, order_step, 0)
    for q in range(length // step):
        piece_copy(q).wait()
    weight = weight_ref[tile_slot]
    for d in range(nz):
        for a in range(2):
            at = pl.multiple_of((a * nz + (ids_ref[1] ^ d)) * points, points)
            if back:
                value = jnp.dot(omega_ref[...], tile_ref[:, pl.ds(at, points)], preferred_element_type=jnp.float32).T
            else:
                value = jnp.dot(tile_ref[pl.ds(at, points), :], omega_ref[...], preferred_element_type=jnp.float32)
            value = value * weight
            if joins:
                value = value + decoded(more_ref[d, a])
            code = coded(value)
            if len(out_refs) == 1:
                out_refs[0][d, a] = code
            else:
                out_refs[d][a] = code


def products(ids, weight, perm, pairs, plane, cross, tiles, back, part, more=()):
    nz, points, probes = plane.shape
    length = tiles.shape[1]
    block = (2, points + EXTRA, probes)
    shapes = [(nz, *block)] if back and part == 0 else [block] * nz
    smem, vmem = pl.BlockSpec(memory_space=pltpu.SMEM), pl.BlockSpec(memory_space=pltpu.VMEM)
    return pl.pallas_call(
        functools.partial(product_kernel, back, part),
        out_shape=[jax.ShapeDtypeStruct(shape, jnp.int16) for shape in shapes],
        in_specs=[smem, smem] + [vmem] * (3 + nz) + [pl.BlockSpec(memory_space=pl.ANY)] + [vmem] * len(more),
        out_specs=[vmem] * len(shapes),
        scratch_shapes=[
            pltpu.VMEM(tiles.shape[1:], jnp.bfloat16),
            pltpu.VMEM((probes, length), jnp.bfloat16),
            pltpu.VMEM((probes, length) if back else (length, probes), jnp.bfloat16),
            pltpu.SemaphoreType.DMA((length // 512,)),
        ],
        compiler_params=pltpu.CompilerParams(vmem_limit_bytes=56 << 20),
        cost_estimate=pl.CostEstimate(flops=4 * length * length * probes, bytes_accessed=11 << 20, transcendentals=0),
    )(ids, weight, perm, *pairs, plane, cross, tiles, *more)


def sum_kernel(*refs):
    *in_refs, out_ref = refs
    for a in range(2):
        total = decoded(in_refs[0][a])
        for ref in in_refs[1:]:
            total = total + decoded(ref[a])
        out_ref[a] = coded(total)


def summed(codes):
    return pl.pallas_call(sum_kernel, out_shape=jax.ShapeDtypeStruct(codes[0].shape, jnp.int16), name="sum_back")(*codes)


def gram_kernel(ids_ref, *refs):
    *in_refs, samples_ref, other_ref, gram_ref = refs
    plane = ids_ref[3]
    half = gram_ref.shape[1]
    total = None
    for a in (plane, 1 - plane):
        block = decoded(in_refs[0][a])
        for ref in in_refs[1:]:
            block = block + decoded(ref[a])
        if total is None:
            samples_ref[plane] = block
        else:
            other_ref[...] = block
        left, right = block[:, :half], block[:, half:]
        parts = [
            lax.dot_general(x, y, (((0,), (0,)), ((), ())), preferred_element_type=jnp.float32, precision=EXACT)
            for x, y in ((left, left), (left, right), (right, right))
        ]
        total = parts if total is None else [x + y for x, y in zip(total, parts)]
    for n, part in enumerate(total):
        gram_ref[n * half : (n + 1) * half, :] = part


def gram_of(ids, codes):
    _, rows, probes = codes[0].shape
    points = rows - EXTRA
    return pl.pallas_call(
        gram_kernel,
        in_specs=[pl.BlockSpec(memory_space=pltpu.SMEM)] + [pl.BlockSpec(memory_space=pltpu.VMEM)] * len(codes),
        out_shape=[
            jax.ShapeDtypeStruct((2, points, probes), jnp.float32),
            jax.ShapeDtypeStruct((points, probes), jnp.float32),
            jax.ShapeDtypeStruct((3 * probes // 2, probes // 2), jnp.float32),
        ],
        name="gram",
    )(ids, *codes)


def half_inverse(a_ref, out_ref, m_ref, tall_ref, u_ref, v_ref):
    n, size = a_ref.shape[0], u_ref.shape[0]
    rows = lax.broadcasted_iota(jnp.int32, (n, n), 0)
    cols = lax.broadcasted_iota(jnp.int32, (n, n), 1)
    m_ref[...] = (rows == cols).astype(jnp.float32)
    for ref in (tall_ref, u_ref, v_ref):
        ref[...] = jnp.zeros_like(ref)
    lane = lax.broadcasted_iota(jnp.int32, (size, n), 1)
    sub = lax.broadcasted_iota(jnp.int32, (size, n), 0)

    def spread(array, i):
        return jnp.broadcast_to(array[i : i + 1, :], (size, n))

    def group(b, carry):
        at = pl.multiple_of(b * size, size)
        u, v, near = u_ref[...], v_ref[...], tall_ref[pl.ds(at, size), :]
        panel, inverse = a_ref[pl.ds(at, size), :], m_ref[pl.ds(at, size), :]
        old_a, old_m, tall = a_ref[...], m_ref[...], tall_ref[...]
        for t in range(size):
            factor = jnp.broadcast_to(near[:, t : t + 1], (size, n))
            panel = panel - factor * u[t : t + 1, :]
            inverse = inverse - factor * v[t : t + 1, :]
        small = pltpu.roll(panel, n - at, axis=1)
        s = [[None] * size for _ in range(size)]
        e = [[None] * size for _ in range(size)]
        for t in range(size):
            column = jnp.broadcast_to(small[:, t : t + 1], (size, n))
            for i in range(t, size):
                s[i][t] = spread(column, i)
        for t in range(size - 1):
            ratio = 1.0 / s[t][t]
            for i in range(t + 1, size):
                factor = s[i][t] * ratio
                for j in range(t + 1, i + 1):
                    s[i][j] = s[i][j] - factor * s[j][t]
                for j in range(t):
                    e[i][j] = e[i][j] - factor * e[t][j]
                e[i][t] = -factor
        scale = s[0][0]
        for t in range(1, size):
            scale = jnp.where(sub == t, s[t][t], scale)
        scale = lax.rsqrt(scale)
        new_u, new_v = panel, inverse
        for t in range(size - 1):
            factor = jnp.zeros((size, n), jnp.float32)
            for i in range(t + 1, size):
                factor = jnp.where(sub == i, e[i][t], factor)
            new_u = new_u + factor * panel[t : t + 1, :]
            new_v = new_v + factor * inverse[t : t + 1, :]
        new_u = jnp.where(lane >= at + sub, new_u * scale, 0.0)
        new_v = new_v * scale
        for t in range(size):
            factor = jnp.broadcast_to(tall[:, t : t + 1], (n, n))
            old_a = old_a - factor * u[t : t + 1, :]
            old_m = old_m - factor * v[t : t + 1, :]
        a_ref[...], m_ref[...] = old_a, old_m
        out_ref[pl.ds(at, size), :] = new_v
        u_ref[...], v_ref[...] = new_u, new_v
        tall_ref[...] = new_u.T
        return carry

    lax.fori_loop(0, n // size, group, 0)


def factor_kernel(scale, ids_ref, samples_ref, other_ref, *refs):
    *gram_refs, basis_ref, out_ref, a_ref, m1_ref, m2_ref = refs[:9]
    work = refs[9:]
    half = a_ref.shape[0]
    plane = ids_ref[3]

    def product(a, b, over):
        return lax.dot_general(
            a, b, ((over[:1], over[1:]), ((), ())), preferred_element_type=jnp.float32, precision=EXACT
        )

    def gram(n):
        rows = slice(n * half, (n + 1) * half)
        one, two, three, four = (ref[rows, :] for ref in gram_refs)
        return ((one + two) + (three + four)) * scale

    a_ref[...] = gram(0)
    half_inverse(a_ref, m1_ref, *work)
    first = m1_ref[...]
    cross = product(first, gram(1), (1, 0))
    a_ref[...] = gram(2) - product(cross, cross, (0, 0))
    half_inverse(a_ref, m2_ref, *work)
    second = m2_ref[...]
    mixed = -product(second, product(cross, first, (0, 0)), (1, 0))
    for n, block in enumerate((samples_ref[plane], other_ref[...])):
        left, right = block[:, :half], block[:, half:]
        made = (product(left, first, (1, 1)), product(left, mixed, (1, 1)) + product(right, second, (1, 1)))
        for m, value in enumerate(made):
            columns = slice(m * half, (m + 1) * half)
            if n:
                out_ref[:, columns] = value
            else:
                basis_ref[plane, :, columns] = value


def orthogonal(ids, samples, other, grams, scale):
    half = grams[0].shape[1]
    return pl.pallas_call(
        functools.partial(factor_kernel, scale),
        in_specs=[pl.BlockSpec(memory_space=pltpu.SMEM)] + [pl.BlockSpec(memory_space=pltpu.VMEM)] * (2 + len(grams)),
        out_shape=[jax.ShapeDtypeStruct(x.shape, jnp.float32) for x in (samples, other)],
        scratch_shapes=[
            pltpu.VMEM(shape, jnp.float32) for shape in [(half, half)] * 4 + [(half, 8), (8, half), (8, half)]
        ],
        name="orthogonal",
    )(ids, samples, other, *grams)


def whole_step(tiles, probe, cluster_perm, tile_keep):
    row_id = lax.axis_index("row")
    col_id = lax.axis_index("col")
    nrows = lax.axis_size("row")
    ncols = lax.axis_size("col")
    tile_len = tiles.shape[1]
    nz = ncols // 2
    plane, depth = col_id // nz, col_id % nz
    wraps = (row_id + col_id >= nrows).astype(jnp.int32)
    ids = jnp.stack([col_id, depth, wraps, plane]).astype(jnp.int32)
    weight = jnp.where(col_id == 0, 0.5, tile_keep[:, 0, 0].astype(jnp.float32))

    def same(d):
        return lambda r, c: (r, c ^ d)

    def slanted(d):
        return lambda r, c: (r + c - (c ^ d), c ^ d)

    def far(r, c):
        return (r - c, c)

    depths = range(1, nz)
    other = sent(probe[0], same(nz))
    singles = [sent(probe[1], same(d)) for d in depths]
    pair = jnp.stack([probe[0], other])
    line = jnp.stack([probe[1], *singles])
    pairs = [sent(pair, same(d)) for d in depths]
    cross = sent(line, same(nz))

    far_pair = sent(pair, far)
    far_line = sent(line, far)
    far_perm = sent(cluster_perm, far)
    far_pairs = [sent(far_pair, slanted(d)) for d in depths]
    far_cross = sent(cross, far)

    perm, far_perm = (x.reshape(-1, 1, tile_len) for x in (cluster_perm, far_perm))
    own_blocks = ([pair, *pairs], line, cross)
    far_blocks = ([far_pair, *far_pairs], far_line, far_cross)

    (more,) = products(ids, weight, perm, *own_blocks, tiles, True, 0)
    more = sent(more, lambda r, c: (r + c, c))
    back = products(ids, weight, perm, *own_blocks, tiles, True, 1)
    back, far_pairs = lax.optimization_barrier((back, far_pairs))
    back = [back[0]] + [sent(back[d], slanted(d)) for d in depths]
    given = products(ids, weight, far_perm, *far_blocks, tiles, False, 1)
    given = [sent(code, same(nz + d)) for d, code in enumerate(given)]
    kept = products(ids, weight, far_perm, *far_blocks, tiles, False, 0, (more,))
    kept = [kept[0]] + [sent(kept[d], same(d)) for d in depths]
    arrived = summed(back)
    arrived = sent(arrived, lambda r, c: (r + c, c ^ nz))
    samples, swapped, gram = gram_of(ids, [*kept, *given, arrived])
    grams = [gram] + [sent(gram, same(d)) for d in depths]
    basis, swapped_basis = orthogonal(ids, samples, swapped, grams, 1.0 / tile_len)

    def placed(array, theirs):
        return lax.dynamic_update_index_in_dim(array, sent(theirs, same(nz)), 1 - plane, 0)

    return (placed(samples, swapped), placed(basis, swapped_basis))


def solution(mesh):
    whole = P(None, ("row", "col"), None)
    return jax.shard_map(
        whole_step,
        mesh=mesh,
        in_specs=(P(None, "row", "col"), whole, P(None, "row", None), P(None, "row", "col")),
        out_specs=(whole, whole),
        check_vma=False,
    )
```

```python
import functools

import jax
import jax.numpy as jnp
from jax import lax
from jax.experimental import pallas as pl
from jax.experimental.pallas import tpu as pltpu
from jax.sharding import PartitionSpec as P


AXES = ("row", "col")
EXACT = lax.Precision.HIGHEST
LEVELS = 32767.0
EXTRA = 16


def sent(value, to):
    nrows, ncols = lax.axis_size("row"), lax.axis_size("col")
    pairs = []
    for r in range(nrows):
        for c in range(ncols):
            r_to, c_to = to(r, c)
            pairs.append((r * ncols + c, (r_to % nrows) * ncols + c_to))
    return lax.ppermute(value, AXES, pairs)


def scale_of(exponent, mantissa):
    return jnp.exp2(exponent) * (mantissa * (1.0 / (LEVELS * LEVELS)))


def coded(block):
    largest = jnp.maximum(jnp.max(jnp.abs(block), axis=0, keepdims=True), 1e-30)
    exponent = jnp.floor(jnp.log2(largest * 1.0001)) + 1.0
    mantissa = jnp.ceil(largest * jnp.exp2(-exponent) * LEVELS)
    scale = scale_of(exponent, mantissa)
    values = jnp.clip(jnp.round(block * (1.0 / scale)), -LEVELS, LEVELS)
    at = lax.broadcasted_iota(jnp.int32, (EXTRA, block.shape[1]), 0)
    tail = jnp.where(at == 0, exponent, mantissa)
    return jnp.concatenate([values, tail], axis=0).astype(jnp.int32).astype(jnp.int16)


def decoded(code):
    wide = code.astype(jnp.int32).astype(jnp.float32)
    rows = code.shape[0] - EXTRA
    return wide[:rows] * scale_of(wide[rows : rows + 1], wide[rows + 1 : rows + 2])


def product_kernel(back, part, ids_ref, weight_ref, perm_ref, tiles_ref, *refs):
    *in_refs, tile_ref, raw_ref, omega_ref, sems = refs
    nz = sems.shape[0] // 2
    length = raw_ref.shape[1]
    points = length // (2 * nz)
    step = 512
    k = ids_ref[3] ^ ids_ref[2] ^ part
    tile_slot = k if back else k ^ ids_ref[2]
    blocks = [(d, a) for d in range(nz) for a in range(2)]

    def place(d, a):
        at = pl.ds(pl.multiple_of((a * nz + (ids_ref[1] ^ d)) * points, points), points)
        return (slice(None), at) if back else (at, slice(None))

    def block_copy(n):
        at = place(*blocks[n])
        return pltpu.make_async_copy(tiles_ref.at[(tile_slot, *at)], tile_ref.at[at], sems.at[n])

    for n in range(len(blocks)):
        block_copy(n).start()
    if back:
        out_refs = in_refs[2 * nz :]
        for o in range(2 * nz):
            raw_ref[:, o * points : (o + 1) * points] = in_refs[o][k].T
    else:
        out_refs = in_refs[nz + 2 - part :]

        @pl.when(k == 0)
        def _():
            for d, a in blocks:
                o = nz * a + d
                raw_ref[:, o * points : (o + 1) * points] = in_refs[d][a].T

        @pl.when(k == 1)
        def _():
            for o in range(2 * nz):
                raw_ref[:, o * points : (o + 1) * points] = in_refs[nz][o].T

    def order_step(i, carry):
        at = pl.multiple_of(i * step, step)
        index = perm_ref[k, :, pl.ds(at, step)] ^ (ids_ref[0] * points)
        places = lax.broadcasted_iota(jnp.int32, (length, step), 0)
        chosen = jnp.where(places == index, 1.0, 0.0).astype(jnp.bfloat16)
        found = jnp.dot(raw_ref[...], chosen, preferred_element_type=jnp.float32)
        if back:
            omega_ref[:, pl.ds(at, step)] = found.astype(jnp.bfloat16)
        else:
            omega_ref[pl.ds(at, step), :] = found.T.astype(jnp.bfloat16)
        return carry

    lax.fori_loop(0, length // step, order_step, 0)
    weight = weight_ref[tile_slot]
    for n, (d, a) in enumerate(blocks):
        block_copy(n).wait()
        tile = tile_ref[place(d, a)]
        if back:
            value = jnp.dot(omega_ref[...], tile, preferred_element_type=jnp.float32).T
        else:
            value = jnp.dot(tile, omega_ref[...], preferred_element_type=jnp.float32)
        value = value * weight
        if not back and part == 0:
            value = value + decoded(in_refs[nz + 1][d, a])
        code = coded(value)
        if len(out_refs) == 1:
            out_refs[0][d, a] = code
        else:
            out_refs[d][a] = code


def products(ids, weight, perm, tiles, blocks, back, part):
    points, probes = blocks[0].shape[1:]
    length = tiles.shape[1]
    nz = length // points // 2
    block = (2, points + EXTRA, probes)
    shapes = [(nz, *block)] if back and part == 0 else [block] * nz
    smem, vmem = pl.BlockSpec(memory_space=pltpu.SMEM), pl.BlockSpec(memory_space=pltpu.VMEM)
    return pl.pallas_call(
        functools.partial(product_kernel, back, part),
        out_shape=[jax.ShapeDtypeStruct(shape, jnp.int16) for shape in shapes],
        in_specs=[smem, smem, vmem, pl.BlockSpec(memory_space=pl.ANY)] + [vmem] * len(blocks),
        out_specs=[vmem] * len(shapes),
        scratch_shapes=[
            pltpu.VMEM(tiles.shape[1:], jnp.bfloat16),
            pltpu.VMEM((probes, length), jnp.bfloat16),
            pltpu.VMEM((probes, length) if back else (length, probes), jnp.bfloat16),
            pltpu.SemaphoreType.DMA((2 * nz,)),
        ],
        compiler_params=pltpu.CompilerParams(vmem_limit_bytes=56 << 20),
        cost_estimate=pl.CostEstimate(flops=4 * length * length * probes, bytes_accessed=11 << 20, transcendentals=0),
    )(ids, weight, perm, tiles, *blocks)


def sum_kernel(*refs):
    *in_refs, out_ref = refs
    for a in range(2):
        total = decoded(in_refs[0][a])
        for ref in in_refs[1:]:
            total = total + decoded(ref[a])
        out_ref[a] = coded(total)


def summed(codes):
    return pl.pallas_call(sum_kernel, out_shape=jax.ShapeDtypeStruct(codes[0].shape, jnp.int16), name="sum_back")(*codes)


def gram_kernel(ids_ref, *refs):
    *in_refs, samples_ref, other_ref, gram_ref = refs
    plane = ids_ref[3]
    half = gram_ref.shape[1]
    total = None
    for a in (plane, 1 - plane):
        block = decoded(in_refs[0][a])
        for ref in in_refs[1:]:
            block = block + decoded(ref[a])
        if total is None:
            samples_ref[plane] = block
        else:
            other_ref[...] = block
        left, right = block[:, :half], block[:, half:]
        parts = [
            lax.dot_general(x, y, (((0,), (0,)), ((), ())), preferred_element_type=jnp.float32, precision=EXACT)
            for x, y in ((left, left), (left, right), (right, right))
        ]
        total = parts if total is None else [x + y for x, y in zip(total, parts)]
    for n, part in enumerate(total):
        gram_ref[n * half : (n + 1) * half, :] = part


def gram_of(ids, codes):
    _, rows, probes = codes[0].shape
    points = rows - EXTRA
    return pl.pallas_call(
        gram_kernel,
        in_specs=[pl.BlockSpec(memory_space=pltpu.SMEM)] + [pl.BlockSpec(memory_space=pltpu.VMEM)] * len(codes),
        out_shape=[
            jax.ShapeDtypeStruct((2, points, probes), jnp.float32),
            jax.ShapeDtypeStruct((points, probes), jnp.float32),
            jax.ShapeDtypeStruct((3 * probes // 2, probes // 2), jnp.float32),
        ],
        name="gram",
    )(ids, *codes)


def half_inverse(a_ref, out_ref, m_ref, tall_ref, u_ref, v_ref):
    n, size = a_ref.shape[0], u_ref.shape[0]
    rows = lax.broadcasted_iota(jnp.int32, (n, n), 0)
    cols = lax.broadcasted_iota(jnp.int32, (n, n), 1)
    m_ref[...] = (rows == cols).astype(jnp.float32)
    for ref in (tall_ref, u_ref, v_ref):
        ref[...] = jnp.zeros_like(ref)
    lane = lax.broadcasted_iota(jnp.int32, (size, n), 1)
    sub = lax.broadcasted_iota(jnp.int32, (size, n), 0)

    def spread(array, i):
        return jnp.broadcast_to(array[i : i + 1, :], (size, n))

    def group(b, carry):
        at = pl.multiple_of(b * size, size)
        u, v, near = u_ref[...], v_ref[...], tall_ref[pl.ds(at, size), :]
        panel, inverse = a_ref[pl.ds(at, size), :], m_ref[pl.ds(at, size), :]
        old_a, old_m, tall = a_ref[...], m_ref[...], tall_ref[...]
        for t in range(size):
            factor = jnp.broadcast_to(near[:, t : t + 1], (size, n))
            panel = panel - factor * u[t : t + 1, :]
            inverse = inverse - factor * v[t : t + 1, :]
        small = pltpu.roll(panel, n - at, axis=1)
        s = [[None] * size for _ in range(size)]
        e = [[None] * size for _ in range(size)]
        for t in range(size):
            column = jnp.broadcast_to(small[:, t : t + 1], (size, n))
            for i in range(t, size):
                s[i][t] = spread(column, i)
        for t in range(size - 1):
            ratio = 1.0 / s[t][t]
            for i in range(t + 1, size):
                factor = s[i][t] * ratio
                for j in range(t + 1, i + 1):
                    s[i][j] = s[i][j] - factor * s[j][t]
                for j in range(t):
                    e[i][j] = e[i][j] - factor * e[t][j]
                e[i][t] = -factor
        scale = s[0][0]
        for t in range(1, size):
            scale = jnp.where(sub == t, s[t][t], scale)
        scale = lax.rsqrt(scale)
        new_u, new_v = panel, inverse
        for t in range(size - 1):
            factor = jnp.zeros((size, n), jnp.float32)
            for i in range(t + 1, size):
                factor = jnp.where(sub == i, e[i][t], factor)
            new_u = new_u + factor * panel[t : t + 1, :]
            new_v = new_v + factor * inverse[t : t + 1, :]
        new_u = jnp.where(lane >= at + sub, new_u * scale, 0.0)
        new_v = new_v * scale
        for t in range(size):
            factor = jnp.broadcast_to(tall[:, t : t + 1], (n, n))
            old_a = old_a - factor * u[t : t + 1, :]
            old_m = old_m - factor * v[t : t + 1, :]
        a_ref[...], m_ref[...] = old_a, old_m
        out_ref[pl.ds(at, size), :] = new_v
        u_ref[...], v_ref[...] = new_u, new_v
        tall_ref[...] = new_u.T
        return carry

    lax.fori_loop(0, n // size, group, 0)


def factor_kernel(scale, ids_ref, samples_ref, other_ref, *refs):
    *gram_refs, basis_ref, out_ref, a_ref, m1_ref, m2_ref = refs[:9]
    work = refs[9:]
    half = a_ref.shape[0]
    plane = ids_ref[3]

    def product(a, b, over):
        return lax.dot_general(
            a, b, ((over[:1], over[1:]), ((), ())), preferred_element_type=jnp.float32, precision=EXACT
        )

    def gram(n):
        rows = slice(n * half, (n + 1) * half)
        one, two, three, four = (ref[rows, :] for ref in gram_refs)
        return ((one + two) + (three + four)) * scale

    a_ref[...] = gram(0)
    half_inverse(a_ref, m1_ref, *work)
    first = m1_ref[...]
    cross = product(first, gram(1), (1, 0))
    a_ref[...] = gram(2) - product(cross, cross, (0, 0))
    half_inverse(a_ref, m2_ref, *work)
    second = m2_ref[...]
    mixed = -product(second, product(cross, first, (0, 0)), (1, 0))
    for n, block in enumerate((samples_ref[plane], other_ref[...])):
        left, right = block[:, :half], block[:, half:]
        made = (product(left, first, (1, 1)), product(left, mixed, (1, 1)) + product(right, second, (1, 1)))
        for m, value in enumerate(made):
            columns = slice(m * half, (m + 1) * half)
            if n:
                out_ref[:, columns] = value
            else:
                basis_ref[plane, :, columns] = value


def orthogonal(ids, samples, other, grams, scale):
    half = grams[0].shape[1]
    return pl.pallas_call(
        functools.partial(factor_kernel, scale),
        in_specs=[pl.BlockSpec(memory_space=pltpu.SMEM)] + [pl.BlockSpec(memory_space=pltpu.VMEM)] * (2 + len(grams)),
        out_shape=[jax.ShapeDtypeStruct(x.shape, jnp.float32) for x in (samples, other)],
        scratch_shapes=[
            pltpu.VMEM(shape, jnp.float32) for shape in [(half, half)] * 4 + [(half, 8), (8, half), (8, half)]
        ],
        name="orthogonal",
    )(ids, samples, other, *grams)


def whole_step(tiles, probe, cluster_perm, tile_keep):
    row_id = lax.axis_index("row")
    col_id = lax.axis_index("col")
    nrows = lax.axis_size("row")
    ncols = lax.axis_size("col")
    tile_len = tiles.shape[1]
    nz = ncols // 2
    plane, depth = col_id // nz, col_id % nz
    wraps = (row_id + col_id >= nrows).astype(jnp.int32)
    ids = jnp.stack([col_id, depth, wraps, plane]).astype(jnp.int32)
    weight = jnp.where(col_id == 0, 0.5, tile_keep[:, 0, 0].astype(jnp.float32))

    def same(d):
        return lambda r, c: (r, c ^ d)

    def slanted(d):
        return lambda r, c: (r + c - (c ^ d), c ^ d)

    def far(r, c):
        return (r - c, c)

    depths = range(1, nz)
    blocks = {nz: sent(probe, same(nz))}
    for o in (*depths, *range(nz + 1, ncols)):
        blocks[o] = sent(probe, same(o))
    blocks = [probe] + [blocks[o] for o in range(1, ncols)]

    far_perm = sent(cluster_perm, far)
    pair = jnp.stack([blocks[0][0], blocks[nz][0]])
    far_pair = sent(pair, far)
    far_whole = sent(jnp.stack([block[1] for block in blocks]), far)
    far_pairs = [sent(far_pair, slanted(d)) for d in depths]

    perm, far_perm = (x.reshape(-1, 1, tile_len) for x in (cluster_perm, far_perm))
    far_blocks = [far_pair, *far_pairs, far_whole]
    (more,) = products(ids, weight, perm, tiles, blocks, True, 0)
    back = products(ids, weight, perm, tiles, blocks, True, 1)
    more = sent(more, lambda r, c: (r + c, c))
    back = [back[0]] + [sent(back[d], slanted(d)) for d in depths]
    given = products(ids, weight, far_perm, tiles, far_blocks, False, 1)
    given = [sent(code, same(nz + d)) for d, code in enumerate(given)]
    kept = products(ids, weight, far_perm, tiles, [*far_blocks, more], False, 0)
    kept = [kept[0]] + [sent(kept[d], same(d)) for d in depths]
    arrived = summed(back)
    arrived = sent(arrived, lambda r, c: (r + c, c ^ nz))
    samples, swapped, gram = gram_of(ids, [*kept, *given, arrived])
    grams = [gram] + [sent(gram, same(d)) for d in depths]
    basis, swapped_basis = orthogonal(ids, samples, swapped, grams, 1.0 / tile_len)

    def placed(array, theirs):
        return lax.dynamic_update_index_in_dim(array, sent(theirs, same(nz)), 1 - plane, 0)

    return (placed(samples, swapped), placed(basis, swapped_basis))


def solution(mesh):
    whole = P(None, ("row", "col"), None)
    return jax.shard_map(
        whole_step,
        mesh=mesh,
        in_specs=(P(None, "row", "col"), whole, P(None, "row", None), P(None, "row", "col")),
        out_specs=(whole, whole),
        check_vma=False,
    )
```

```python
import functools

import jax
import jax.numpy as jnp
from jax import lax
from jax.experimental import pallas as pl
from jax.experimental.pallas import tpu as pltpu
from jax.sharding import PartitionSpec as P


AXES = ("row", "col")
EXACT = lax.Precision.HIGHEST
LEVELS = 32767.0
EXTRA = 16


def sent(value, to):
    nrows, ncols = lax.axis_size("row"), lax.axis_size("col")
    pairs = []
    for r in range(nrows):
        for c in range(ncols):
            r_to, c_to = to(r, c)
            pairs.append((r * ncols + c, (r_to % nrows) * ncols + c_to))
    return lax.ppermute(value, AXES, pairs)


def scale_of(exponent, mantissa):
    return jnp.exp2(exponent) * (mantissa * (1.0 / (LEVELS * LEVELS)))


def coded(block):
    largest = jnp.maximum(jnp.max(jnp.abs(block), axis=0, keepdims=True), 1e-30)
    exponent = jnp.floor(jnp.log2(largest * 1.0001)) + 1.0
    mantissa = jnp.ceil(largest * jnp.exp2(-exponent) * LEVELS)
    scale = scale_of(exponent, mantissa)
    values = jnp.clip(jnp.round(block * (1.0 / scale)), -LEVELS, LEVELS)
    at = lax.broadcasted_iota(jnp.int32, (EXTRA, block.shape[1]), 0)
    tail = jnp.where(at == 0, exponent, mantissa)
    return jnp.concatenate([values, tail], axis=0).astype(jnp.int32).astype(jnp.int16)


def decoded(code):
    wide = code.astype(jnp.int32).astype(jnp.float32)
    rows = code.shape[0] - EXTRA
    return wide[:rows] * scale_of(wide[rows : rows + 1], wide[rows + 1 : rows + 2])


def product_kernel(back, part, ids_ref, weight_ref, perm_ref, *refs):
    *pair_refs, plane_ref, cross_ref, tiles_ref = refs[:7]
    joins = not back and part == 0
    more_ref = refs[7] if joins else None
    *out_refs, tile_ref, raw_ref, omega_ref, sems = refs[8 if joins else 7 :]
    nz, points, _ = plane_ref.shape
    length = raw_ref.shape[1]
    step = 512
    k = ids_ref[3] ^ ids_ref[2] ^ part
    tile_slot = k if back else k ^ ids_ref[2]

    def piece_copy(q):
        rows = pl.ds(q * step, step)
        return pltpu.make_async_copy(tiles_ref.at[tile_slot, rows], tile_ref.at[rows], sems.at[q])

    for q in range(length // step):
        piece_copy(q).start()
    for slot in range(2):

        @pl.when(k == slot)
        def _(slot=slot):
            for d in range(nz):
                for a in range(2):
                    piece = (cross_ref[d] if a else plane_ref[d]) if slot else pair_refs[d][a]
                    at = (nz * a + d) * points
                    raw_ref[:, at : at + points] = piece.T

    def order_step(i, carry):
        at = pl.multiple_of(i * step, step)
        index = perm_ref[k, :, pl.ds(at, step)] ^ (ids_ref[0] * points)
        place = lax.broadcasted_iota(jnp.int32, (length, step), 0)
        chosen = jnp.where(place == index, 1.0, 0.0).astype(jnp.bfloat16)
        found = jnp.dot(raw_ref[...], chosen, preferred_element_type=jnp.float32)
        if back:
            omega_ref[:, pl.ds(at, step)] = found.astype(jnp.bfloat16)
        else:
            omega_ref[pl.ds(at, step), :] = found.T.astype(jnp.bfloat16)
        return carry

    lax.fori_loop(0, length // step, order_step, 0)
    for q in range(length // step):
        piece_copy(q).wait()
    weight = weight_ref[tile_slot]
    for d in range(nz):
        for a in range(2):
            at = pl.multiple_of((a * nz + (ids_ref[1] ^ d)) * points, points)
            if back:
                value = jnp.dot(omega_ref[...], tile_ref[:, pl.ds(at, points)], preferred_element_type=jnp.float32).T
            else:
                value = jnp.dot(tile_ref[pl.ds(at, points), :], omega_ref[...], preferred_element_type=jnp.float32)
            value = value * weight
            if joins:
                value = value + decoded(more_ref[d, a])
            code = coded(value)
            if len(out_refs) == 1:
                out_refs[0][d, a] = code
            else:
                out_refs[d][a] = code


def products(ids, weight, perm, pairs, plane, cross, tiles, back, part, more=()):
    nz, points, probes = plane.shape
    length = tiles.shape[1]
    block = (2, points + EXTRA, probes)
    shapes = [(nz, *block)] if back and part == 0 else [block] * nz
    smem, vmem = pl.BlockSpec(memory_space=pltpu.SMEM), pl.BlockSpec(memory_space=pltpu.VMEM)
    return pl.pallas_call(
        functools.partial(product_kernel, back, part),
        out_shape=[jax.ShapeDtypeStruct(shape, jnp.int16) for shape in shapes],
        in_specs=[smem, smem] + [vmem] * (3 + nz) + [pl.BlockSpec(memory_space=pl.ANY)] + [vmem] * len(more),
        out_specs=[vmem] * len(shapes),
        scratch_shapes=[
            pltpu.VMEM(tiles.shape[1:], jnp.bfloat16),
            pltpu.VMEM((probes, length), jnp.bfloat16),
            pltpu.VMEM((probes, length) if back else (length, probes), jnp.bfloat16),
            pltpu.SemaphoreType.DMA((length // 512,)),
        ],
        compiler_params=pltpu.CompilerParams(vmem_limit_bytes=40 << 20),
        cost_estimate=pl.CostEstimate(flops=4 * length * length * probes, bytes_accessed=11 << 20, transcendentals=0),
    )(ids, weight, perm, *pairs, plane, cross, tiles, *more)


def sum_kernel(*refs):
    *in_refs, out_ref = refs
    for a in range(2):
        total = decoded(in_refs[0][a])
        for ref in in_refs[1:]:
            total = total + decoded(ref[a])
        out_ref[a] = coded(total)


def summed(codes):
    return pl.pallas_call(sum_kernel, out_shape=jax.ShapeDtypeStruct(codes[0].shape, jnp.int16), name="sum_back")(*codes)


def gram_kernel(ids_ref, *refs):
    *in_refs, samples_ref, other_ref, gram_ref = refs
    plane = ids_ref[3]
    half = gram_ref.shape[1]
    total = None
    for a in (plane, 1 - plane):
        block = decoded(in_refs[0][a])
        for ref in in_refs[1:]:
            block = block + decoded(ref[a])
        if total is None:
            samples_ref[plane] = block
        else:
            other_ref[...] = block
        left, right = block[:, :half], block[:, half:]
        parts = [
            lax.dot_general(x, y, (((0,), (0,)), ((), ())), preferred_element_type=jnp.float32, precision=EXACT)
            for x, y in ((left, left), (left, right), (right, right))
        ]
        total = parts if total is None else [x + y for x, y in zip(total, parts)]
    for n, part in enumerate(total):
        gram_ref[n * half : (n + 1) * half, :] = part


def gram_of(ids, codes):
    _, rows, probes = codes[0].shape
    points = rows - EXTRA
    return pl.pallas_call(
        gram_kernel,
        in_specs=[pl.BlockSpec(memory_space=pltpu.SMEM)] + [pl.BlockSpec(memory_space=pltpu.VMEM)] * len(codes),
        out_shape=[
            jax.ShapeDtypeStruct((2, points, probes), jnp.float32),
            jax.ShapeDtypeStruct((points, probes), jnp.float32),
            jax.ShapeDtypeStruct((3 * probes // 2, probes // 2), jnp.float32),
        ],
        name="gram",
    )(ids, *codes)


def half_inverse(a_ref, out_ref, m_ref, tall_ref, u_ref, v_ref):
    n, size = a_ref.shape[0], u_ref.shape[0]
    rows = lax.broadcasted_iota(jnp.int32, (n, n), 0)
    cols = lax.broadcasted_iota(jnp.int32, (n, n), 1)
    m_ref[...] = (rows == cols).astype(jnp.float32)
    for ref in (tall_ref, u_ref, v_ref):
        ref[...] = jnp.zeros_like(ref)
    lane = lax.broadcasted_iota(jnp.int32, (size, n), 1)
    sub = lax.broadcasted_iota(jnp.int32, (size, n), 0)

    def spread(array, i):
        return jnp.broadcast_to(array[i : i + 1, :], (size, n))

    def group(b, carry):
        at = pl.multiple_of(b * size, size)
        u, v, near = u_ref[...], v_ref[...], tall_ref[pl.ds(at, size), :]
        panel, inverse = a_ref[pl.ds(at, size), :], m_ref[pl.ds(at, size), :]
        old_a, old_m, tall = a_ref[...], m_ref[...], tall_ref[...]
        for t in range(size):
            factor = jnp.broadcast_to(near[:, t : t + 1], (size, n))
            panel = panel - factor * u[t : t + 1, :]
            inverse = inverse - factor * v[t : t + 1, :]
        small = pltpu.roll(panel, n - at, axis=1)
        s = [[None] * size for _ in range(size)]
        e = [[None] * size for _ in range(size)]
        for t in range(size):
            column = jnp.broadcast_to(small[:, t : t + 1], (size, n))
            for i in range(t, size):
                s[i][t] = spread(column, i)
        for t in range(size - 1):
            ratio = 1.0 / s[t][t]
            for i in range(t + 1, size):
                factor = s[i][t] * ratio
                for j in range(t + 1, i + 1):
                    s[i][j] = s[i][j] - factor * s[j][t]
                for j in range(t):
                    e[i][j] = e[i][j] - factor * e[t][j]
                e[i][t] = -factor
        scale = s[0][0]
        for t in range(1, size):
            scale = jnp.where(sub == t, s[t][t], scale)
        scale = lax.rsqrt(scale)
        new_u, new_v = panel, inverse
        for t in range(size - 1):
            factor = jnp.zeros((size, n), jnp.float32)
            for i in range(t + 1, size):
                factor = jnp.where(sub == i, e[i][t], factor)
            new_u = new_u + factor * panel[t : t + 1, :]
            new_v = new_v + factor * inverse[t : t + 1, :]
        new_u = jnp.where(lane >= at + sub, new_u * scale, 0.0)
        new_v = new_v * scale
        for t in range(size):
            factor = jnp.broadcast_to(tall[:, t : t + 1], (n, n))
            old_a = old_a - factor * u[t : t + 1, :]
            old_m = old_m - factor * v[t : t + 1, :]
        a_ref[...], m_ref[...] = old_a, old_m
        out_ref[pl.ds(at, size), :] = new_v
        u_ref[...], v_ref[...] = new_u, new_v
        tall_ref[...] = new_u.T
        return carry

    lax.fori_loop(0, n // size, group, 0)


def factor_kernel(scale, ids_ref, samples_ref, other_ref, *refs):
    *gram_refs, basis_ref, out_ref, a_ref, m1_ref, m2_ref = refs[:9]
    work = refs[9:]
    half = a_ref.shape[0]
    plane = ids_ref[3]

    def product(a, b, over):
        return lax.dot_general(
            a, b, ((over[:1], over[1:]), ((), ())), preferred_element_type=jnp.float32, precision=EXACT
        )

    def gram(n):
        rows = slice(n * half, (n + 1) * half)
        one, two, three, four = (ref[rows, :] for ref in gram_refs)
        return ((one + two) + (three + four)) * scale

    a_ref[...] = gram(0)
    half_inverse(a_ref, m1_ref, *work)
    first = m1_ref[...]
    cross = product(first, gram(1), (1, 0))
    a_ref[...] = gram(2) - product(cross, cross, (0, 0))
    half_inverse(a_ref, m2_ref, *work)
    second = m2_ref[...]
    mixed = -product(second, product(cross, first, (0, 0)), (1, 0))
    for n, block in enumerate((samples_ref[plane], other_ref[...])):
        left, right = block[:, :half], block[:, half:]
        made = (product(left, first, (1, 1)), product(left, mixed, (1, 1)) + product(right, second, (1, 1)))
        for m, value in enumerate(made):
            columns = slice(m * half, (m + 1) * half)
            if n:
                out_ref[:, columns] = value
            else:
                basis_ref[plane, :, columns] = value


def orthogonal(ids, samples, other, grams, scale):
    half = grams[0].shape[1]
    return pl.pallas_call(
        functools.partial(factor_kernel, scale),
        in_specs=[pl.BlockSpec(memory_space=pltpu.SMEM)] + [pl.BlockSpec(memory_space=pltpu.VMEM)] * (2 + len(grams)),
        out_shape=[jax.ShapeDtypeStruct(x.shape, jnp.float32) for x in (samples, other)],
        scratch_shapes=[
            pltpu.VMEM(shape, jnp.float32) for shape in [(half, half)] * 4 + [(half, 8), (8, half), (8, half)]
        ],
        name="orthogonal",
    )(ids, samples, other, *grams)


def whole_step(tiles, probe, cluster_perm, tile_keep):
    row_id = lax.axis_index("row")
    col_id = lax.axis_index("col")
    nrows = lax.axis_size("row")
    ncols = lax.axis_size("col")
    tile_len = tiles.shape[1]
    nz = ncols // 2
    plane, depth = col_id // nz, col_id % nz
    wraps = (row_id + col_id >= nrows).astype(jnp.int32)
    ids = jnp.stack([col_id, depth, wraps, plane]).astype(jnp.int32)
    weight = jnp.where(col_id == 0, 0.5, tile_keep[:, 0, 0].astype(jnp.float32))

    def same(d):
        return lambda r, c: (r, c ^ d)

    def slanted(d):
        return lambda r, c: (r + c - (c ^ d), c ^ d)

    def far(r, c):
        return (r - c, c)

    depths = range(1, nz)
    other = sent(probe[0], same(nz))
    singles = [sent(probe[1], same(d)) for d in depths]
    far_own = sent(probe[0], far)
    far_other = sent(probe[0], lambda r, c: (r - (c ^ nz), c ^ nz))
    far_perm = sent(cluster_perm, far)

    pair = jnp.stack([probe[0], other])
    line = jnp.stack([probe[1], *singles])
    far_pair = jnp.stack([far_own, far_other])
    cross = sent(line, same(nz))
    far_line = sent(line, far)
    pairs = [sent(pair, same(d)) for d in depths]
    far_pairs = [sent(far_pair, slanted(d)) for d in depths]
    far_cross = sent(cross, far)

    perm, far_perm = (x.reshape(-1, 1, tile_len) for x in (cluster_perm, far_perm))
    own_blocks = ([pair, *pairs], line, cross)
    far_blocks = ([far_pair, *far_pairs], far_line, far_cross)

    (more,) = products(ids, weight, perm, *own_blocks, tiles, True, 0)
    more = sent(more, lambda r, c: (r + c, c))
    back = products(ids, weight, perm, *own_blocks, tiles, True, 1)
    back, far_pairs = lax.optimization_barrier((back, far_pairs))
    back = [back[0]] + [sent(back[d], slanted(d)) for d in depths]
    given = products(ids, weight, far_perm, *far_blocks, tiles, False, 1)
    given = [sent(code, same(nz + d)) for d, code in enumerate(given)]
    kept = products(ids, weight, far_perm, *far_blocks, tiles, False, 0, (more,))
    kept = [kept[0]] + [sent(kept[d], same(d)) for d in depths]
    arrived = summed(back)
    arrived = sent(arrived, lambda r, c: (r + c, c ^ nz))
    samples, swapped, gram = gram_of(ids, [*kept, *given, arrived])
    grams = [gram] + [sent(gram, same(d)) for d in depths]
    basis, swapped_basis = orthogonal(ids, samples, swapped, grams, 1.0 / tile_len)

    def placed(array, theirs):
        return lax.dynamic_update_index_in_dim(array, sent(theirs, same(nz)), 1 - plane, 0)

    return (placed(samples, swapped), placed(basis, swapped_basis))


def solution(mesh):
    whole = P(None, ("row", "col"), None)
    return jax.shard_map(
        whole_step,
        mesh=mesh,
        in_specs=(P(None, "row", "col"), whole, P(None, "row", None), P(None, "row", "col")),
        out_specs=(whole, whole),
        check_vma=False,
    )
```

```python
import functools

import jax
import jax.numpy as jnp
from jax import lax
from jax.experimental import pallas as pl
from jax.experimental.pallas import tpu as pltpu
from jax.sharding import PartitionSpec as P


AXES = ("row", "col")
EXACT = lax.Precision.HIGHEST
LEVELS = 32767.0
EXTRA = 16


def sent(value, to):
    nrows, ncols = lax.axis_size("row"), lax.axis_size("col")
    pairs = []
    for r in range(nrows):
        for c in range(ncols):
            r_to, c_to = to(r, c)
            pairs.append((r * ncols + c, (r_to % nrows) * ncols + c_to))
    return lax.ppermute(value, AXES, pairs)


def scale_of(exponent, mantissa):
    return jnp.exp2(exponent) * (mantissa * (1.0 / (LEVELS * LEVELS)))


def coded(block):
    largest = jnp.maximum(jnp.max(jnp.abs(block), axis=0, keepdims=True), 1e-30)
    exponent = jnp.floor(jnp.log2(largest * 1.0001)) + 1.0
    mantissa = jnp.ceil(largest * jnp.exp2(-exponent) * LEVELS)
    scale = scale_of(exponent, mantissa)
    values = jnp.clip(jnp.round(block * (1.0 / scale)), -LEVELS, LEVELS)
    at = lax.broadcasted_iota(jnp.int32, (EXTRA, block.shape[1]), 0)
    tail = jnp.where(at == 0, exponent, mantissa)
    return jnp.concatenate([values, tail], axis=0).astype(jnp.int32).astype(jnp.int16)


def decoded(code):
    wide = code.astype(jnp.int32).astype(jnp.float32)
    rows = code.shape[0] - EXTRA
    return wide[:rows] * scale_of(wide[rows : rows + 1], wide[rows + 1 : rows + 2])


def product_kernel(back, part, ids_ref, weight_ref, perm_ref, *refs):
    *pair_refs, plane_ref, cross_ref, tiles_ref = refs[:7]
    joins = not back and part == 0
    more_ref = refs[7] if joins else None
    *out_refs, tile_ref, raw_ref, omega_ref, sems = refs[8 if joins else 7 :]
    nz, points, _ = plane_ref.shape
    length = raw_ref.shape[1]
    step = 512
    k = ids_ref[3] ^ ids_ref[2] ^ part
    tile_slot = k if back else k ^ ids_ref[2]

    def piece_copy(q):
        rows = pl.ds(q * step, step)
        return pltpu.make_async_copy(tiles_ref.at[tile_slot, rows], tile_ref.at[rows], sems.at[q])

    for q in range(length // step):
        piece_copy(q).start()
    for slot in range(2):

        @pl.when(k == slot)
        def _(slot=slot):
            for d in range(nz):
                for a in range(2):
                    piece = (cross_ref[d] if a else plane_ref[d]) if slot else pair_refs[d][a]
                    at = (nz * a + d) * points
                    raw_ref[:, at : at + points] = piece.T

    def order_step(i, carry):
        at = pl.multiple_of(i * step, step)
        index = perm_ref[k, :, pl.ds(at, step)] ^ (ids_ref[0] * points)
        place = lax.broadcasted_iota(jnp.int32, (length, step), 0)
        chosen = jnp.where(place == index, 1.0, 0.0).astype(jnp.bfloat16)
        found = jnp.dot(raw_ref[...], chosen, preferred_element_type=jnp.float32)
        if back:
            omega_ref[:, pl.ds(at, step)] = found.astype(jnp.bfloat16)
        else:
            omega_ref[pl.ds(at, step), :] = found.T.astype(jnp.bfloat16)
        return carry

    lax.fori_loop(0, length // step, order_step, 0)
    for q in range(length // step):
        piece_copy(q).wait()
    weight = weight_ref[tile_slot]
    for d in range(nz):
        for a in range(2):
            at = pl.multiple_of((a * nz + (ids_ref[1] ^ d)) * points, points)
            if back:
                value = jnp.dot(omega_ref[...], tile_ref[:, pl.ds(at, points)], preferred_element_type=jnp.float32).T
            else:
                value = jnp.dot(tile_ref[pl.ds(at, points), :], omega_ref[...], preferred_element_type=jnp.float32)
            value = value * weight
            if joins:
                value = value + decoded(more_ref[d, a])
            code = coded(value)
            if len(out_refs) == 1:
                out_refs[0][d, a] = code
            else:
                out_refs[d][a] = code


def products(ids, weight, perm, pairs, plane, cross, tiles, back, part, more=()):
    nz, points, probes = plane.shape
    length = tiles.shape[1]
    block = (2, points + EXTRA, probes)
    shapes = [(nz, *block)] if back and part == 0 else [block] * nz
    smem, vmem = pl.BlockSpec(memory_space=pltpu.SMEM), pl.BlockSpec(memory_space=pltpu.VMEM)
    return pl.pallas_call(
        functools.partial(product_kernel, back, part),
        out_shape=[jax.ShapeDtypeStruct(shape, jnp.int16) for shape in shapes],
        in_specs=[smem, smem] + [vmem] * (3 + nz) + [pl.BlockSpec(memory_space=pl.ANY)] + [vmem] * len(more),
        out_specs=[vmem] * len(shapes),
        scratch_shapes=[
            pltpu.VMEM(tiles.shape[1:], jnp.bfloat16),
            pltpu.VMEM((probes, length), jnp.bfloat16),
            pltpu.VMEM((probes, length) if back else (length, probes), jnp.bfloat16),
            pltpu.SemaphoreType.DMA((length // 512,)),
        ],
        compiler_params=pltpu.CompilerParams(vmem_limit_bytes=40 << 20),
        cost_estimate=pl.CostEstimate(flops=4 * length * length * probes, bytes_accessed=11 << 20, transcendentals=0),
    )(ids, weight, perm, *pairs, plane, cross, tiles, *more)


def sum_kernel(count, *refs):
    out_ref = refs[-1]
    for a in range(2):
        total = decoded(refs[0][a])
        for ref in refs[1:count]:
            total = total + decoded(ref[a])
        out_ref[a] = coded(total)


def summed(codes, after=()):
    vmem, unread = pl.BlockSpec(memory_space=pltpu.VMEM), pl.BlockSpec(memory_space=pl.ANY)
    return pl.pallas_call(
        functools.partial(sum_kernel, len(codes)),
        in_specs=[vmem] * len(codes) + [unread] * len(after),
        out_shape=jax.ShapeDtypeStruct(codes[0].shape, jnp.int16),
        name="sum",
    )(*codes, *after)


def gram_kernel(ids_ref, *refs):
    *in_refs, samples_ref, other_ref, gram_ref = refs
    plane = ids_ref[3]
    half = gram_ref.shape[1]
    total = None
    for a in (plane, 1 - plane):
        block = decoded(in_refs[0][a])
        for ref in in_refs[1:]:
            block = block + decoded(ref[a])
        if total is None:
            samples_ref[plane] = block
        else:
            other_ref[...] = block
        left, right = block[:, :half], block[:, half:]
        parts = [
            lax.dot_general(x, y, (((0,), (0,)), ((), ())), preferred_element_type=jnp.float32, precision=EXACT)
            for x, y in ((left, left), (left, right), (right, right))
        ]
        total = parts if total is None else [x + y for x, y in zip(total, parts)]
    for n, part in enumerate(total):
        gram_ref[n * half : (n + 1) * half, :] = part


def gram_of(ids, codes):
    _, rows, probes = codes[0].shape
    points = rows - EXTRA
    return pl.pallas_call(
        gram_kernel,
        in_specs=[pl.BlockSpec(memory_space=pltpu.SMEM)] + [pl.BlockSpec(memory_space=pltpu.VMEM)] * len(codes),
        out_shape=[
            jax.ShapeDtypeStruct((2, points, probes), jnp.float32),
            jax.ShapeDtypeStruct((points, probes), jnp.float32),
            jax.ShapeDtypeStruct((3 * probes // 2, probes // 2), jnp.float32),
        ],
        name="gram",
    )(ids, *codes)


def half_inverse(a_ref, out_ref, m_ref, tall_ref, u_ref, v_ref):
    n, size = a_ref.shape[0], u_ref.shape[0]
    rows = lax.broadcasted_iota(jnp.int32, (n, n), 0)
    cols = lax.broadcasted_iota(jnp.int32, (n, n), 1)
    m_ref[...] = (rows == cols).astype(jnp.float32)
    for ref in (tall_ref, u_ref, v_ref):
        ref[...] = jnp.zeros_like(ref)
    lane = lax.broadcasted_iota(jnp.int32, (size, n), 1)
    sub = lax.broadcasted_iota(jnp.int32, (size, n), 0)

    def spread(array, i):
        return jnp.broadcast_to(array[i : i + 1, :], (size, n))

    def group(b, carry):
        at = pl.multiple_of(b * size, size)
        u, v, near = u_ref[...], v_ref[...], tall_ref[pl.ds(at, size), :]
        panel, inverse = a_ref[pl.ds(at, size), :], m_ref[pl.ds(at, size), :]
        old_a, old_m, tall = a_ref[...], m_ref[...], tall_ref[...]
        for t in range(size):
            factor = jnp.broadcast_to(near[:, t : t + 1], (size, n))
            panel = panel - factor * u[t : t + 1, :]
            inverse = inverse - factor * v[t : t + 1, :]
        small = pltpu.roll(panel, n - at, axis=1)
        s = [[None] * size for _ in range(size)]
        e = [[None] * size for _ in range(size)]
        for t in range(size):
            column = jnp.broadcast_to(small[:, t : t + 1], (size, n))
            for i in range(t, size):
                s[i][t] = spread(column, i)
        for t in range(size - 1):
            ratio = 1.0 / s[t][t]
            for i in range(t + 1, size):
                factor = s[i][t] * ratio
                for j in range(t + 1, i + 1):
                    s[i][j] = s[i][j] - factor * s[j][t]
                for j in range(t):
                    e[i][j] = e[i][j] - factor * e[t][j]
                e[i][t] = -factor
        scale = s[0][0]
        for t in range(1, size):
            scale = jnp.where(sub == t, s[t][t], scale)
        scale = lax.rsqrt(scale)
        new_u, new_v = panel, inverse
        for t in range(size - 1):
            factor = jnp.zeros((size, n), jnp.float32)
            for i in range(t + 1, size):
                factor = jnp.where(sub == i, e[i][t], factor)
            new_u = new_u + factor * panel[t : t + 1, :]
            new_v = new_v + factor * inverse[t : t + 1, :]
        new_u = jnp.where(lane >= at + sub, new_u * scale, 0.0)
        new_v = new_v * scale
        for t in range(size):
            factor = jnp.broadcast_to(tall[:, t : t + 1], (n, n))
            old_a = old_a - factor * u[t : t + 1, :]
            old_m = old_m - factor * v[t : t + 1, :]
        a_ref[...], m_ref[...] = old_a, old_m
        out_ref[pl.ds(at, size), :] = new_v
        u_ref[...], v_ref[...] = new_u, new_v
        tall_ref[...] = new_u.T
        return carry

    lax.fori_loop(0, n // size, group, 0)


def factor_kernel(scale, ids_ref, samples_ref, other_ref, *refs):
    *gram_refs, basis_ref, out_ref, a_ref, m1_ref, m2_ref = refs[:9]
    work = refs[9:]
    half = a_ref.shape[0]
    plane = ids_ref[3]

    def product(a, b, over):
        return lax.dot_general(
            a, b, ((over[:1], over[1:]), ((), ())), preferred_element_type=jnp.float32, precision=EXACT
        )

    def gram(n):
        rows = slice(n * half, (n + 1) * half)
        one, two, three, four = (ref[rows, :] for ref in gram_refs)
        return ((one + two) + (three + four)) * scale

    a_ref[...] = gram(0)
    half_inverse(a_ref, m1_ref, *work)
    first = m1_ref[...]
    cross = product(first, gram(1), (1, 0))
    a_ref[...] = gram(2) - product(cross, cross, (0, 0))
    half_inverse(a_ref, m2_ref, *work)
    second = m2_ref[...]
    mixed = -product(second, product(cross, first, (0, 0)), (1, 0))
    for n, block in enumerate((samples_ref[plane], other_ref[...])):
        left, right = block[:, :half], block[:, half:]
        made = (product(left, first, (1, 1)), product(left, mixed, (1, 1)) + product(right, second, (1, 1)))
        for m, value in enumerate(made):
            columns = slice(m * half, (m + 1) * half)
            if n:
                out_ref[:, columns] = value
            else:
                basis_ref[plane, :, columns] = value


def orthogonal(ids, samples, other, grams, scale):
    half = grams[0].shape[1]
    return pl.pallas_call(
        functools.partial(factor_kernel, scale),
        in_specs=[pl.BlockSpec(memory_space=pltpu.SMEM)] + [pl.BlockSpec(memory_space=pltpu.VMEM)] * (2 + len(grams)),
        out_shape=[jax.ShapeDtypeStruct(x.shape, jnp.float32) for x in (samples, other)],
        scratch_shapes=[
            pltpu.VMEM(shape, jnp.float32) for shape in [(half, half)] * 4 + [(half, 8), (8, half), (8, half)]
        ],
        name="orthogonal",
    )(ids, samples, other, *grams)


def whole_step(tiles, probe, cluster_perm, tile_keep):
    row_id = lax.axis_index("row")
    col_id = lax.axis_index("col")
    nrows = lax.axis_size("row")
    ncols = lax.axis_size("col")
    tile_len = tiles.shape[1]
    nz = ncols // 2
    plane, depth = col_id // nz, col_id % nz
    wraps = (row_id + col_id >= nrows).astype(jnp.int32)
    ids = jnp.stack([col_id, depth, wraps, plane]).astype(jnp.int32)
    weight = jnp.where(col_id == 0, 0.5, tile_keep[:, 0, 0].astype(jnp.float32))

    def same(d):
        return lambda r, c: (r, c ^ d)

    def slanted(d):
        return lambda r, c: (r + c - (c ^ d), c ^ d)

    def far(r, c):
        return (r - c, c)

    depths = range(1, nz)
    other = sent(probe[0], same(nz))
    singles = [sent(probe[1], same(d)) for d in depths]
    far_own = sent(probe[0], far)
    far_other = sent(probe[0], lambda r, c: (r - (c ^ nz), c ^ nz))
    far_perm = sent(cluster_perm, far)

    pair = jnp.stack([probe[0], other])
    line = jnp.stack([probe[1], *singles])
    far_pair = jnp.stack([far_own, far_other])
    cross = sent(line, same(nz))
    far_line = sent(line, far)
    pairs = [sent(pair, same(d)) for d in depths]
    far_pairs = [sent(far_pair, slanted(d)) for d in depths]
    far_cross = sent(cross, far)

    perm, far_perm = (x.reshape(-1, 1, tile_len) for x in (cluster_perm, far_perm))
    own_blocks = ([pair, *pairs], line, cross)
    far_blocks = ([far_pair, *far_pairs], far_line, far_cross)

    (more,) = products(ids, weight, perm, *own_blocks, tiles, True, 0)
    more = sent(more, lambda r, c: (r + c, c))
    back = products(ids, weight, perm, *own_blocks, tiles, True, 1)
    back, far_pairs = lax.optimization_barrier((back, far_pairs))
    back = [back[0]] + [sent(back[d], slanted(d)) for d in depths]
    given = products(ids, weight, far_perm, *far_blocks, tiles, False, 1)
    given = [given[0]] + [sent(given[d], same(d)) for d in depths]
    kept = products(ids, weight, far_perm, *far_blocks, tiles, False, 0, (more,))
    arrived = sent(summed(back, kept[:1]), lambda r, c: (r + c, c))
    kept = [kept[0]] + [sent(kept[d], same(d)) for d in depths]
    crossed = sent(summed([*given, arrived]), same(nz))
    samples, swapped, gram = gram_of(ids, [*kept, crossed])
    grams = [gram] + [sent(gram, same(d)) for d in depths]
    basis, swapped_basis = orthogonal(ids, samples, swapped, grams, 1.0 / tile_len)

    def placed(array, theirs):
        return lax.dynamic_update_index_in_dim(array, sent(theirs, same(nz)), 1 - plane, 0)

    return (placed(samples, swapped), placed(basis, swapped_basis))


def solution(mesh):
    whole = P(None, ("row", "col"), None)
    return jax.shard_map(
        whole_step,
        mesh=mesh,
        in_specs=(P(None, "row", "col"), whole, P(None, "row", None), P(None, "row", "col")),
        out_specs=(whole, whole),
        check_vma=False,
    )
```

```python
import functools

import jax
import jax.numpy as jnp
from jax import lax
from jax.experimental import pallas as pl
from jax.experimental.pallas import tpu as pltpu
from jax.sharding import PartitionSpec as P


AXES = ("row", "col")
EXACT = lax.Precision.HIGHEST
LEVELS = 32767.0
EXTRA = 16


def sent(value, to):
    nrows, ncols = lax.axis_size("row"), lax.axis_size("col")
    pairs = []
    for r in range(nrows):
        for c in range(ncols):
            r_to, c_to = to(r, c)
            pairs.append((r * ncols + c, (r_to % nrows) * ncols + c_to))
    return lax.ppermute(value, AXES, pairs)


def scale_of(exponent, mantissa):
    return jnp.exp2(exponent) * (mantissa * (1.0 / (LEVELS * LEVELS)))


def coded(block):
    largest = jnp.maximum(jnp.max(jnp.abs(block), axis=0, keepdims=True), 1e-30)
    exponent = jnp.floor(jnp.log2(largest * 1.0001)) + 1.0
    mantissa = jnp.ceil(largest * jnp.exp2(-exponent) * LEVELS)
    scale = scale_of(exponent, mantissa)
    values = jnp.clip(jnp.round(block * (1.0 / scale)), -LEVELS, LEVELS)
    at = lax.broadcasted_iota(jnp.int32, (EXTRA, block.shape[1]), 0)
    tail = jnp.where(at == 0, exponent, mantissa)
    return jnp.concatenate([values, tail], axis=0).astype(jnp.int32).astype(jnp.int16)


def decoded(code):
    wide = code.astype(jnp.int32).astype(jnp.float32)
    rows = code.shape[0] - EXTRA
    return wide[:rows] * scale_of(wide[rows : rows + 1], wide[rows + 1 : rows + 2])


def product_kernel(back, part, ids_ref, weight_ref, perm_ref, *refs):
    *pair_refs, plane_ref, cross_ref, tiles_ref = refs[:7]
    joins = not back and part == 0
    more_ref = refs[7] if joins else None
    *out_refs, tile_ref, raw_ref, omega_ref, sems = refs[8 if joins else 7 :]
    nz, points, _ = plane_ref.shape
    length = raw_ref.shape[1]
    step = 512
    k = ids_ref[3] ^ ids_ref[2] ^ part
    tile_slot = k if back else k ^ ids_ref[2]

    def piece_copy(q):
        rows = pl.ds(q * step, step)
        return pltpu.make_async_copy(tiles_ref.at[tile_slot, rows], tile_ref.at[rows], sems.at[q])

    for q in range(length // step):
        piece_copy(q).start()
    for slot in range(2):

        @pl.when(k == slot)
        def _(slot=slot):
            for d in range(nz):
                for a in range(2):
                    piece = (cross_ref[d] if a else plane_ref[d]) if slot else pair_refs[d][a]
                    at = (nz * a + d) * points
                    raw_ref[:, at : at + points] = piece.T

    def order_step(i, carry):
        at = pl.multiple_of(i * step, step)
        index = perm_ref[k, :, pl.ds(at, step)] ^ (ids_ref[0] * points)
        place = lax.broadcasted_iota(jnp.int32, (length, step), 0)
        chosen = jnp.where(place == index, 1.0, 0.0).astype(jnp.bfloat16)
        found = jnp.dot(raw_ref[...], chosen, preferred_element_type=jnp.float32)
        if back:
            omega_ref[:, pl.ds(at, step)] = found.astype(jnp.bfloat16)
        else:
            omega_ref[pl.ds(at, step), :] = found.T.astype(jnp.bfloat16)
        return carry

    lax.fori_loop(0, length // step, order_step, 0)
    for q in range(length // step):
        piece_copy(q).wait()
    weight = weight_ref[tile_slot]
    for d in range(nz):
        for a in range(2):
            at = pl.multiple_of((a * nz + (ids_ref[1] ^ d)) * points, points)
            if back:
                value = jnp.dot(omega_ref[...], tile_ref[:, pl.ds(at, points)], preferred_element_type=jnp.float32).T
            else:
                value = jnp.dot(tile_ref[pl.ds(at, points), :], omega_ref[...], preferred_element_type=jnp.float32)
            value = value * weight
            if joins:
                value = value + decoded(more_ref[d, a])
            code = coded(value)
            if len(out_refs) == 1:
                out_refs[0][d, a] = code
            else:
                out_refs[d][a] = code


def products(ids, weight, perm, pairs, plane, cross, tiles, back, part, more=()):
    nz, points, probes = plane.shape
    length = tiles.shape[1]
    block = (2, points + EXTRA, probes)
    shapes = [(nz, *block)] if back and part == 0 else [block] * nz
    smem, vmem = pl.BlockSpec(memory_space=pltpu.SMEM), pl.BlockSpec(memory_space=pltpu.VMEM)
    return pl.pallas_call(
        functools.partial(product_kernel, back, part),
        out_shape=[jax.ShapeDtypeStruct(shape, jnp.int16) for shape in shapes],
        in_specs=[smem, smem] + [vmem] * (3 + nz) + [pl.BlockSpec(memory_space=pl.ANY)] + [vmem] * len(more),
        out_specs=[vmem] * len(shapes),
        scratch_shapes=[
            pltpu.VMEM(tiles.shape[1:], jnp.bfloat16),
            pltpu.VMEM((probes, length), jnp.bfloat16),
            pltpu.VMEM((probes, length) if back else (length, probes), jnp.bfloat16),
            pltpu.SemaphoreType.DMA((length // 512,)),
        ],
        compiler_params=pltpu.CompilerParams(vmem_limit_bytes=40 << 20),
        cost_estimate=pl.CostEstimate(flops=4 * length * length * probes, bytes_accessed=11 << 20, transcendentals=0),
    )(ids, weight, perm, *pairs, plane, cross, tiles, *more)


def sum_kernel(count, *refs):
    out_ref = refs[-1]
    for a in range(2):
        total = decoded(refs[0][a])
        for ref in refs[1:count]:
            total = total + decoded(ref[a])
        out_ref[a] = coded(total)


def summed(codes, after=()):
    vmem, unread = pl.BlockSpec(memory_space=pltpu.VMEM), pl.BlockSpec(memory_space=pl.ANY)
    return pl.pallas_call(
        functools.partial(sum_kernel, len(codes)),
        in_specs=[vmem] * len(codes) + [unread] * len(after),
        out_shape=jax.ShapeDtypeStruct(codes[0].shape, jnp.int16),
        name="sum",
    )(*codes, *after)


def gram_kernel(ids_ref, *refs):
    *in_refs, samples_ref, other_ref, gram_ref = refs
    plane = ids_ref[3]
    half = gram_ref.shape[1]
    total = None
    for a in (plane, 1 - plane):
        block = decoded(in_refs[0][a])
        for ref in in_refs[1:]:
            block = block + decoded(ref[a])
        if total is None:
            samples_ref[plane] = block
        else:
            other_ref[...] = block
        left, right = block[:, :half], block[:, half:]
        parts = [
            lax.dot_general(x, y, (((0,), (0,)), ((), ())), preferred_element_type=jnp.float32, precision=EXACT)
            for x, y in ((left, left), (left, right), (right, right))
        ]
        total = parts if total is None else [x + y for x, y in zip(total, parts)]
    for n, part in enumerate(total):
        gram_ref[n * half : (n + 1) * half, :] = part


def gram_of(ids, codes):
    _, rows, probes = codes[0].shape
    points = rows - EXTRA
    return pl.pallas_call(
        gram_kernel,
        in_specs=[pl.BlockSpec(memory_space=pltpu.SMEM)] + [pl.BlockSpec(memory_space=pltpu.VMEM)] * len(codes),
        out_shape=[
            jax.ShapeDtypeStruct((2, points, probes), jnp.float32),
            jax.ShapeDtypeStruct((points, probes), jnp.float32),
            jax.ShapeDtypeStruct((3 * probes // 2, probes // 2), jnp.float32),
        ],
        name="gram",
    )(ids, *codes)


def half_inverse(a_ref, out_ref, m_ref, tall_ref, u_ref, v_ref):
    n, size = a_ref.shape[0], u_ref.shape[0]
    rows = lax.broadcasted_iota(jnp.int32, (n, n), 0)
    cols = lax.broadcasted_iota(jnp.int32, (n, n), 1)
    m_ref[...] = (rows == cols).astype(jnp.float32)
    for ref in (tall_ref, u_ref, v_ref):
        ref[...] = jnp.zeros_like(ref)
    lane = lax.broadcasted_iota(jnp.int32, (size, n), 1)
    sub = lax.broadcasted_iota(jnp.int32, (size, n), 0)

    def spread(array, i):
        return jnp.broadcast_to(array[i : i + 1, :], (size, n))

    def group(b, carry):
        at = pl.multiple_of(b * size, size)
        u, v, near = u_ref[...], v_ref[...], tall_ref[pl.ds(at, size), :]
        panel, inverse = a_ref[pl.ds(at, size), :], m_ref[pl.ds(at, size), :]
        old_a, old_m, tall = a_ref[...], m_ref[...], tall_ref[...]
        for t in range(size):
            factor = jnp.broadcast_to(near[:, t : t + 1], (size, n))
            panel = panel - factor * u[t : t + 1, :]
            inverse = inverse - factor * v[t : t + 1, :]
        small = pltpu.roll(panel, n - at, axis=1)
        s = [[None] * size for _ in range(size)]
        e = [[None] * size for _ in range(size)]
        for t in range(size):
            column = jnp.broadcast_to(small[:, t : t + 1], (size, n))
            for i in range(t, size):
                s[i][t] = spread(column, i)
        for t in range(size - 1):
            ratio = 1.0 / s[t][t]
            for i in range(t + 1, size):
                factor = s[i][t] * ratio
                for j in range(t + 1, i + 1):
                    s[i][j] = s[i][j] - factor * s[j][t]
                for j in range(t):
                    e[i][j] = e[i][j] - factor * e[t][j]
                e[i][t] = -factor
        scale = s[0][0]
        for t in range(1, size):
            scale = jnp.where(sub == t, s[t][t], scale)
        scale = lax.rsqrt(scale)
        new_u, new_v = panel, inverse
        for t in range(size - 1):
            factor = jnp.zeros((size, n), jnp.float32)
            for i in range(t + 1, size):
                factor = jnp.where(sub == i, e[i][t], factor)
            new_u = new_u + factor * panel[t : t + 1, :]
            new_v = new_v + factor * inverse[t : t + 1, :]
        new_u = jnp.where(lane >= at + sub, new_u * scale, 0.0)
        new_v = new_v * scale
        update = jnp.dot(
            tall, jnp.concatenate([u, v], axis=1), preferred_element_type=jnp.float32, precision=EXACT
        )
        a_ref[...], m_ref[...] = old_a - update[:, :n], old_m - update[:, n:]
        out_ref[pl.ds(at, size), :] = new_v
        u_ref[...], v_ref[...] = new_u, new_v
        tall_ref[...] = new_u.T
        return carry

    lax.fori_loop(0, n // size, group, 0)


def factor_kernel(scale, ids_ref, samples_ref, other_ref, *refs):
    *gram_refs, basis_ref, out_ref, a_ref, m1_ref, m2_ref = refs[:9]
    work = refs[9:]
    half = a_ref.shape[0]
    plane = ids_ref[3]

    def product(a, b, over):
        return lax.dot_general(
            a, b, ((over[:1], over[1:]), ((), ())), preferred_element_type=jnp.float32, precision=EXACT
        )

    def gram(n):
        rows = slice(n * half, (n + 1) * half)
        one, two, three, four = (ref[rows, :] for ref in gram_refs)
        return ((one + two) + (three + four)) * scale

    a_ref[...] = gram(0)
    half_inverse(a_ref, m1_ref, *work)
    first = m1_ref[...]
    cross = product(first, gram(1), (1, 0))
    a_ref[...] = gram(2) - product(cross, cross, (0, 0))
    half_inverse(a_ref, m2_ref, *work)
    second = m2_ref[...]
    mixed = -product(second, product(cross, first, (0, 0)), (1, 0))
    for n, block in enumerate((samples_ref[plane], other_ref[...])):
        left, right = block[:, :half], block[:, half:]
        made = (product(left, first, (1, 1)), product(left, mixed, (1, 1)) + product(right, second, (1, 1)))
        for m, value in enumerate(made):
            columns = slice(m * half, (m + 1) * half)
            if n:
                out_ref[:, columns] = coded(value)
            else:
                basis_ref[plane, :, columns] = value


def orthogonal(ids, samples, other, grams, scale):
    half = grams[0].shape[1]
    return pl.pallas_call(
        functools.partial(factor_kernel, scale),
        in_specs=[pl.BlockSpec(memory_space=pltpu.SMEM)] + [pl.BlockSpec(memory_space=pltpu.VMEM)] * (2 + len(grams)),
        out_shape=[
            jax.ShapeDtypeStruct(samples.shape, jnp.float32),
            jax.ShapeDtypeStruct((other.shape[0] + EXTRA, other.shape[1]), jnp.int16),
        ],
        scratch_shapes=[
            pltpu.VMEM(shape, jnp.float32) for shape in [(half, half)] * 4 + [(half, 8), (8, half), (8, half)]
        ],
        name="orthogonal",
    )(ids, samples, other, *grams)


def whole_step(tiles, probe, cluster_perm, tile_keep):
    row_id = lax.axis_index("row")
    col_id = lax.axis_index("col")
    nrows = lax.axis_size("row")
    ncols = lax.axis_size("col")
    tile_len = tiles.shape[1]
    nz = ncols // 2
    plane, depth = col_id // nz, col_id % nz
    wraps = (row_id + col_id >= nrows).astype(jnp.int32)
    ids = jnp.stack([col_id, depth, wraps, plane]).astype(jnp.int32)
    weight = jnp.where(col_id == 0, 0.5, tile_keep[:, 0, 0].astype(jnp.float32))

    def same(d):
        return lambda r, c: (r, c ^ d)

    def slanted(d):
        return lambda r, c: (r + c - (c ^ d), c ^ d)

    def far(r, c):
        return (r - c, c)

    depths = range(1, nz)
    other = sent(probe[0], same(nz))
    singles = [sent(probe[1], same(d)) for d in depths]
    far_own = sent(probe[0], far)
    far_other = sent(probe[0], lambda r, c: (r - (c ^ nz), c ^ nz))
    far_perm = sent(cluster_perm, far)

    pair = jnp.stack([probe[0], other])
    line = jnp.stack([probe[1], *singles])
    far_pair = jnp.stack([far_own, far_other])
    cross = sent(line, same(nz))
    far_line = sent(line, far)
    pairs = [sent(pair, same(d)) for d in depths]
    far_pairs = [sent(far_pair, slanted(d)) for d in depths]
    far_cross = sent(cross, far)

    perm, far_perm = (x.reshape(-1, 1, tile_len) for x in (cluster_perm, far_perm))
    own_blocks = ([pair, *pairs], line, cross)
    far_blocks = ([far_pair, *far_pairs], far_line, far_cross)

    (more,) = products(ids, weight, perm, *own_blocks, tiles, True, 0)
    more = sent(more, lambda r, c: (r + c, c))
    back = products(ids, weight, perm, *own_blocks, tiles, True, 1)
    back, far_pairs = lax.optimization_barrier((back, far_pairs))
    back = [back[0]] + [sent(back[d], slanted(d)) for d in depths]
    given = products(ids, weight, far_perm, *far_blocks, tiles, False, 1)
    given = [given[0]] + [sent(given[d], same(d)) for d in depths]
    kept = products(ids, weight, far_perm, *far_blocks, tiles, False, 0, (more,))
    after = kept[:1]
    kept = [kept[0]] + [sent(kept[d], same(d)) for d in depths]
    crossed = summed(given, after)
    crossed = sent(crossed, same(nz))
    arrived = summed(back, after)
    arrived = sent(arrived, lambda r, c: (r + c, c ^ nz))
    samples, swapped, gram = gram_of(ids, [*kept, crossed, arrived])
    grams = [gram] + [sent(gram, same(d)) for d in depths]
    basis, swapped_basis = orthogonal(ids, samples, swapped, grams, 1.0 / tile_len)

    def placed(array, theirs):
        return lax.dynamic_update_index_in_dim(array, theirs, 1 - plane, 0)

    return (placed(samples, sent(swapped, same(nz))), placed(basis, decoded(sent(swapped_basis, same(nz)))))


def solution(mesh):
    whole = P(None, ("row", "col"), None)
    return jax.shard_map(
        whole_step,
        mesh=mesh,
        in_specs=(P(None, "row", "col"), whole, P(None, "row", None), P(None, "row", "col")),
        out_specs=(whole, whole),
        check_vma=False,
    )
```

```python
import functools

import jax
import jax.numpy as jnp
from jax import lax
from jax.experimental import pallas as pl
from jax.experimental.pallas import tpu as pltpu
from jax.sharding import PartitionSpec as P


AXES = ("row", "col")
EXACT = lax.Precision.HIGHEST
LEVELS = 32767.0
EXTRA = 16


def sent(value, to):
    nrows, ncols = lax.axis_size("row"), lax.axis_size("col")
    pairs = []
    for r in range(nrows):
        for c in range(ncols):
            r_to, c_to = to(r, c)
            pairs.append((r * ncols + c, (r_to % nrows) * ncols + c_to))
    return lax.ppermute(value, AXES, pairs)


def scale_of(exponent, mantissa):
    return jnp.exp2(exponent) * (mantissa * (1.0 / (LEVELS * LEVELS)))


def coded(block):
    largest = jnp.maximum(jnp.max(jnp.abs(block), axis=0, keepdims=True), 1e-30)
    exponent = jnp.floor(jnp.log2(largest * 1.0001)) + 1.0
    mantissa = jnp.ceil(largest * jnp.exp2(-exponent) * LEVELS)
    scale = scale_of(exponent, mantissa)
    values = jnp.clip(jnp.round(block * (1.0 / scale)), -LEVELS, LEVELS)
    at = lax.broadcasted_iota(jnp.int32, (EXTRA, block.shape[1]), 0)
    tail = jnp.where(at == 0, exponent, mantissa)
    return jnp.concatenate([values, tail], axis=0).astype(jnp.int32).astype(jnp.int16)


def decoded(code):
    wide = code.astype(jnp.int32).astype(jnp.float32)
    rows = code.shape[0] - EXTRA
    return wide[:rows] * scale_of(wide[rows : rows + 1], wide[rows + 1 : rows + 2])


def product_kernel(back, part, ids_ref, weight_ref, perm_ref, *refs):
    *pair_refs, plane_ref, cross_ref, tiles_ref = refs[:7]
    joins = not back and part == 0
    more_ref = refs[7] if joins else None
    *out_refs, tile_ref, raw_ref, omega_ref, sems = refs[8 if joins else 7 :]
    nz, points, _ = plane_ref.shape
    length = raw_ref.shape[1]
    step = 512
    k = ids_ref[3] ^ ids_ref[2] ^ part
    tile_slot = k if back else k ^ ids_ref[2]

    def piece_copy(q):
        rows = pl.ds(q * step, step)
        return pltpu.make_async_copy(tiles_ref.at[tile_slot, rows], tile_ref.at[rows], sems.at[q])

    for q in range(length // step):
        piece_copy(q).start()
    for slot in range(2):

        @pl.when(k == slot)
        def _(slot=slot):
            for d in range(nz):
                for a in range(2):
                    piece = (cross_ref[d] if a else plane_ref[d]) if slot else pair_refs[d][a]
                    at = (nz * a + d) * points
                    raw_ref[:, at : at + points] = piece.T

    def order_step(i, carry):
        at = pl.multiple_of(i * step, step)
        index = perm_ref[k, :, pl.ds(at, step)] ^ (ids_ref[0] * points)
        place = lax.broadcasted_iota(jnp.int32, (length, step), 0)
        chosen = jnp.where(place == index, 1.0, 0.0).astype(jnp.bfloat16)
        found = jnp.dot(raw_ref[...], chosen, preferred_element_type=jnp.float32)
        if back:
            omega_ref[:, pl.ds(at, step)] = found.astype(jnp.bfloat16)
        else:
            omega_ref[pl.ds(at, step), :] = found.T.astype(jnp.bfloat16)
        return carry

    lax.fori_loop(0, length // step, order_step, 0)
    for q in range(length // step):
        piece_copy(q).wait()
    weight = weight_ref[tile_slot]
    for d in range(nz):
        for a in range(2):
            at = pl.multiple_of((a * nz + (ids_ref[1] ^ d)) * points, points)
            if back:
                value = jnp.dot(omega_ref[...], tile_ref[:, pl.ds(at, points)], preferred_element_type=jnp.float32).T
            else:
                value = jnp.dot(tile_ref[pl.ds(at, points), :], omega_ref[...], preferred_element_type=jnp.float32)
            value = value * weight
            if joins:
                value = value + decoded(more_ref[d, a])
            code = coded(value)
            if len(out_refs) == 1:
                out_refs[0][d, a] = code
            else:
                out_refs[d][a] = code


def products(ids, weight, perm, pairs, plane, cross, tiles, back, part, more=()):
    nz, points, probes = plane.shape
    length = tiles.shape[1]
    block = (2, points + EXTRA, probes)
    shapes = [(nz, *block)] if back and part == 0 else [block] * nz
    smem, vmem = pl.BlockSpec(memory_space=pltpu.SMEM), pl.BlockSpec(memory_space=pltpu.VMEM)
    return pl.pallas_call(
        functools.partial(product_kernel, back, part),
        out_shape=[jax.ShapeDtypeStruct(shape, jnp.int16) for shape in shapes],
        in_specs=[smem, smem] + [vmem] * (3 + nz) + [pl.BlockSpec(memory_space=pl.ANY)] + [vmem] * len(more),
        out_specs=[vmem] * len(shapes),
        scratch_shapes=[
            pltpu.VMEM(tiles.shape[1:], jnp.bfloat16),
            pltpu.VMEM((probes, length), jnp.bfloat16),
            pltpu.VMEM((probes, length) if back else (length, probes), jnp.bfloat16),
            pltpu.SemaphoreType.DMA((length // 512,)),
        ],
        compiler_params=pltpu.CompilerParams(vmem_limit_bytes=40 << 20),
        cost_estimate=pl.CostEstimate(flops=4 * length * length * probes, bytes_accessed=11 << 20, transcendentals=0),
    )(ids, weight, perm, *pairs, plane, cross, tiles, *more)


def sum_kernel(count, *refs):
    first_ref, second_ref = refs[-2:]
    for out_ref, codes in ((first_ref, refs[:count]), (second_ref, refs[count : 2 * count])):
        for a in range(2):
            total = decoded(codes[0][a])
            for ref in codes[1:]:
                total = total + decoded(ref[a])
            out_ref[a] = coded(total)


def summed(first, second, after):
    vmem, unread = pl.BlockSpec(memory_space=pltpu.VMEM), pl.BlockSpec(memory_space=pl.ANY)
    return pl.pallas_call(
        functools.partial(sum_kernel, len(first)),
        in_specs=[vmem] * (2 * len(first)) + [unread],
        out_shape=[jax.ShapeDtypeStruct(first[0].shape, jnp.int16)] * 2,
        name="sum",
    )(*first, *second, after)


def gram_kernel(ids_ref, *refs):
    *in_refs, samples_ref, other_ref, gram_ref = refs
    plane = ids_ref[3]
    half = gram_ref.shape[1]
    total = None
    for a in (plane, 1 - plane):
        block = decoded(in_refs[0][a])
        for ref in in_refs[1:]:
            block = block + decoded(ref[a])
        if total is None:
            samples_ref[plane] = block
        else:
            other_ref[...] = block
        left, right = block[:, :half], block[:, half:]
        parts = [
            lax.dot_general(x, y, (((0,), (0,)), ((), ())), preferred_element_type=jnp.float32, precision=EXACT)
            for x, y in ((left, left), (left, right), (right, right))
        ]
        total = parts if total is None else [x + y for x, y in zip(total, parts)]
    for n, part in enumerate(total):
        gram_ref[n * half : (n + 1) * half, :] = part


def gram_of(ids, codes):
    _, rows, probes = codes[0].shape
    points = rows - EXTRA
    return pl.pallas_call(
        gram_kernel,
        in_specs=[pl.BlockSpec(memory_space=pltpu.SMEM)] + [pl.BlockSpec(memory_space=pltpu.VMEM)] * len(codes),
        out_shape=[
            jax.ShapeDtypeStruct((2, points, probes), jnp.float32),
            jax.ShapeDtypeStruct((points, probes), jnp.float32),
            jax.ShapeDtypeStruct((3 * probes // 2, probes // 2), jnp.float32),
        ],
        name="gram",
    )(ids, *codes)


def half_inverse(a_ref, out_ref, m_ref, tall_ref, u_ref, v_ref):
    n, size = a_ref.shape[0], u_ref.shape[0]
    rows = lax.broadcasted_iota(jnp.int32, (n, n), 0)
    cols = lax.broadcasted_iota(jnp.int32, (n, n), 1)
    m_ref[...] = (rows == cols).astype(jnp.float32)
    for ref in (tall_ref, u_ref, v_ref):
        ref[...] = jnp.zeros_like(ref)
    lane = lax.broadcasted_iota(jnp.int32, (size, n), 1)
    sub = lax.broadcasted_iota(jnp.int32, (size, n), 0)

    def spread(array, i):
        return jnp.broadcast_to(array[i : i + 1, :], (size, n))

    def group(b, carry):
        at = pl.multiple_of(b * size, size)
        u, v, near = u_ref[...], v_ref[...], tall_ref[pl.ds(at, size), :]
        panel, inverse = a_ref[pl.ds(at, size), :], m_ref[pl.ds(at, size), :]
        old_a, old_m, tall = a_ref[...], m_ref[...], tall_ref[...]
        for t in range(size):
            factor = jnp.broadcast_to(near[:, t : t + 1], (size, n))
            panel = panel - factor * u[t : t + 1, :]
            inverse = inverse - factor * v[t : t + 1, :]
        small = pltpu.roll(panel, n - at, axis=1)
        s = [[None] * size for _ in range(size)]
        e = [[None] * size for _ in range(size)]
        for t in range(size):
            column = jnp.broadcast_to(small[:, t : t + 1], (size, n))
            for i in range(t, size):
                s[i][t] = spread(column, i)
        for t in range(size - 1):
            ratio = 1.0 / s[t][t]
            for i in range(t + 1, size):
                factor = s[i][t] * ratio
                for j in range(t + 1, i + 1):
                    s[i][j] = s[i][j] - factor * s[j][t]
                for j in range(t):
                    e[i][j] = e[i][j] - factor * e[t][j]
                e[i][t] = -factor
        scale = s[0][0]
        for t in range(1, size):
            scale = jnp.where(sub == t, s[t][t], scale)
        scale = lax.rsqrt(scale)
        new_u, new_v = panel, inverse
        for t in range(size - 1):
            factor = jnp.zeros((size, n), jnp.float32)
            for i in range(t + 1, size):
                factor = jnp.where(sub == i, e[i][t], factor)
            new_u = new_u + factor * panel[t : t + 1, :]
            new_v = new_v + factor * inverse[t : t + 1, :]
        new_u = jnp.where(lane >= at + sub, new_u * scale, 0.0)
        new_v = new_v * scale
        update = jnp.dot(
            tall, jnp.concatenate([u, v], axis=1), preferred_element_type=jnp.float32, precision=EXACT
        )
        a_ref[...], m_ref[...] = old_a - update[:, :n], old_m - update[:, n:]
        out_ref[pl.ds(at, size), :] = new_v
        u_ref[...], v_ref[...] = new_u, new_v
        tall_ref[...] = new_u.T
        return carry

    lax.fori_loop(0, n // size, group, 0)


def factor_kernel(scale, ids_ref, samples_ref, other_ref, *refs):
    *gram_refs, basis_ref, out_ref, a_ref, m1_ref, m2_ref = refs[:9]
    work = refs[9:]
    half = a_ref.shape[0]
    plane = ids_ref[3]

    def product(a, b, over):
        return lax.dot_general(
            a, b, ((over[:1], over[1:]), ((), ())), preferred_element_type=jnp.float32, precision=EXACT
        )

    def gram(n):
        rows = slice(n * half, (n + 1) * half)
        one, two, three, four = (ref[rows, :] for ref in gram_refs)
        return ((one + two) + (three + four)) * scale

    a_ref[...] = gram(0)
    half_inverse(a_ref, m1_ref, *work)
    first = m1_ref[...]
    cross = product(first, gram(1), (1, 0))
    a_ref[...] = gram(2) - product(cross, cross, (0, 0))
    half_inverse(a_ref, m2_ref, *work)
    second = m2_ref[...]
    mixed = -product(second, product(cross, first, (0, 0)), (1, 0))
    for n, block in enumerate((samples_ref[plane], other_ref[...])):
        left, right = block[:, :half], block[:, half:]
        made = (product(left, first, (1, 1)), product(left, mixed, (1, 1)) + product(right, second, (1, 1)))
        for m, value in enumerate(made):
            columns = slice(m * half, (m + 1) * half)
            if n:
                out_ref[:, columns] = coded(value)
            else:
                basis_ref[plane, :, columns] = value


def orthogonal(ids, samples, other, grams, scale):
    half = grams[0].shape[1]
    return pl.pallas_call(
        functools.partial(factor_kernel, scale),
        in_specs=[pl.BlockSpec(memory_space=pltpu.SMEM)] + [pl.BlockSpec(memory_space=pltpu.VMEM)] * (2 + len(grams)),
        out_shape=[
            jax.ShapeDtypeStruct(samples.shape, jnp.float32),
            jax.ShapeDtypeStruct((other.shape[0] + EXTRA, other.shape[1]), jnp.int16),
        ],
        scratch_shapes=[
            pltpu.VMEM(shape, jnp.float32) for shape in [(half, half)] * 4 + [(half, 8), (8, half), (8, half)]
        ],
        name="orthogonal",
    )(ids, samples, other, *grams)


def whole_step(tiles, probe, cluster_perm, tile_keep):
    row_id = lax.axis_index("row")
    col_id = lax.axis_index("col")
    nrows = lax.axis_size("row")
    ncols = lax.axis_size("col")
    tile_len = tiles.shape[1]
    nz = ncols // 2
    plane, depth = col_id // nz, col_id % nz
    wraps = (row_id + col_id >= nrows).astype(jnp.int32)
    ids = jnp.stack([col_id, depth, wraps, plane]).astype(jnp.int32)
    weight = jnp.where(col_id == 0, 0.5, tile_keep[:, 0, 0].astype(jnp.float32))

    def same(d):
        return lambda r, c: (r, c ^ d)

    def slanted(d):
        return lambda r, c: (r + c - (c ^ d), c ^ d)

    def far(r, c):
        return (r - c, c)

    depths = range(1, nz)
    other = sent(probe[0], same(nz))
    singles = [sent(probe[1], same(d)) for d in depths]
    far_own = sent(probe[0], far)
    far_other = sent(probe[0], lambda r, c: (r - (c ^ nz), c ^ nz))
    far_perm = sent(cluster_perm, far)

    pair = jnp.stack([probe[0], other])
    line = jnp.stack([probe[1], *singles])
    far_pair = jnp.stack([far_own, far_other])
    cross = sent(line, same(nz))
    far_line = sent(line, far)
    pairs = [sent(pair, same(d)) for d in depths]
    far_pairs = [sent(far_pair, slanted(d)) for d in depths]
    far_cross = sent(cross, far)

    perm, far_perm = (x.reshape(-1, 1, tile_len) for x in (cluster_perm, far_perm))
    own_blocks = ([pair, *pairs], line, cross)
    far_blocks = ([far_pair, *far_pairs], far_line, far_cross)

    (more,) = products(ids, weight, perm, *own_blocks, tiles, True, 0)
    more = sent(more, lambda r, c: (r + c, c))
    back = products(ids, weight, perm, *own_blocks, tiles, True, 1)
    back = [back[0]] + [sent(back[d], slanted(d)) for d in depths]
    given = products(ids, weight, far_perm, *far_blocks, tiles, False, 1)
    given = [given[0]] + [sent(given[d], same(d)) for d in depths]
    kept = products(ids, weight, far_perm, *far_blocks, tiles, False, 0, (more,))
    after = kept[0]
    kept = [kept[0]] + [sent(kept[d], same(d)) for d in depths]
    crossed, arrived = summed(given, back, after)
    crossed = sent(crossed, same(nz))
    arrived = sent(arrived, lambda r, c: (r + c, c ^ nz))
    samples, swapped, gram = gram_of(ids, [*kept, crossed, arrived])
    grams = [gram] + [sent(gram, same(d)) for d in depths]
    basis, swapped_basis = orthogonal(ids, samples, swapped, grams, 1.0 / tile_len)

    def placed(array, theirs):
        return lax.dynamic_update_index_in_dim(array, theirs, 1 - plane, 0)

    return (placed(samples, sent(swapped, same(nz))), placed(basis, decoded(sent(swapped_basis, same(nz)))))


def solution(mesh):
    whole = P(None, ("row", "col"), None)
    return jax.shard_map(
        whole_step,
        mesh=mesh,
        in_specs=(P(None, "row", "col"), whole, P(None, "row", None), P(None, "row", "col")),
        out_specs=(whole, whole),
        check_vma=False,
    )
```

```python
import functools

import jax
import jax.numpy as jnp
from jax import lax
from jax.experimental import pallas as pl
from jax.experimental.pallas import tpu as pltpu
from jax.sharding import PartitionSpec as P


AXES = ("row", "col")
EXACT = lax.Precision.HIGHEST
LEVELS = 32767.0
EXTRA = 16


def sent(value, to):
    nrows, ncols = lax.axis_size("row"), lax.axis_size("col")
    pairs = []
    for r in range(nrows):
        for c in range(ncols):
            r_to, c_to = to(r, c)
            pairs.append((r * ncols + c, (r_to % nrows) * ncols + c_to))
    return lax.ppermute(value, AXES, pairs)


def scale_of(exponent, mantissa):
    return jnp.exp2(exponent) * (mantissa * (1.0 / (LEVELS * LEVELS)))


def coded(block):
    largest = jnp.maximum(jnp.max(jnp.abs(block), axis=0, keepdims=True), 1e-30)
    exponent = jnp.floor(jnp.log2(largest * 1.0001)) + 1.0
    mantissa = jnp.ceil(largest * jnp.exp2(-exponent) * LEVELS)
    scale = scale_of(exponent, mantissa)
    values = jnp.clip(jnp.round(block * (1.0 / scale)), -LEVELS, LEVELS)
    at = lax.broadcasted_iota(jnp.int32, (EXTRA, block.shape[1]), 0)
    tail = jnp.where(at == 0, exponent, mantissa)
    return jnp.concatenate([values, tail], axis=0).astype(jnp.int32).astype(jnp.int16)


def decoded(code):
    wide = code.astype(jnp.int32).astype(jnp.float32)
    rows = code.shape[0] - EXTRA
    return wide[:rows] * scale_of(wide[rows : rows + 1], wide[rows + 1 : rows + 2])


def product_kernel(back, part, ids_ref, weight_ref, perm_ref, *refs):
    *pair_refs, plane_ref, cross_ref, tiles_ref = refs[:7]
    *out_refs, tile_ref, raw_ref, omega_ref, sems = refs[7:]
    nz, points, _ = plane_ref.shape
    length = raw_ref.shape[1]
    step = 512
    k = ids_ref[3] ^ ids_ref[2] ^ part
    tile_slot = k if back else k ^ ids_ref[2]

    def piece_copy(q):
        rows = pl.ds(q * step, step)
        return pltpu.make_async_copy(tiles_ref.at[tile_slot, rows], tile_ref.at[rows], sems.at[q])

    for q in range(length // step):
        piece_copy(q).start()
    for slot in range(2):

        @pl.when(k == slot)
        def _(slot=slot):
            for d in range(nz):
                for a in range(2):
                    piece = (cross_ref[d] if a else plane_ref[d]) if slot else pair_refs[d][a]
                    at = (nz * a + d) * points
                    raw_ref[:, at : at + points] = piece.T

    def order_step(i, carry):
        at = pl.multiple_of(i * step, step)
        index = perm_ref[k, :, pl.ds(at, step)] ^ (ids_ref[0] * points)
        place = lax.broadcasted_iota(jnp.int32, (length, step), 0)
        chosen = jnp.where(place == index, 1.0, 0.0).astype(jnp.bfloat16)
        found = jnp.dot(raw_ref[...], chosen, preferred_element_type=jnp.float32)
        if back:
            omega_ref[:, pl.ds(at, step)] = found.astype(jnp.bfloat16)
        else:
            omega_ref[pl.ds(at, step), :] = found.T.astype(jnp.bfloat16)
        return carry

    lax.fori_loop(0, length // step, order_step, 0)
    for q in range(length // step):
        piece_copy(q).wait()
    weight = weight_ref[tile_slot]
    for d in range(nz):
        for a in range(2):
            at = pl.multiple_of((a * nz + (ids_ref[1] ^ d)) * points, points)
            if back:
                value = jnp.dot(omega_ref[...], tile_ref[:, pl.ds(at, points)], preferred_element_type=jnp.float32).T
            else:
                value = jnp.dot(tile_ref[pl.ds(at, points), :], omega_ref[...], preferred_element_type=jnp.float32)
            code = coded(value * weight)
            if len(out_refs) == 1:
                out_refs[0][d, a] = code
            else:
                out_refs[d][a] = code


def products(ids, weight, perm, pairs, plane, cross, tiles, back, part):
    nz, points, probes = plane.shape
    length = tiles.shape[1]
    block = (2, points + EXTRA, probes)
    shapes = [(nz, *block)] if back and part == 0 else [block] * nz
    smem, vmem = pl.BlockSpec(memory_space=pltpu.SMEM), pl.BlockSpec(memory_space=pltpu.VMEM)
    return pl.pallas_call(
        functools.partial(product_kernel, back, part),
        out_shape=[jax.ShapeDtypeStruct(shape, jnp.int16) for shape in shapes],
        in_specs=[smem, smem] + [vmem] * (3 + nz) + [pl.BlockSpec(memory_space=pl.ANY)],
        out_specs=[vmem] * len(shapes),
        scratch_shapes=[
            pltpu.VMEM(tiles.shape[1:], jnp.bfloat16),
            pltpu.VMEM((probes, length), jnp.bfloat16),
            pltpu.VMEM((probes, length) if back else (length, probes), jnp.bfloat16),
            pltpu.SemaphoreType.DMA((length // 512,)),
        ],
        compiler_params=pltpu.CompilerParams(vmem_limit_bytes=40 << 20),
        cost_estimate=pl.CostEstimate(flops=4 * length * length * probes, bytes_accessed=11 << 20, transcendentals=0),
    )(ids, weight, perm, *pairs, plane, cross, tiles)


def join_kernel(nz, *refs):
    more_ref = refs[nz]
    for d in range(nz):
        for a in range(2):
            refs[nz + 1 + d][a] = coded(decoded(refs[d][a]) + decoded(more_ref[d, a]))


def joined(codes, more):
    return pl.pallas_call(
        functools.partial(join_kernel, len(codes)),
        out_shape=[jax.ShapeDtypeStruct(x.shape, jnp.int16) for x in codes],
        name="join",
    )(*codes, more)


def sum_kernel(count, *refs):
    out_ref = refs[-1]
    for a in range(2):
        total = decoded(refs[0][a])
        for ref in refs[1:count]:
            total = total + decoded(ref[a])
        out_ref[a] = coded(total)


def summed(codes, after=()):
    vmem, unread = pl.BlockSpec(memory_space=pltpu.VMEM), pl.BlockSpec(memory_space=pl.ANY)
    return pl.pallas_call(
        functools.partial(sum_kernel, len(codes)),
        in_specs=[vmem] * len(codes) + [unread] * len(after),
        out_shape=jax.ShapeDtypeStruct(codes[0].shape, jnp.int16),
        name="sum",
    )(*codes, *after)


def gram_kernel(ids_ref, *refs):
    *in_refs, samples_ref, other_ref, gram_ref = refs
    plane = ids_ref[3]
    half = gram_ref.shape[1]
    total = None
    for a in (plane, 1 - plane):
        block = decoded(in_refs[0][a])
        for ref in in_refs[1:]:
            block = block + decoded(ref[a])
        if total is None:
            samples_ref[plane] = block
        else:
            other_ref[...] = block
        left, right = block[:, :half], block[:, half:]
        parts = [
            lax.dot_general(x, y, (((0,), (0,)), ((), ())), preferred_element_type=jnp.float32, precision=EXACT)
            for x, y in ((left, left), (left, right), (right, right))
        ]
        total = parts if total is None else [x + y for x, y in zip(total, parts)]
    for n, part in enumerate(total):
        gram_ref[n * half : (n + 1) * half, :] = part


def gram_of(ids, codes):
    _, rows, probes = codes[0].shape
    points = rows - EXTRA
    return pl.pallas_call(
        gram_kernel,
        in_specs=[pl.BlockSpec(memory_space=pltpu.SMEM)] + [pl.BlockSpec(memory_space=pltpu.VMEM)] * len(codes),
        out_shape=[
            jax.ShapeDtypeStruct((2, points, probes), jnp.float32),
            jax.ShapeDtypeStruct((points, probes), jnp.float32),
            jax.ShapeDtypeStruct((3 * probes // 2, probes // 2), jnp.float32),
        ],
        name="gram",
    )(ids, *codes)


def half_inverse(a_ref, out_ref, m_ref, tall_ref, u_ref, v_ref):
    n, size = a_ref.shape[0], u_ref.shape[0]
    rows = lax.broadcasted_iota(jnp.int32, (n, n), 0)
    cols = lax.broadcasted_iota(jnp.int32, (n, n), 1)
    m_ref[...] = (rows == cols).astype(jnp.float32)
    for ref in (tall_ref, u_ref, v_ref):
        ref[...] = jnp.zeros_like(ref)
    lane = lax.broadcasted_iota(jnp.int32, (size, n), 1)
    sub = lax.broadcasted_iota(jnp.int32, (size, n), 0)

    def spread(array, i):
        return jnp.broadcast_to(array[i : i + 1, :], (size, n))

    def group(b, carry):
        at = pl.multiple_of(b * size, size)
        u, v, near = u_ref[...], v_ref[...], tall_ref[pl.ds(at, size), :]
        panel, inverse = a_ref[pl.ds(at, size), :], m_ref[pl.ds(at, size), :]
        old_a, old_m, tall = a_ref[...], m_ref[...], tall_ref[...]
        for t in range(size):
            factor = jnp.broadcast_to(near[:, t : t + 1], (size, n))
            panel = panel - factor * u[t : t + 1, :]
            inverse = inverse - factor * v[t : t + 1, :]
        small = pltpu.roll(panel, n - at, axis=1)
        s = [[None] * size for _ in range(size)]
        e = [[None] * size for _ in range(size)]
        for t in range(size):
            column = jnp.broadcast_to(small[:, t : t + 1], (size, n))
            for i in range(t, size):
                s[i][t] = spread(column, i)
        for t in range(size - 1):
            ratio = 1.0 / s[t][t]
            for i in range(t + 1, size):
                factor = s[i][t] * ratio
                for j in range(t + 1, i + 1):
                    s[i][j] = s[i][j] - factor * s[j][t]
                for j in range(t):
                    e[i][j] = e[i][j] - factor * e[t][j]
                e[i][t] = -factor
        scale = s[0][0]
        for t in range(1, size):
            scale = jnp.where(sub == t, s[t][t], scale)
        scale = lax.rsqrt(scale)
        new_u, new_v = panel, inverse
        for t in range(size - 1):
            factor = jnp.zeros((size, n), jnp.float32)
            for i in range(t + 1, size):
                factor = jnp.where(sub == i, e[i][t], factor)
            new_u = new_u + factor * panel[t : t + 1, :]
            new_v = new_v + factor * inverse[t : t + 1, :]
        new_u = jnp.where(lane >= at + sub, new_u * scale, 0.0)
        new_v = new_v * scale
        update = jnp.dot(
            tall, jnp.concatenate([u, v], axis=1), preferred_element_type=jnp.float32, precision=EXACT
        )
        a_ref[...], m_ref[...] = old_a - update[:, :n], old_m - update[:, n:]
        out_ref[pl.ds(at, size), :] = new_v
        u_ref[...], v_ref[...] = new_u, new_v
        tall_ref[...] = new_u.T
        return carry

    lax.fori_loop(0, n // size, group, 0)


def factor_kernel(scale, ids_ref, samples_ref, other_ref, *refs):
    *gram_refs, basis_ref, out_ref, a_ref, m1_ref, m2_ref = refs[:9]
    work = refs[9:]
    half = a_ref.shape[0]
    plane = ids_ref[3]

    def product(a, b, over):
        return lax.dot_general(
            a, b, ((over[:1], over[1:]), ((), ())), preferred_element_type=jnp.float32, precision=EXACT
        )

    def gram(n):
        rows = slice(n * half, (n + 1) * half)
        one, two, three, four = (ref[rows, :] for ref in gram_refs)
        return ((one + two) + (three + four)) * scale

    a_ref[...] = gram(0)
    half_inverse(a_ref, m1_ref, *work)
    first = m1_ref[...]
    cross = product(first, gram(1), (1, 0))
    a_ref[...] = gram(2) - product(cross, cross, (0, 0))
    half_inverse(a_ref, m2_ref, *work)
    second = m2_ref[...]
    mixed = -product(second, product(cross, first, (0, 0)), (1, 0))
    for n, block in enumerate((samples_ref[plane], other_ref[...])):
        left, right = block[:, :half], block[:, half:]
        made = (product(left, first, (1, 1)), product(left, mixed, (1, 1)) + product(right, second, (1, 1)))
        for m, value in enumerate(made):
            columns = slice(m * half, (m + 1) * half)
            if n:
                out_ref[:, columns] = coded(value)
            else:
                basis_ref[plane, :, columns] = value


def orthogonal(ids, samples, other, grams, scale):
    half = grams[0].shape[1]
    return pl.pallas_call(
        functools.partial(factor_kernel, scale),
        in_specs=[pl.BlockSpec(memory_space=pltpu.SMEM)] + [pl.BlockSpec(memory_space=pltpu.VMEM)] * (2 + len(grams)),
        out_shape=[
            jax.ShapeDtypeStruct(samples.shape, jnp.float32),
            jax.ShapeDtypeStruct((other.shape[0] + EXTRA, other.shape[1]), jnp.int16),
        ],
        scratch_shapes=[
            pltpu.VMEM(shape, jnp.float32) for shape in [(half, half)] * 4 + [(half, 8), (8, half), (8, half)]
        ],
        name="orthogonal",
    )(ids, samples, other, *grams)


def whole_step(tiles, probe, cluster_perm, tile_keep):
    row_id = lax.axis_index("row")
    col_id = lax.axis_index("col")
    nrows = lax.axis_size("row")
    ncols = lax.axis_size("col")
    tile_len = tiles.shape[1]
    nz = ncols // 2
    plane, depth = col_id // nz, col_id % nz
    wraps = (row_id + col_id >= nrows).astype(jnp.int32)
    ids = jnp.stack([col_id, depth, wraps, plane]).astype(jnp.int32)
    weight = jnp.where(col_id == 0, 0.5, tile_keep[:, 0, 0].astype(jnp.float32))

    def same(d):
        return lambda r, c: (r, c ^ d)

    def slanted(d):
        return lambda r, c: (r + c - (c ^ d), c ^ d)

    def far(r, c):
        return (r - c, c)

    depths = range(1, nz)
    other = sent(probe[0], same(nz))
    singles = [sent(probe[1], same(d)) for d in depths]
    far_own = sent(probe[0], far)
    far_other = sent(probe[0], lambda r, c: (r - (c ^ nz), c ^ nz))
    far_perm = sent(cluster_perm, far)

    pair = jnp.stack([probe[0], other])
    line = jnp.stack([probe[1], *singles])
    far_pair = jnp.stack([far_own, far_other])
    cross = sent(line, same(nz))
    far_line = sent(line, far)
    pairs = [sent(pair, same(d)) for d in depths]
    far_pairs = [sent(far_pair, slanted(d)) for d in depths]
    far_cross = sent(cross, far)

    perm, far_perm = (x.reshape(-1, 1, tile_len) for x in (cluster_perm, far_perm))
    own_blocks = ([pair, *pairs], line, cross)
    far_blocks = ([far_pair, *far_pairs], far_line, far_cross)

    (more,) = products(ids, weight, perm, *own_blocks, tiles, True, 0)
    more = sent(more, lambda r, c: (r + c, c))
    back = products(ids, weight, perm, *own_blocks, tiles, True, 1)
    back, far_pairs = lax.optimization_barrier((back, far_pairs))
    back = [back[0]] + [sent(back[d], slanted(d)) for d in depths]
    given = products(ids, weight, far_perm, *far_blocks, tiles, False, 1)
    given = [given[0]] + [sent(given[d], same(d)) for d in depths]
    kept = joined(products(ids, weight, far_perm, *far_blocks, tiles, False, 0), more)
    after = kept[:1]
    kept = [kept[0]] + [sent(kept[d], same(d)) for d in depths]
    crossed = summed(given, after)
    crossed = sent(crossed, same(nz))
    arrived = summed(back, after)
    arrived = sent(arrived, lambda r, c: (r + c, c ^ nz))
    samples, swapped, gram = gram_of(ids, [*kept, crossed, arrived])
    grams = [gram] + [sent(gram, same(d)) for d in depths]
    basis, swapped_basis = orthogonal(ids, samples, swapped, grams, 1.0 / tile_len)

    def placed(array, theirs):
        return lax.dynamic_update_index_in_dim(array, theirs, 1 - plane, 0)

    return (placed(samples, sent(swapped, same(nz))), placed(basis, decoded(sent(swapped_basis, same(nz)))))


def solution(mesh):
    whole = P(None, ("row", "col"), None)
    return jax.shard_map(
        whole_step,
        mesh=mesh,
        in_specs=(P(None, "row", "col"), whole, P(None, "row", None), P(None, "row", "col")),
        out_specs=(whole, whole),
        check_vma=False,
    )
```
